32 devices in a mesh: dp: 8 (over z, x), fsdp: 4 (over y, core).
Axes of the slice: x: 2, y: 2, z: 4, core: 2. Of those that a mesh axis runs over, the one named last changes fastest.
Arguments:
- tokens: bfloat16 [32768, 768], P(('dp', 'fsdp')), may hold values from -6 to 6
- lengths: int32 [64, 4], P(('dp', 'fsdp')), may hold values from 1 to 192, 512 in all within a row
- exit_layers: int32 [64, 4], P(('dp', 'fsdp')), may hold values from 3 to 6
- destination: int32 [32, 8], P(('dp', 'fsdp')), may hold values from 0 to 7, each once within a row
- carried_grad: bfloat16 [49152, 768], P(('dp', 'fsdp')), may hold values from -6 to 6
- logits_grad: float32 [256, 14], P(('dp', 'fsdp')), may hold values from -6 to 6
- qkv_weight: bfloat16 [768, 2304], P(('dp', 'fsdp')), may hold values from -0.21875 to 0.21875
- query_bias: bfloat16 [768], P(('dp', 'fsdp')), may hold values from -3 to 3
- value_bias: bfloat16 [768], P(('dp', 'fsdp')), may hold values from -3 to 3
- out_weight: bfloat16 [768, 768], P(('dp', 'fsdp')), may hold values from -1 to 1
- out_bias: bfloat16 [768], P(('dp', 'fsdp')), may hold values from -1.75 to 1.75
- norm1_gain: bfloat16 [768], P(('dp', 'fsdp')), may hold values from 0.5 to 1.5
- norm1_bias: bfloat16 [768], P(('dp', 'fsdp')), may hold values from -1.75 to 1.75
- up_weight: bfloat16 [768, 3072], P(('dp', 'fsdp')), may hold values from -0.21875 to 0.21875
- up_bias: bfloat16 [3072], P(('dp', 'fsdp')), may hold values from -3 to 3
- down_weight: bfloat16 [3072, 768], P(('dp', 'fsdp')), may hold values from -0.109375 to 0.109375
- down_bias: bfloat16 [768], P(('dp', 'fsdp')), may hold values from -1.75 to 1.75
- norm2_gain: bfloat16 [768], P(('dp', 'fsdp')), may hold values from 0.5 to 1.5
- norm2_bias: bfloat16 [768], P(('dp', 'fsdp')), may hold values from -1.75 to 1.75
- student_weight: bfloat16 [768, 128], P(('dp', 'fsdp')), may hold values from -0.21875 to 0.21875
- student_bias: float32 [128], replicated, may hold values from -3 to 3
- pool_query: float32 [128], replicated, may hold values from -12 to 12
- dense_weight: float32 [128, 128], replicated, may hold values from -1 to 1
- dense_bias: float32 [128], replicated, may hold values from -1.75 to 1.75
- class_weight: float32 [128, 14], replicated, may hold values from -0.5 to 0.5
- class_bias: float32 [14], replicated, may hold values from -6 to 6
Outputs:
- carried: bfloat16 [49152, 768], P(('dp', 'fsdp'))
- logits: float32 [256, 14], P(('dp', 'fsdp'))
- tokens_grad: bfloat16 [32768, 768], P(('dp', 'fsdp'))
- qkv_weight_grad: float32 [768, 2304], P(('dp', 'fsdp'))
- query_bias_grad: float32 [768], P(('dp', 'fsdp'))
- value_bias_grad: float32 [768], P(('dp', 'fsdp'))
- out_weight_grad: float32 [768, 768], P(('dp', 'fsdp'))
- out_bias_grad: float32 [768], P(('dp', 'fsdp'))
- norm1_gain_grad: float32 [768], P(('dp', 'fsdp'))
- norm1_bias_grad: float32 [768], P(('dp', 'fsdp'))
- up_weight_grad: float32 [768, 3072], P(('dp', 'fsdp'))
- up_bias_grad: float32 [3072], P(('dp', 'fsdp'))
- down_weight_grad: float32 [3072, 768], P(('dp', 'fsdp'))
- down_bias_grad: float32 [768], P(('dp', 'fsdp'))
- norm2_gain_grad: float32 [768], P(('dp', 'fsdp'))
- norm2_bias_grad: float32 [768], P(('dp', 'fsdp'))
- student_weight_grad: float32 [768, 128], P(('dp', 'fsdp'))
- student_bias_grad: float32 [128], replicated
- pool_query_grad: float32 [128], replicated
- dense_weight_grad: float32 [128, 128], replicated
- dense_bias_grad: float32 [128], replicated
- class_weight_grad: float32 [128, 14], replicated
- class_bias_grad: float32 [14], replicated
The draws below stay inside these ranges and needn't reach their ends.
Inputs may be any that keep to these rules, and one draw needn't show every extreme that they name: In every row the 4 lengths sum to 512 and one of them is exactly 192. Each device's row names every dp index once; its entry r * 4 + k is the destination of pair k of the device's row r.
All inputs are finite; a program needn't handle non-finite values.
Results may differ from the reference program's by a relative error of at most 0.02.
The reference program's roundings to bfloat16 on the way count: a program that leaves them out, or rounds other values in their place, can miss the bound.
Values may be sent and summed in bfloat16 or wider, within the bound.
No kernel may reach another device: no remote copies, remote signals or barrier semaphores. Data moves between devices by JAX's collectives and lax.ppermute only.
A program may use at most 256 MiB of HBM per device.

```python
import math
import jax
import jax.numpy as jnp
import numpy as np
from jax import lax

D = 768
HD = 64
FF = 3072
SD = 128
CLS = 14
SH = 2
LAYER = 3
ROW = 512
MICRO = 2
SLOT = 192
PAIRS = 4
NDEV = 32
ROWS = 64
TOKENS = 32768
NPAIR = 256
OUTROWS = 49152
N_DP = 8
N_FSDP = 4


def plant(drawn, own_key, smallest, largest):
    index_at = [jax.random.randint(jax.random.fold_in(own_key, axis), (), 0, length) for axis, length in enumerate(drawn.shape)]
    longest = drawn.shape.index(max(drawn.shape))
    next_to = index_at[:longest] + [(index_at[longest] + 1) % drawn.shape[longest]] + index_at[longest + 1:]
    return drawn.at[tuple(index_at)].set(smallest).at[tuple(next_to)].set(largest)


def raised(result, own_key, source, target, shards_of, factor):
    def block_of(position):
        return (jnp.arange(result.shape[position]) // (result.shape[position] // shards_of)).reshape((-1,) + (1,) * (result.ndim - 1 - position))

    one_side = jax.random.permutation(own_key, shards_of)[block_of(target)]
    second = (block_of(target) + shards_of // 2) % shards_of
    return jnp.where((block_of(source) == one_side) | (block_of(source) == second), factor * result, result)


def block_levels(key, extent, split, low, high):
    loudness, own = 1.0, jax.random.fold_in(key, 6)
    for axis_at, blocks in split:
        draws = jnp.exp(jax.random.uniform(jax.random.fold_in(own, axis_at), (blocks,), jnp.float32, low / len(split), high / len(split)))
        loudness = loudness * jnp.repeat(draws, extent[axis_at] // blocks).reshape([-1 if axis == axis_at else 1 for axis in range(len(extent))])
    return loudness


def split_up(number_of, total, most, slope):
    weights = [(1 << 20) // math.isqrt(standing ** slope) + 1 for standing in range(2, number_of + 1)]
    surplus, counts = total - most - (number_of - 1), [1] * (number_of - 1)
    while surplus > 0:
        candidates = [i for i in range(number_of - 1) if counts[i] < most]
        pool, remaining = sum([weights[i] for i in candidates]), surplus
        for i in candidates:
            extra = min(most - counts[i], max(1, remaining * weights[i] // pool), surplus)
            counts[i] = counts[i] + extra
            surplus = surplus - extra
    return np.array([most] + counts)


def ragged_sizes(key, count, total, most, skew):
    if count == 2:
        one = jax.random.randint(key, (), max(1, total - most), min(most, total - 1) + 1)
        return jnp.stack([one, total - one])
    sizes = jnp.asarray(split_up(count, total, most, skew), jnp.int32)
    couples = (count - 1) // 2
    donor, receiver = sizes[1:1 + 2 * couples:2], sizes[2:2 + 2 * couples:2]
    room = jnp.minimum(donor - 1, most - receiver)
    passed = jax.random.randint(jax.random.fold_in(key, 1), (couples,), 0, 1 << 20) % (room + 1)
    sizes = sizes.at[1:1 + 2 * couples:2].set(donor - passed).at[2:2 + 2 * couples:2].set(receiver + passed)
    return sizes[jax.random.permutation(jax.random.fold_in(key, 2), count)]


def gaussian(key, extent, scale, bound, split=(), held_as=jnp.bfloat16):
    drawn = jax.random.normal(key, extent, jnp.float32) * scale
    if len(split) > 0:
        drawn = block_levels(key, extent, split, -0.22, 0.18) * drawn
    return jnp.clip(drawn, min=-bound, max=bound).astype(held_as)


def bell_draw_with(stream_key, dims, scale, bound, cuts, heavy, kind=jnp.bfloat16):
    result = scale * jax.random.normal(stream_key, dims, jnp.float32)
    if cuts:
        result = result * block_levels(stream_key, dims, cuts, -0.22, 0.18)
    return jnp.clip(raised(result, jax.random.fold_in(stream_key, 3), *heavy), -bound, bound).astype(kind)


def setup_inputs(seed: int = 0) -> dict:
    key_list = jax.random.split(jax.random.key(seed), 27)
    tokens = bell_draw_with(key_list[0], (TOKENS, D), 1.0, 6.0, ((0, 32),), (0, 1, 32, 2.75))
    lengths = jax.vmap(lambda own: ragged_sizes(own, PAIRS, ROW, SLOT, 1))(jax.random.split(key_list[1], ROWS)).reshape((ROWS, PAIRS)).astype(jnp.int32)
    exit_layers = plant(jax.random.randint(key_list[2], (ROWS, PAIRS), LAYER, LAYER + 4), jax.random.fold_in(key_list[2], 1), LAYER, (LAYER + 4) - 1).astype(jnp.int32)
    destination = jax.vmap(lambda own: jax.random.permutation(own, N_DP))(jax.random.split(key_list[3], NDEV)).reshape((NDEV, N_DP)).astype(jnp.int32)
    carried_grad = gaussian(key_list[4], (OUTROWS, D), 1.0, 6.0, ((0, 32),))
    logits_grad = gaussian(key_list[5], (NPAIR, CLS), 1.0, 6.0, ((0, 32),), jnp.float32)
    qkv_weight = gaussian(key_list[6], (D, 3 * D), D ** -0.5, 0.21875, ((0, 32),))
    query_bias = gaussian(key_list[7], (D,), 0.5, 3.0, ((0, 32),))
    value_bias = gaussian(key_list[8], (D,), 0.5, 3.0, ((0, 32),))
    out_weight = gaussian(key_list[9], (D, D), (min(D, max(16, D * 8 // SLOT))) ** -0.5, 1.0, ((0, 32),))
    out_bias = gaussian(key_list[10], (D,), 0.3, 1.75, ((0, 32),))
    norm1_gain = jnp.clip(1.0 + 0.1 * jax.random.normal(key_list[11], (D,), jnp.float32), 0.5, 1.5).astype(jnp.bfloat16)
    norm1_bias = gaussian(key_list[12], (D,), 0.3, 1.75, ((0, 32),))
    up_weight = gaussian(key_list[13], (D, FF), D ** -0.5, 0.21875, ((0, 32),))
    up_bias = gaussian(key_list[14], (FF,), 0.5, 3.0, ((0, 32),))
    down_weight = gaussian(key_list[15], (FF, D), FF ** -0.5, 0.109375, ((0, 32),))
    down_bias = gaussian(key_list[16], (D,), 0.3, 1.75, ((0, 32),))
    norm2_gain = jnp.clip(1.0 + 0.1 * jax.random.normal(key_list[17], (D,), jnp.float32), 0.5, 1.5).astype(jnp.bfloat16)
    norm2_bias = gaussian(key_list[18], (D,), 0.3, 1.75, ((0, 32),))
    student_weight = gaussian(key_list[19], (D, SD), D ** -0.5, 0.21875, ((0, 32),))
    student_bias = gaussian(key_list[20], (SD,), 0.5, 3.0, (), jnp.float32)
    pool_query = gaussian(key_list[21], (SD,), 2.0, 12.0, (), jnp.float32)
    dense_weight = gaussian(key_list[22], (SD, SD), (SD // 4) ** -0.5, 1.0, (), jnp.float32)
    dense_bias = gaussian(key_list[23], (SD,), 0.3, 1.75, (), jnp.float32)
    class_weight = gaussian(key_list[24], (SD, CLS), SD ** -0.5, 0.5, (), jnp.float32)
    class_bias = gaussian(key_list[25], (CLS,), 1.0, 6.0, (), jnp.float32)
    return dict(tokens=tokens, lengths=lengths, exit_layers=exit_layers, destination=destination, carried_grad=carried_grad, logits_grad=logits_grad, qkv_weight=qkv_weight, query_bias=query_bias, value_bias=value_bias, out_weight=out_weight, out_bias=out_bias, norm1_gain=norm1_gain, norm1_bias=norm1_bias, up_weight=up_weight, up_bias=up_bias, down_weight=down_weight, down_bias=down_bias, norm2_gain=norm2_gain, norm2_bias=norm2_bias, student_weight=student_weight, student_bias=student_bias, pool_query=pool_query, dense_weight=dense_weight, dense_bias=dense_bias, class_weight=class_weight, class_bias=class_bias)


@jax.custom_vjp
def low(v):
    return lax.optimization_barrier(v.astype(jnp.bfloat16)).astype(jnp.float32)

@jax.custom_vjp
def low_back(v):
    return v

def low_keep(v):
    return (low(v), None)

def low_pass(kept, grad):
    return (grad,)

def back_keep(v):
    return (v, None)

def back_low(kept, grad):
    return (low(grad),)
low.defvjp(low_keep, low_pass)
low_back.defvjp(back_keep, back_low)
highest = lax.Precision.HIGHEST
norm_eps = 1e-12
masked_value = -1e+30

def rounded_both(value):
    return low_back(low(value))

def matmul(left, right):
    return jnp.dot(left, right, precision=highest, preferred_element_type=jnp.float32)

def layer_norm(values, gain, shift):
    average = lax.optimization_barrier(jnp.mean(values, axis=-1, keepdims=True))
    centered = values - average
    spread = lax.optimization_barrier(jnp.mean(centered * centered, axis=-1, keepdims=True))
    return centered * lax.rsqrt(spread + norm_eps) * gain + shift

def student_head(student_rows, segment, pair_count, pool_query, dense_weight, dense_bias, class_weight, class_bias):
    token_count = student_rows.shape[0]
    head_width = SD // SH
    split_rows = student_rows.reshape(token_count, SH, head_width)
    pool_heads = pool_query.reshape(SH, head_width)
    pool_scores = jnp.einsum('tad,ad->at', split_rows, pool_heads, precision=highest) / math.sqrt(head_width)
    member = segment[None, :] == jnp.arange(pair_count, dtype=jnp.int32)[:, None]
    pool_weight = jax.nn.softmax(jnp.where(member[None], pool_scores[:, None, :], masked_value), axis=-1)
    pooled = jnp.einsum('apt,tad->pad', pool_weight, split_rows, precision=highest).reshape(pair_count, SD)
    dense = jnp.tanh(jnp.dot(pooled, dense_weight, precision=highest) + dense_bias)
    return jnp.dot(dense, class_weight, precision=highest) + class_bias

def segment_ids(row_lengths):
    ends = jnp.cumsum(row_lengths).astype(jnp.int32)
    place = jnp.arange(ROW, dtype=jnp.int32)
    return lax.optimization_barrier(jnp.sum((place[:, None] >= ends[None, :]).astype(jnp.int32), axis=1)).astype(jnp.int32)

def row_forward(row_tokens, segment, weights):
    qkv_weight, query_bias, value_bias, out_weight, out_bias, norm1_gain, norm1_bias, up_weight, up_bias, down_weight, down_bias, norm2_gain, norm2_bias, student_weight, student_bias, pool_query, dense_weight, dense_bias, class_weight, class_bias = weights
    head_count = D // HD
    scale = 1.0 / math.sqrt(HD)
    same_pair = segment[:, None] == segment[None, :]
    projected = matmul(row_tokens, qkv_weight)
    query_rows = rounded_both(projected[:, :D] + query_bias).reshape(ROW, head_count, HD)
    key_rows = rounded_both(projected[:, D:2 * D]).reshape(ROW, head_count, HD)
    value_rows = rounded_both(projected[:, 2 * D:] + value_bias).reshape(ROW, head_count, HD)
    scores = low_back(jnp.einsum('qhd,khd->hqk', query_rows, key_rows, precision=highest) * scale)
    probs = jax.nn.softmax(jnp.where(same_pair[None], scores, masked_value), axis=-1)
    context = jnp.einsum('hqk,khd->qhd', low(probs), value_rows, precision=highest).reshape(ROW, D)
    context = rounded_both(context)
    branch = low_back(matmul(context, out_weight) + out_bias)
    normed = low(layer_norm(row_tokens + branch, norm1_gain, norm1_bias))
    inner = low_back(matmul(normed, up_weight) + up_bias)
    activated = low(jax.nn.gelu(inner, approximate=False))
    second = low_back(matmul(activated, down_weight) + down_bias)
    output_rows = low(layer_norm(normed + second, norm2_gain, norm2_bias))
    student_rows = low_back(matmul(output_rows, student_weight) + student_bias)
    logits = student_head(student_rows, segment, PAIRS, pool_query, dense_weight, dense_bias, class_weight, class_bias)
    return (output_rows, logits)

def reference(tokens, lengths, exit_layers, destination, carried_grad, logits_grad, qkv_weight, query_bias, value_bias, out_weight, out_bias, norm1_gain, norm1_bias, up_weight, up_bias, down_weight, down_bias, norm2_gain, norm2_bias, student_weight, student_bias, pool_query, dense_weight, dense_bias, class_weight, class_bias):
    weights = tuple((array_item.astype(jnp.float32) for array_item in (qkv_weight, query_bias, value_bias, out_weight, out_bias, norm1_gain, norm1_bias, up_weight, up_bias, down_weight, down_bias, norm2_gain, norm2_bias, student_weight, student_bias, pool_query, dense_weight, dense_bias, class_weight, class_bias)))
    token_rows = tokens.astype(jnp.float32).reshape(ROWS, ROW, D)
    segments = jax.vmap(segment_ids)(lengths)

    def forward(all_rows, all_weights):
        checked = jax.checkpoint(row_forward)

        def step_rows(loop_state, inputs):
            row_tokens, segment = inputs
            output_rows, row_logits = checked(row_tokens, segment, all_weights)
            return (loop_state, (output_rows, row_logits))
        unused, (outputs, all_logits) = lax.scan(step_rows, jnp.zeros((), jnp.float32), (all_rows, segments))
        return (outputs, all_logits)
    (outputs, logits), pullback = jax.vjp(forward, token_rows, weights)
    dp_ids = jnp.arange(N_DP, dtype=jnp.int32)
    hits = (destination[:, :, None] == dp_ids[None, None, :]).astype(jnp.int32)
    pair_of = lax.optimization_barrier(jnp.sum(hits * dp_ids[None, :, None], axis=1)).astype(jnp.int32)
    ends = jnp.cumsum(lengths, axis=1).astype(jnp.int32)
    starts = (ends - lengths).reshape(NDEV, N_DP)
    device_lengths = lengths.reshape(NDEV, N_DP)
    alive = (exit_layers > LAYER).reshape(NDEV, N_DP)
    target_full = jnp.broadcast_to(dp_ids[:, None, None], (N_DP, N_FSDP, N_DP))
    fsdp_ids = jnp.arange(N_FSDP, dtype=jnp.int32)[None, :, None]
    source_dev = jnp.broadcast_to(dp_ids[None, None, :] * N_FSDP + fsdp_ids, (N_DP, N_FSDP, N_DP))
    pair_index = pair_of[source_dev, target_full]
    pair_start = starts[source_dev, pair_index]
    pair_length = device_lengths[source_dev, pair_index]
    pair_alive = alive[source_dev, pair_index]
    row_global = source_dev * MICRO + pair_index // PAIRS
    slot_place = jnp.arange(SLOT, dtype=jnp.int32)
    token_index = row_global[..., None] * ROW + pair_start[..., None] + slot_place
    valid = (slot_place < pair_length[..., None]) & pair_alive[..., None]
    token_index = jnp.where(valid, token_index, 0).reshape(-1).astype(jnp.int32)
    valid = valid.reshape(-1)
    flat_outputs = outputs.reshape(TOKENS, D)
    carried = jnp.where(valid[:, None], flat_outputs[token_index], 0.0).astype(jnp.bfloat16)
    slot_grads = jnp.where(valid[:, None], carried_grad.astype(jnp.float32), 0.0)
    output_cot = jnp.zeros((TOKENS, D), jnp.float32).at[token_index].add(slot_grads)
    grads = pullback((output_cot.reshape(ROWS, ROW, D), logits_grad.reshape(ROWS, PAIRS, CLS)))
    tokens_grad = grads[0].reshape(TOKENS, D).astype(jnp.bfloat16)
    weight_grads = grads[1]
    return (carried, logits.reshape(NPAIR, CLS), tokens_grad, weight_grads[0], weight_grads[1], weight_grads[2], weight_grads[3], weight_grads[4], weight_grads[5], weight_grads[6], weight_grads[7], weight_grads[8], weight_grads[9], weight_grads[10], weight_grads[11], weight_grads[12], weight_grads[13], weight_grads[14], weight_grads[15], weight_grads[16], weight_grads[17], weight_grads[18], weight_grads[19])
```

```python
import functools
import math

import jax
import jax.numpy as jnp
from jax import lax
from jax.experimental import pallas as pl
from jax.experimental.pallas import tpu as pltpu
from jax.sharding import Mesh
from jax.sharding import PartitionSpec as P

HD = 64
SD = 128
SH = 2
LAYER = 3
ROW = 512
MICRO = 2
LANES = 128

BF16 = jnp.bfloat16
F32 = jnp.float32
highest = lax.Precision.HIGHEST
norm_eps = 1e-12
masked_value = -1e30

tail_scale = 0.425
tail_terms = (
    0.2397720031195156,
    0.2404005560164679,
    0.20920268278012027,
    0.22961437095935636,
    -0.06054995293320506,
    0.3670545366443018,
    -0.292749557721544,
    0.06725537014453116,
)

QUERY_BIAS, VALUE_BIAS, OUT_BIAS, GAIN1, BIAS1, DOWN_BIAS, GAIN2, BIAS2, UP_BIAS = range(9)


def narrow(value):
    return value.astype(BF16)


def widen(value):
    return value.astype(F32)


def matmul(left, right, precision=None):
    return lax.dot_general(
        left, right, (((1,), (0,)), ((), ())), preferred_element_type=F32, precision=precision
    )


def left_inner(left, right, precision=None):
    return lax.dot_general(
        left, right, (((0,), (0,)), ((), ())), preferred_element_type=F32, precision=precision
    )


def right_inner(left, right, precision=None):
    return lax.dot_general(
        left, right, (((1,), (1,)), ((), ())), preferred_element_type=F32, precision=precision
    )


def params(*semantics, limit=58):
    return pltpu.CompilerParams(
        dimension_semantics=semantics or None, vmem_limit_bytes=limit * 1024 * 1024
    )


def cost(flops, nbytes, transcendentals=0):
    return pl.CostEstimate(
        flops=int(flops), bytes_accessed=int(nbytes), transcendentals=int(transcendentals)
    )


def fixed(shape, *at):
    where = at or (0,) * len(shape)
    return pl.BlockSpec(shape, lambda *_: where)


class Layout:
    def __init__(self, mesh):
        dp, fsdp = mesh.shape["dp"], mesh.shape["fsdp"]
        devices = mesh.devices
        if (dp, fsdp) == (8, 4):
            self.mesh = Mesh(devices.reshape(4, 2, 2, 2), ("z", "x", "y", "core"))
            self.dp = ("z", "x")
            self.stages = (("core",), ("x", "y"), ("z",))
        elif (dp, fsdp) == (64, 4):
            self.mesh = Mesh(devices.reshape(8, 4, 2, 4), ("z", "x", "core", "y"))
            self.dp = ("z", "x", "core")
            self.stages = (("core",), ("x", "y"), ("z",))
        else:
            self.mesh = mesh
            self.dp = ("dp",)
            self.stages = (("fsdp",), ("dp",))
        self.axes = tuple(self.mesh.axis_names)
        self.sizes = tuple(self.mesh.shape[name] for name in self.axes)
        self.count = math.prod(self.sizes)
        self.dp_count = dp
        self.extents = tuple(math.prod(self.mesh.shape[n] for n in stage) for stage in self.stages)
        order = [self.axes.index(name) for stage in self.stages for name in stage]
        self.place = []
        for device in range(self.count):
            at, rest = [], device
            for size in reversed(self.sizes):
                at.append(rest % size)
                rest //= size
            at = at[::-1]
            position = 0
            for axis in order:
                position = position * self.sizes[axis] + at[axis]
            self.place.append(position)
        self.device_at = [self.place.index(i) for i in range(self.count)]

    def exchange(self, value, stage):
        extent = self.extents[stage]
        value = value.reshape((extent, value.shape[0] // extent) + value.shape[1:])
        return lax.all_to_all(
            value, self.stages[stage], split_axis=0, concat_axis=0, tiled=True
        )

    def scatter_sum(self, value):
        for stage in range(len(self.stages)):
            value = jnp.sum(widen(self.exchange(narrow(value), stage)), axis=0)
        return value[0]


def store_parts(ref, value, place, column):
    count, part, _ = ref.shape
    width = value.shape[1]
    value = value.astype(ref.dtype) if part % 16 == 0 else value
    for device in range(count):
        ref[place[device], :, pl.ds(column, width)] = value[
            device * part : (device + 1) * part
        ].astype(ref.dtype)


class Sums:
    def __init__(self, layout, rows):
        self.layout = layout
        self.count, self.part = layout.count, rows // layout.count
        self.split = self.part % 8 == 0

    def shape(self, columns):
        if self.split:
            return jax.ShapeDtypeStruct((self.count, self.part, columns), BF16)
        return jax.ShapeDtypeStruct((self.count * self.part, columns), BF16)

    def spec(self, columns):
        return fixed(self.shape(columns).shape)

    def store(self, ref, value, column):
        if self.split:
            store_parts(ref, value, self.layout.place, column)
        else:
            ref[:, pl.ds(column, value.shape[1])] = value.astype(ref.dtype)

    def parts(self, value):
        if self.split:
            return value
        value = value.reshape(self.count, self.part, value.shape[1])
        return value[jnp.asarray(self.layout.device_at)]


def interleave(width, ratio, dtype):
    size = width * ratio
    source = lax.broadcasted_iota(jnp.int32, (size, size), 0)
    target = lax.broadcasted_iota(jnp.int32, (size, size), 1)
    return (source == (target % width) * ratio + target // width).astype(dtype)


def pack_body(qkv, out, up, down, student, columns, packed, *, ratio, hidden):
    part = qkv.shape[0]
    packed[:, : 3 * hidden] = qkv[...]
    packed[:, 3 * hidden : 4 * hidden] = out[...]
    base = 4 * hidden
    mix = interleave(LANES, ratio, BF16)
    for chunk in range(hidden // LANES):
        piece = narrow(
            matmul(up[:, chunk * ratio * LANES : (chunk + 1) * ratio * LANES], mix)
        )
        for j in range(ratio):
            at = base + j * hidden + chunk * LANES
            packed[:, at : at + LANES] = piece[:, j * LANES : (j + 1) * LANES]
    base += ratio * hidden
    row = lax.broadcasted_iota(jnp.int32, (part, part * ratio), 0)
    column = lax.broadcasted_iota(jnp.int32, (part, part * ratio), 1)
    for j in range(ratio):
        pick = (column == row * ratio + j).astype(BF16)
        packed[:, base + j * hidden : base + (j + 1) * hidden] = narrow(matmul(pick, down[...]))
    base += ratio * hidden
    packed[:, base : base + SD] = student[...]
    packed[:, base + SD :] = columns[...]


def turned(vectors):
    return widen(vectors).T


def attention_body(
    tokens, seg_column, seg_row, wq, wk, wv, vectors, query, key, value, context, mask, rows
):
    step = pl.program_id(1)
    width = wq.shape[1]

    @pl.when((step == 0) & (pl.program_id(0) == 0))
    def _():
        rows[...] = turned(vectors[...])

    @pl.when(step == 0)
    def _():
        mask[...] = jnp.where(seg_column[0] == seg_row[0], 0.0, masked_value)

    here = pl.ds(pl.multiple_of(step * width, width), width)
    x = tokens[...]
    q = narrow(matmul(x, wq[...]) + rows[QUERY_BIAS : QUERY_BIAS + 1, here])
    k = narrow(matmul(x, wk[...]))
    v = narrow(matmul(x, wv[...]) + rows[VALUE_BIAS : VALUE_BIAS + 1, here])
    query[...] = q
    key[...] = k
    value[...] = v
    lane = lax.broadcasted_iota(jnp.int32, (x.shape[0], LANES), 1)
    scale = BF16(1.0 / math.sqrt(HD))
    for block in range(width // LANES):
        cut = slice(block * LANES, (block + 1) * LANES)
        q_block, k_block, v_turned = q[:, cut] * scale, k[:, cut], v[:, cut].T
        parts = []
        for head in range(LANES // HD):
            mine = (lane >= head * HD) & (lane < (head + 1) * HD)
            scores = right_inner(k_block, jnp.where(mine, q_block, BF16(0))) + mask[...]
            exponent = jnp.exp(scores - jnp.max(scores, axis=0, keepdims=True))
            total = jnp.sum(exponent, axis=0, keepdims=True)
            probs = narrow(exponent * (1.0 / total))
            parts.append(matmul(v_turned[head * HD : (head + 1) * HD], probs))
        context[:, cut] = narrow(jnp.concatenate(parts, axis=0)).T


def attention_grad_body(
    branch, seg_column, seg_row, query, key, value, out_weight, grads, mask
):
    width = query.shape[1]

    @pl.when(pl.program_id(1) == 0)
    def _():
        mask[...] = jnp.where(seg_column[0] == seg_row[0], 0.0, masked_value)

    grad_context = narrow(right_inner(branch[...], out_weight[...]))
    lane = lax.broadcasted_iota(jnp.int32, (branch.shape[0], LANES), 1)
    scale = 1.0 / math.sqrt(HD)
    for block in range(width // LANES):
        cut = slice(block * LANES, (block + 1) * LANES)
        q_block, k_block, v_block = query[:, cut] * BF16(scale), key[:, cut], value[:, cut]
        g_block, k_turned = grad_context[:, cut], k_block.T
        grad_q, grad_k, grad_v = [], 0.0, 0.0
        for head in range(LANES // HD):
            mine = (lane >= head * HD) & (lane < (head + 1) * HD)
            q_head = jnp.where(mine, q_block, BF16(0))
            g_head = jnp.where(mine, g_block, BF16(0))
            scores = right_inner(k_block, q_head) + mask[...]
            exponent = jnp.exp(scores - jnp.max(scores, axis=0, keepdims=True))
            total = jnp.sum(exponent, axis=0, keepdims=True)
            probs = exponent * (1.0 / total)
            grad_probs = right_inner(v_block, g_head)
            inner = jnp.sum(probs * grad_probs, axis=0, keepdims=True)
            grad_scores = narrow(probs * (grad_probs - inner))
            grad_v += matmul(narrow(probs), g_head)
            grad_k += matmul(grad_scores, q_head)
            grad_q.append(matmul(k_turned[head * HD : (head + 1) * HD], grad_scores))
        grads[0, :, cut] = narrow(jnp.concatenate(grad_q, axis=0) * scale).T
        grads[1, :, cut] = narrow(grad_k)
        grads[2, :, cut] = narrow(grad_v)


def normalize(values):
    average = jnp.mean(values, axis=-1, keepdims=True)
    centered = values - average
    spread = jnp.mean(centered * centered, axis=-1, keepdims=True)
    scale = lax.rsqrt(spread + norm_eps)
    return centered * scale, scale


def gelu_and_slope(x):
    t = 1.0 / (1.0 + (tail_scale / math.sqrt(2.0)) * jnp.abs(x))
    bell = jnp.exp(-0.5 * (x * x))
    tail = F32(0.5 * tail_terms[-1])
    for term in tail_terms[-2::-1]:
        tail = tail * t + 0.5 * term
    tail = tail * t * bell
    phi = jnp.where(x < 0.0, tail, 1.0 - tail)
    return x * phi, phi + x * (bell * (1.0 / math.sqrt(2.0 * math.pi)))


CHUNK = 256


def forward_body(
    tokens, context, out_weight, up, down, student, vectors, student_bias,
    pre_first, normed, activated, slope, pre_second, outputs, student_rows, total, rows,
):
    step = pl.program_id(0)
    count = tokens.shape[0]

    @pl.when(step == 0)
    def _():
        rows[...] = turned(vectors[...])
        for low in range(0, count, CHUNK):
            cut = slice(low, low + CHUNK)
            pre = (
                widen(tokens[cut])
                + matmul(context[cut], out_weight[...])
                + rows[OUT_BIAS : OUT_BIAS + 1]
            )
            pre_first[cut] = pre
            hat, _ = normalize(pre)
            value = narrow(hat * rows[GAIN1 : GAIN1 + 1] + rows[BIAS1 : BIAS1 + 1])
            normed[cut] = value
            total[cut] = widen(value) + rows[DOWN_BIAS : DOWN_BIAS + 1]

    bias = rows[pl.ds(UP_BIAS + step, 1)]
    for low in range(0, count, CHUNK):
        cut = slice(low, low + CHUNK)
        value, grad = gelu_and_slope(matmul(normed[cut], up[...]) + bias)
        value = narrow(value)
        activated[cut] = value
        slope[cut] = narrow(grad)
        total[cut] += matmul(value, down[...])

    @pl.when(step == pl.num_programs(0) - 1)
    def _():
        for low in range(0, count, CHUNK):
            cut = slice(low, low + CHUNK)
            pre = total[cut]
            pre_second[cut] = pre
            hat, _ = normalize(pre)
            value = narrow(hat * rows[GAIN2 : GAIN2 + 1] + rows[BIAS2 : BIAS2 + 1])
            outputs[cut] = value
            student_rows[cut] = matmul(value, student[...]) + student_bias[...]


def select_body(index, source, target):
    place = lax.broadcasted_iota(jnp.int32, (index.shape[0], source.shape[0]), 1)
    target[...] = narrow(matmul((index[...] == place).astype(BF16), source[...]))


def student_body(
    student_rows, segment, query, dense_weight, dense_bias, class_weight, class_bias, logits_grad,
    logits, student_grad, small, *, small_rows,
):
    count, _ = student_rows.shape
    pairs, classes = logits_grad.shape
    wide = -(-pairs // LANES) * LANES
    head = SD // SH
    scale = 1.0 / math.sqrt(head)
    rows = student_rows[...]
    member = segment[...] == lax.broadcasted_iota(jnp.int32, (count, wide), 1)
    one_hot = member.astype(F32)
    lane = lax.broadcasted_iota(jnp.int32, (count, SD), 1)

    def by_head(values):
        return [
            jnp.sum(
                jnp.where((lane >= a * head) & (lane < (a + 1) * head), values, 0.0),
                axis=1,
                keepdims=True,
            )
            for a in range(SH)
        ]

    def spread(columns):
        value = columns[0]
        for a in range(1, SH):
            value = jnp.where(lane >= a * head, columns[a], value)
        return jnp.broadcast_to(value, (count, SD))

    def of_pair(row):
        return jnp.sum(jnp.where(member, row, 0.0), axis=1, keepdims=True)

    def over_pair(column):
        return jnp.sum(jnp.where(member, column, 0.0), axis=0, keepdims=True)

    weights = []
    for score in by_head(rows * query[...]):
        score = score * scale
        top = jnp.max(jnp.where(member, score, masked_value), axis=0, keepdims=True)
        exponent = jnp.exp(score - of_pair(top))
        weights.append(exponent / of_pair(over_pair(exponent)))
    weight = spread(weights)
    pooled = left_inner(one_hot, weight * rows, highest)
    dense = jnp.tanh(matmul(pooled, dense_weight[...], highest) + dense_bias[...])
    logits[...] = matmul(dense[:pairs], class_weight[...], highest) + class_bias[...]

    grad = logits_grad[...]
    grad_pre = right_inner(grad, class_weight[...], highest) * (
        1.0 - dense[:pairs] * dense[:pairs]
    )
    small[...] = jnp.zeros_like(small)
    small[:SD] = left_inner(pooled[:pairs], grad_pre, highest)
    small[SD : SD + classes] = left_inner(grad, dense[:pairs], highest)
    at = small_rows
    small[at : at + 1] = jnp.sum(grad_pre, axis=0, keepdims=True)
    small[at + 1 : at + 2, :classes] = jnp.sum(grad, axis=0, keepdims=True)
    grad_pooled = right_inner(grad_pre, dense_weight[...], highest)
    grad_token = matmul(one_hot[:, :pairs], grad_pooled, highest)
    grad_score = []
    for a, inner in enumerate(by_head(rows * grad_token)):
        product = weights[a] * inner
        grad_score.append(weights[a] * (inner - of_pair(over_pair(product))))
    grad_score = spread(grad_score) * scale
    small[at + 2 : at + 3] = jnp.sum(grad_score * rows, axis=0, keepdims=True)
    result = narrow(weight * grad_token + grad_score * query[...])
    student_grad[...] = result
    small[at + 3 : at + 4] = jnp.sum(widen(result), axis=0, keepdims=True)


def norm_grad(grad, pre, gain):
    hat, scale = normalize(pre)
    scaled = grad * gain
    result = scale * (
        scaled
        - jnp.mean(scaled, axis=-1, keepdims=True)
        - hat * jnp.mean(scaled * hat, axis=-1, keepdims=True)
    )
    return (
        result,
        jnp.sum(grad * hat, axis=0, keepdims=True),
        jnp.sum(grad, axis=0, keepdims=True),
    )


def as_columns(rows, count, hidden):
    row = lax.broadcasted_iota(jnp.int32, (LANES, hidden), 0)
    block = jnp.zeros((LANES, hidden), F32)
    for i in range(count):
        block = jnp.where(row == i, rows[i], block)
    return block.T


def down_grad_body(
    slot, returned, student_grad, student, vectors, pre_second, outputs, activated,
    grad_second, grad_down, shards, sums_ref, *, sums, ratio,
):
    step = pl.program_id(0)
    count, hidden = pre_second.shape

    @pl.when(step == 0)
    def _():
        gain = turned(vectors[...])[GAIN2 : GAIN2 + 1]
        place = lax.broadcasted_iota(jnp.int32, (CHUNK, returned.shape[0]), 1)
        parts = []
        for low in range(0, count, CHUNK):
            cut = slice(low, low + CHUNK)
            pick = (slot[cut] == place).astype(BF16)
            grad = matmul(pick, returned[...]) + right_inner(student_grad[cut], student[...])
            result, gain_part, bias_part = norm_grad(grad, pre_second[cut], gain)
            grad_second[cut] = result
            low_result = narrow(result)
            grad_down[cut] = low_result
            parts.append((jnp.sum(widen(low_result), axis=0, keepdims=True), gain_part, bias_part))
        for i in range(3):
            sums_ref[i : i + 1] = sum(part[i] for part in parts)

    sums.store(
        shards,
        left_inner(activated[...], grad_down[...]),
        pl.multiple_of(step * hidden, LANES),
    )

    @pl.when(step == pl.num_programs(0) - 1)
    def _():
        sums.store(shards, left_inner(outputs[...], student_grad[...]), ratio * hidden)
        vector_rows = [sums_ref[i : i + 1] for i in range(3)]
        sums.store(shards, as_columns(vector_rows, 3, hidden), ratio * hidden + SD)


def up_grad_body(
    grad_down, grad_second, down, up, slope, normed, pre_first, context, vectors,
    grad_first, grad_branch, shards, total, bias_rows, *, sums, ratio,
):
    step = pl.program_id(0)
    count, hidden = pre_first.shape
    bias_part = 0.0
    pieces = []
    for low in range(0, count, CHUNK):
        cut = slice(low, low + CHUNK)
        grad = right_inner(grad_down[cut], down[...])
        grad = narrow(grad * widen(slope[cut]))
        pieces.append(grad)
        bias_part = bias_part + jnp.sum(widen(grad), axis=0, keepdims=True)
        update = right_inner(grad, up[...])

        @pl.when(step == 0)
        def _():
            total[cut] = grad_second[cut] + update

        @pl.when(step > 0)
        def _():
            total[cut] += update

    bias_rows[pl.ds(step, 1)] = bias_part
    sums.store(
        shards,
        left_inner(normed[...], jnp.concatenate(pieces, axis=0)),
        pl.multiple_of(step * hidden, LANES),
    )

    @pl.when(step == pl.num_programs(0) - 1)
    def _():
        gain = turned(vectors[...])[GAIN1 : GAIN1 + 1]
        parts = []
        for low in range(0, count, CHUNK):
            cut = slice(low, low + CHUNK)
            result, gain_part, shift_part = norm_grad(total[cut], pre_first[cut], gain)
            grad_first[cut] = result
            low_result = narrow(result)
            grad_branch[cut] = low_result
            parts.append((jnp.sum(widen(low_result), axis=0, keepdims=True), gain_part, shift_part))
        vector_rows = [sum(part[i] for part in parts) for i in range(3)]
        vector_rows += [bias_rows[i : i + 1] for i in range(ratio)]
        sums.store(shards, left_inner(context[...], grad_branch[...]), ratio * hidden)
        sums.store(
            shards, as_columns(vector_rows, 3 + ratio, hidden), (ratio + 1) * hidden
        )


def qkv_grad_body(tokens, grads, shards, bias_rows, *, sums):
    step = pl.program_id(0)
    hidden = tokens.shape[1]
    grad = grads[0]
    bias_rows[pl.ds(step, 1)] = jnp.sum(widen(grad), axis=0, keepdims=True)
    sums.store(
        shards, left_inner(tokens[...], grad), pl.multiple_of(step * hidden, LANES)
    )

    @pl.when(step == pl.num_programs(0) - 1)
    def _():
        vector_rows = [bias_rows[0:1], bias_rows[2:3]]
        sums.store(shards, as_columns(vector_rows, 2, hidden), 3 * hidden)


def token_grad_body(grads, weight, grad_first, result, total):
    step = pl.program_id(0)
    update = right_inner(grads[0], weight[...])

    @pl.when(step == 0)
    def _():
        total[...] = grad_first[...] + update

    @pl.when(step > 0)
    def _():
        total[...] += update

    @pl.when(step == pl.num_programs(0) - 1)
    def _():
        result[...] = narrow(total[...])


def local(
    layout,
    tokens,
    lengths,
    exit_layers,
    destination,
    carried_grad,
    logits_grad,
    qkv_weight,
    query_bias,
    value_bias,
    out_weight,
    out_bias,
    norm1_gain,
    norm1_bias,
    up_weight,
    up_bias,
    down_weight,
    down_bias,
    norm2_gain,
    norm2_bias,
    student_weight,
    student_bias,
    pool_query,
    dense_weight,
    dense_bias,
    class_weight,
    class_bias,
):
    axes, count, dp_count = layout.axes, layout.count, layout.dp_count
    pair_count = lengths.shape[1]
    slots = carried_grad.shape[0]
    slot_width = slots // dp_count
    token_count, hidden = tokens.shape
    inner_dim = up_weight.shape[1]
    part = hidden // count
    ratio = inner_dim // hidden
    classes = class_weight.shape[1]
    sums = Sums(layout, hidden)
    width = 2 * LANES
    blocks = hidden // width
    micro = token_count // ROW

    def array(*shape, dtype=F32):
        return jax.ShapeDtypeStruct(shape, dtype)

    vector_list = (
        query_bias, value_bias, out_bias, norm1_gain, norm1_bias, down_bias, norm2_gain, norm2_bias,
    )
    columns = jnp.concatenate(
        [v[:, None] for v in vector_list]
        + [up_bias.reshape(part, ratio), jnp.zeros((part, LANES - len(vector_list) - ratio), BF16)],
        axis=1,
    )
    packed_width = (4 + 2 * ratio) * hidden + SD + LANES
    packed = pl.pallas_call(
        functools.partial(pack_body, ratio=ratio, hidden=hidden),
        out_shape=array(part, packed_width, dtype=BF16),
        compiler_params=params(),
        name="pack",
    )(qkv_weight, out_weight, up_weight, down_weight, student_weight, columns)
    gathered = lax.all_gather(packed, axes, axis=0, tiled=True)
    student_at = (4 + 2 * ratio) * hidden // LANES
    out_spec = fixed((hidden, hidden), 0, 3)
    up_spec = pl.BlockSpec((hidden, hidden), lambda j: (0, 4 + j))
    down_spec = pl.BlockSpec((hidden, hidden), lambda j: (0, 4 + ratio + j))
    student_spec = fixed((hidden, SD), 0, student_at)
    vector_spec = fixed((hidden, LANES), 0, student_at + 1)
    full_spec = fixed((token_count, hidden))
    column_spec = pl.BlockSpec((token_count, hidden), lambda j: (0, j))

    place = jnp.arange(ROW, dtype=jnp.int32)
    pair_ids = jnp.arange(pair_count, dtype=jnp.int32)
    ends = jnp.cumsum(lengths, axis=1)
    starts = ends - lengths
    alive = (exit_layers > LAYER).astype(jnp.int32)
    targets = destination.reshape(micro, pair_count)
    segment = jnp.sum((place[None, :, None] >= ends[:, None, :]).astype(jnp.int32), axis=2)
    member = (segment[:, :, None] == pair_ids[None, None, :]).astype(jnp.int32)
    token_slot = jnp.sum(
        member * jnp.where(alive > 0, targets * slot_width - starts, -slots - ROW)[:, None, :], axis=2
    ) + place[None, :]
    token_slot = jnp.where(token_slot < 0, -1, token_slot).reshape(token_count, 1)
    flat_segment = (segment + pair_count * jnp.arange(micro, dtype=jnp.int32)[:, None]).reshape(
        token_count, 1
    )
    seg_column, seg_row = segment[:, :, None], segment[:, None, :]
    flat_starts = (starts + ROW * jnp.arange(micro, dtype=jnp.int32)[:, None]).reshape(-1)
    dp_ids = jnp.arange(dp_count, dtype=jnp.int32)
    chosen = (destination.reshape(-1)[None, :] == dp_ids[:, None]).astype(jnp.int32)
    send_start = jnp.sum(chosen * flat_starts[None, :], axis=1)
    send_length = jnp.sum(chosen * (lengths * alive).reshape(-1)[None, :], axis=1)
    slot_place = jnp.arange(slot_width, dtype=jnp.int32)
    slot_token = jnp.where(
        slot_place[None, :] < send_length[:, None], send_start[:, None] + slot_place[None, :], -1
    ).reshape(slots, 1)

    returned = lax.all_to_all(carried_grad, layout.dp, split_axis=0, concat_axis=0, tiled=True)

    row_specs = [
        pl.BlockSpec((1, ROW, 1), lambda r, p: (r, 0, 0)),
        pl.BlockSpec((1, 1, ROW), lambda r, p: (r, 0, 0)),
    ]
    block_spec = pl.BlockSpec((ROW, width), lambda r, p: (r, p))
    pair_flops = 2 * token_count * ROW * hidden
    query, key, value, context = pl.pallas_call(
        attention_body,
        grid=(micro, blocks),
        in_specs=[pl.BlockSpec((ROW, hidden), lambda r, p: (r, 0))]
        + row_specs
        + [
            pl.BlockSpec((hidden, width), lambda r, p: (0, p)),
            pl.BlockSpec((hidden, width), lambda r, p: (0, blocks + p)),
            pl.BlockSpec((hidden, width), lambda r, p: (0, 2 * blocks + p)),
            vector_spec,
        ],
        out_specs=(block_spec,) * 4,
        out_shape=(array(token_count, hidden, dtype=BF16),) * 4,
        scratch_shapes=[pltpu.VMEM((ROW, ROW), F32), pltpu.VMEM((LANES, hidden), F32)],
        compiler_params=params(),
        cost_estimate=cost(16e9, 12e6),
        name="attention",
    )(tokens, seg_column, seg_row, gathered, gathered, gathered, gathered)

    pre_first, normed, activated, slope, pre_second, outputs, student_rows = pl.pallas_call(
        forward_body,
        grid=(ratio,),
        in_specs=[full_spec, full_spec, out_spec, up_spec, down_spec, student_spec, vector_spec, fixed((1, SD))],
        out_specs=(full_spec, full_spec, column_spec, column_spec, full_spec, full_spec, fixed((token_count, SD))),
        out_shape=(
            array(token_count, hidden),
            array(token_count, hidden, dtype=BF16),
            array(token_count, inner_dim, dtype=BF16),
            array(token_count, inner_dim, dtype=BF16),
            array(token_count, hidden),
            array(token_count, hidden, dtype=BF16),
            array(token_count, SD),
        ),
        scratch_shapes=[pltpu.VMEM((token_count, hidden), F32), pltpu.VMEM((LANES, hidden), F32)],
        compiler_params=params(),
        cost_estimate=cost(16e9, 30e6),
        name="forward",
    )(tokens, context, gathered, gathered, gathered, gathered, gathered, student_bias[None, :])

    step = 512 if slots % 512 == 0 else slots
    outgoing = pl.pallas_call(
        select_body,
        grid=(slots // step,),
        in_specs=[pl.BlockSpec((step, 1), lambda i: (i, 0)), full_spec],
        out_specs=pl.BlockSpec((step, hidden), lambda i: (i, 0)),
        out_shape=array(slots, hidden, dtype=BF16),
        compiler_params=params(),
        cost_estimate=cost(2.4e9, 5e6),
        name="select",
    )(slot_token, outputs)
    carried = lax.all_to_all(outgoing, layout.dp, split_axis=0, concat_axis=0, tiled=True)

    small_rows = -(-(SD + classes) // 8) * 8
    logits, student_grad, small = pl.pallas_call(
        functools.partial(student_body, small_rows=small_rows),
        out_shape=(
            array(*logits_grad.shape),
            array(token_count, SD, dtype=BF16),
            array(small_rows + 8, SD),
        ),
        compiler_params=params(),
        cost_estimate=cost(1e9, 2e6),
        name="student",
    )(
        student_rows, flat_segment, pool_query[None, :], dense_weight, dense_bias[None, :],
        class_weight, class_bias[None, :], logits_grad,
    )
    small = jnp.sum(
        lax.all_gather(small, axes, axis=0, tiled=False).reshape((count,) + small.shape), axis=0
    )

    first_width = ratio * hidden + SD + LANES
    grad_second, grad_down, first = pl.pallas_call(
        functools.partial(down_grad_body, sums=sums, ratio=ratio),
        grid=(ratio,),
        in_specs=[
            fixed((token_count, 1)), fixed((slots, hidden)), fixed((token_count, SD)), student_spec,
            vector_spec, full_spec, full_spec, column_spec,
        ],
        out_specs=(full_spec, full_spec, sums.spec(first_width)),
        out_shape=(
            array(token_count, hidden),
            array(token_count, hidden, dtype=BF16),
            sums.shape(first_width),
        ),
        scratch_shapes=[pltpu.VMEM((8, hidden), F32)],
        compiler_params=params(),
        cost_estimate=cost(10e9, 25e6),
        name="down_grad",
    )(token_slot, returned, student_grad, gathered, gathered, pre_second, outputs, activated)
    first_sum = layout.scatter_sum(sums.parts(first))

    second_width = (ratio + 1) * hidden + LANES
    grad_first, grad_branch, second = pl.pallas_call(
        functools.partial(up_grad_body, sums=sums, ratio=ratio),
        grid=(ratio,),
        in_specs=[
            full_spec, full_spec, down_spec, up_spec, column_spec, full_spec, full_spec, full_spec, vector_spec,
        ],
        out_specs=(full_spec, full_spec, sums.spec(second_width)),
        out_shape=(
            array(token_count, hidden),
            array(token_count, hidden, dtype=BF16),
            sums.shape(second_width),
        ),
        scratch_shapes=[pltpu.VMEM((token_count, hidden), F32), pltpu.VMEM((8, hidden), F32)],
        compiler_params=params(),
        cost_estimate=cost(20e9, 35e6),
        name="up_grad",
    )(grad_down, grad_second, gathered, gathered, slope, normed, pre_first, context, gathered)
    second_sum = layout.scatter_sum(sums.parts(second))

    grads = pl.pallas_call(
        attention_grad_body,
        grid=(micro, blocks),
        in_specs=[pl.BlockSpec((ROW, hidden), lambda r, p: (r, 0))]
        + row_specs
        + [block_spec] * 3
        + [pl.BlockSpec((width, hidden), lambda r, p: (p, 3))],
        out_specs=pl.BlockSpec((3, ROW, width), lambda r, p: (0, r, p)),
        out_shape=array(3, token_count, hidden, dtype=BF16),
        scratch_shapes=[pltpu.VMEM((ROW, ROW), F32)],
        compiler_params=params(),
        cost_estimate=cost(28e9, 15e6),
        name="attention_grad",
    )(grad_branch, seg_column, seg_row, query, key, value, gathered)

    third_width = 3 * hidden + LANES
    grads_spec = pl.BlockSpec((1, token_count, hidden), lambda j: (j, 0, 0))
    third = pl.pallas_call(
        functools.partial(qkv_grad_body, sums=sums),
        grid=(3,),
        in_specs=[full_spec, grads_spec],
        out_specs=sums.spec(third_width),
        out_shape=sums.shape(third_width),
        scratch_shapes=[pltpu.VMEM((8, hidden), F32)],
        compiler_params=params(),
        cost_estimate=cost(4e9, 10e6),
        name="qkv_grad",
    )(tokens, grads)
    third_sum = layout.scatter_sum(sums.parts(third))
    tokens_grad = pl.pallas_call(
        token_grad_body,
        grid=(3,),
        in_specs=[grads_spec, pl.BlockSpec((hidden, hidden), lambda j: (0, j)), full_spec],
        out_specs=full_spec,
        out_shape=array(token_count, hidden, dtype=BF16),
        scratch_shapes=[pltpu.VMEM((token_count, hidden), F32)],
        compiler_params=params(),
        cost_estimate=cost(4e9, 14e6),
        name="token_grad",
    )(grads, gathered, grad_first)

    down_grad = first_sum[:, : ratio * hidden].reshape(ratio * part, hidden)
    student_weight_grad = first_sum[:, ratio * hidden : ratio * hidden + SD]
    first_vectors = first_sum[:, ratio * hidden + SD :]
    up_grad = (
        second_sum[:, : ratio * hidden]
        .reshape(part, ratio, hidden)
        .transpose(0, 2, 1)
        .reshape(part, ratio * hidden)
    )
    out_grad = second_sum[:, ratio * hidden : (ratio + 1) * hidden]
    second_vectors = second_sum[:, (ratio + 1) * hidden :]
    qkv_grad = third_sum[:, : 3 * hidden]
    third_vectors = third_sum[:, 3 * hidden :]
    return (
        carried,
        logits,
        tokens_grad,
        qkv_grad,
        third_vectors[:, 0],
        third_vectors[:, 1],
        out_grad,
        second_vectors[:, 0],
        second_vectors[:, 1],
        second_vectors[:, 2],
        up_grad,
        second_vectors[:, 3 : 3 + ratio].reshape(-1),
        down_grad,
        first_vectors[:, 0],
        first_vectors[:, 1],
        first_vectors[:, 2],
        student_weight_grad,
        small[small_rows + 3],
        small[small_rows + 2],
        small[:SD],
        small[small_rows],
        small[SD : SD + classes].T,
        small[small_rows + 1, :classes],
    )


def solution(mesh):
    layout = Layout(mesh)
    rows, flat, whole = P(layout.axes, None), P(layout.axes), P()

    def step(*args):
        return local(layout, *args)

    shard = (flat, flat, rows, flat, flat, flat, rows, flat, rows, flat, flat, flat, rows)
    return jax.shard_map(
        step,
        mesh=layout.mesh,
        in_specs=(rows,) * 7 + shard + (whole,) * 6,
        out_specs=(rows,) * 4 + shard + (whole,) * 6,
        check_vma=False,
    )
```

```python
import functools
import math

import jax
import jax.numpy as jnp
from jax import lax
from jax.experimental import pallas as pl
from jax.experimental.pallas import tpu as pltpu
from jax.sharding import Mesh
from jax.sharding import PartitionSpec as P

HD = 64
SD = 128
SH = 2
LAYER = 3
ROW = 512
MICRO = 2
LANES = 128

BF16 = jnp.bfloat16
F32 = jnp.float32
highest = lax.Precision.HIGHEST
norm_eps = 1e-12
masked_value = -1e30

QUERY_BIAS, VALUE_BIAS, OUT_BIAS, GAIN1, BIAS1, DOWN_BIAS, GAIN2, BIAS2, UP_BIAS = range(9)


def narrow(value):
    return value.astype(BF16)


def widen(value):
    return value.astype(F32)


def matmul(left, right, precision=None):
    return lax.dot_general(
        left, right, (((1,), (0,)), ((), ())), preferred_element_type=F32, precision=precision
    )


def left_inner(left, right, precision=None):
    return lax.dot_general(
        left, right, (((0,), (0,)), ((), ())), preferred_element_type=F32, precision=precision
    )


def right_inner(left, right, precision=None):
    return lax.dot_general(
        left, right, (((1,), (1,)), ((), ())), preferred_element_type=F32, precision=precision
    )


def params(*semantics, limit=58):
    return pltpu.CompilerParams(
        dimension_semantics=semantics or None, vmem_limit_bytes=limit * 1024 * 1024
    )


def cost(flops, nbytes, transcendentals=0):
    return pl.CostEstimate(
        flops=int(flops), bytes_accessed=int(nbytes), transcendentals=int(transcendentals)
    )


def fixed(shape, *at):
    where = at or (0,) * len(shape)
    return pl.BlockSpec(shape, lambda *_: where)


class Layout:
    def __init__(self, mesh):
        dp, fsdp = mesh.shape["dp"], mesh.shape["fsdp"]
        devices = mesh.devices
        if (dp, fsdp) == (8, 4):
            self.mesh = Mesh(devices.reshape(4, 2, 2, 2), ("z", "x", "y", "core"))
            self.dp = ("z", "x")
            self.stages = (("core",), ("x", "y"), ("z",))
        elif (dp, fsdp) == (64, 4):
            self.mesh = Mesh(devices.reshape(8, 4, 2, 4), ("z", "x", "core", "y"))
            self.dp = ("z", "x", "core")
            self.stages = (("core",), ("x", "y"), ("z",))
        else:
            self.mesh = mesh
            self.dp = ("dp",)
            self.stages = (("fsdp",), ("dp",))
        self.axes = tuple(self.mesh.axis_names)
        self.sizes = tuple(self.mesh.shape[name] for name in self.axes)
        self.count = math.prod(self.sizes)
        self.dp_count = dp
        self.extents = tuple(math.prod(self.mesh.shape[n] for n in stage) for stage in self.stages)
        order = [self.axes.index(name) for stage in self.stages for name in stage]
        self.place = []
        for device in range(self.count):
            at, rest = [], device
            for size in reversed(self.sizes):
                at.append(rest % size)
                rest //= size
            at = at[::-1]
            position = 0
            for axis in order:
                position = position * self.sizes[axis] + at[axis]
            self.place.append(position)
        self.device_at = [self.place.index(i) for i in range(self.count)]

    def exchange(self, value, stage):
        extent = self.extents[stage]
        value = value.reshape((extent, value.shape[0] // extent) + value.shape[1:])
        return lax.all_to_all(
            value, self.stages[stage], split_axis=0, concat_axis=0, tiled=True
        )

    def gather(self, value):
        for stage in reversed(range(len(self.stages))):
            copies = jnp.broadcast_to(value, (self.extents[stage],) + value.shape)
            value = lax.all_to_all(
                copies, self.stages[stage], split_axis=0, concat_axis=0, tiled=True
            )
        order = [name for stage in self.stages for name in stage]
        tail = value.shape[-2:]
        value = value.reshape(tuple(self.mesh.shape[name] for name in order) + tail)
        back = tuple(order.index(name) for name in self.axes)
        value = value.transpose(back + (len(order), len(order) + 1))
        return value.reshape(self.count * tail[0], tail[1])

    def permutes(self, value, stage):
        extent, axes = self.extents[stage], self.stages[stage]
        value = value.reshape((extent, value.shape[0] // extent) + value.shape[1:])
        me = lax.axis_index(axes)
        parts = [lax.dynamic_index_in_dim(value, me, 0, keepdims=False)]
        for step in range(1, extent):
            part = lax.dynamic_index_in_dim(value, lax.rem(me + step, extent), 0, keepdims=False)
            pairs = [(i, (i + step) % extent) for i in range(extent)]
            parts.append(lax.ppermute(part, axes, pairs))
        return parts

    def total(self, arrived, dtype=BF16):
        if isinstance(arrived, list):
            return sum(widen(part) for part in arrived).astype(dtype)
        return jnp.sum(widen(arrived), axis=0).astype(dtype)


def store_parts(ref, value, place, column):
    count, part, _ = ref.shape
    width = value.shape[1]
    value = value.astype(ref.dtype) if part % 16 == 0 else value
    for device in range(count):
        ref[place[device], :, pl.ds(column, width)] = value[
            device * part : (device + 1) * part
        ].astype(ref.dtype)


class Sums:
    def __init__(self, layout, rows, split=True):
        self.layout = layout
        self.count, self.part = layout.count, rows // layout.count
        self.split = split and self.part % 8 == 0

    def shape(self, columns):
        if self.split:
            return jax.ShapeDtypeStruct((self.count, self.part, columns), BF16)
        return jax.ShapeDtypeStruct((self.count * self.part, columns), BF16)

    def spec(self, columns):
        return fixed(self.shape(columns).shape)

    def store(self, ref, value, column):
        if self.split:
            store_parts(ref, value, self.layout.place, column)
        else:
            ref[:, pl.ds(column, value.shape[1])] = value.astype(ref.dtype)

    def parts(self, value):
        if self.split:
            return value
        value = value.reshape(self.count, self.part, value.shape[1])
        return value[jnp.asarray(self.layout.device_at)]


def interleave(width, ratio, dtype):
    size = width * ratio
    source = lax.broadcasted_iota(jnp.int32, (size, size), 0)
    target = lax.broadcasted_iota(jnp.int32, (size, size), 1)
    return (source == (target % width) * ratio + target // width).astype(dtype)


def pack_body(out, up, down, student, packed, *, ratio, hidden):
    part = out.shape[0]
    packed[:, :hidden] = out[...]
    base = hidden
    mix = interleave(LANES, ratio, BF16)
    for chunk in range(hidden // LANES):
        piece = narrow(
            matmul(up[:, chunk * ratio * LANES : (chunk + 1) * ratio * LANES], mix)
        )
        for j in range(ratio):
            at = base + j * hidden + chunk * LANES
            packed[:, at : at + LANES] = piece[:, j * LANES : (j + 1) * LANES]
    base += ratio * hidden
    row = lax.broadcasted_iota(jnp.int32, (part, part * ratio), 0)
    column = lax.broadcasted_iota(jnp.int32, (part, part * ratio), 1)
    for j in range(ratio):
        pick = (column == row * ratio + j).astype(BF16)
        packed[:, base + j * hidden : base + (j + 1) * hidden] = narrow(matmul(pick, down[...]))
    base += ratio * hidden
    packed[:, base : base + SD] = student[...]


def turned(vectors):
    return widen(vectors).T


def attention_body(
    tokens, seg_column, seg_row, wq, wk, wv, vectors, query, key, value, context, mask, rows
):
    step = pl.program_id(1)
    width = wq.shape[1]

    @pl.when((step == 0) & (pl.program_id(0) == 0))
    def _():
        rows[...] = turned(vectors[...])

    @pl.when(step == 0)
    def _():
        mask[...] = jnp.where(seg_column[0] == seg_row[0], 0.0, masked_value)

    here = pl.ds(pl.multiple_of(step * width, width), width)
    x = tokens[...]
    q = narrow(matmul(x, wq[...]) + rows[QUERY_BIAS : QUERY_BIAS + 1, here])
    k = narrow(matmul(x, wk[...]))
    v = narrow(matmul(x, wv[...]) + rows[VALUE_BIAS : VALUE_BIAS + 1, here])
    query[...] = q
    key[...] = k
    value[...] = v
    lane = lax.broadcasted_iota(jnp.int32, (x.shape[0], LANES), 1)
    scale = BF16(1.0 / math.sqrt(HD))
    for block in range(width // LANES):
        cut = slice(block * LANES, (block + 1) * LANES)
        q_block, k_block, v_turned = q[:, cut] * scale, k[:, cut], v[:, cut].T
        parts = []
        for head in range(LANES // HD):
            mine = (lane >= head * HD) & (lane < (head + 1) * HD)
            scores = right_inner(k_block, jnp.where(mine, q_block, BF16(0))) + mask[...]
            exponent = jnp.exp(scores - jnp.max(scores, axis=0, keepdims=True))
            total = jnp.sum(exponent, axis=0, keepdims=True)
            probs = narrow(exponent * (1.0 / total))
            parts.append(matmul(v_turned[head * HD : (head + 1) * HD], probs))
        context[:, cut] = narrow(jnp.concatenate(parts, axis=0)).T


def attention_grad_body(
    branch, seg_column, seg_row, query, key, value, out_weight, grads, mask
):
    width = query.shape[1]

    @pl.when(pl.program_id(1) == 0)
    def _():
        mask[...] = jnp.where(seg_column[0] == seg_row[0], 0.0, masked_value)

    grad_context = narrow(right_inner(branch[...], out_weight[...]))
    lane = lax.broadcasted_iota(jnp.int32, (branch.shape[0], LANES), 1)
    scale = 1.0 / math.sqrt(HD)
    for block in range(width // LANES):
        cut = slice(block * LANES, (block + 1) * LANES)
        q_block, k_block, v_block = query[:, cut] * BF16(scale), key[:, cut], value[:, cut]
        g_block, k_turned = grad_context[:, cut], k_block.T
        grad_q, grad_k, grad_v = [], 0.0, 0.0
        for head in range(LANES // HD):
            mine = (lane >= head * HD) & (lane < (head + 1) * HD)
            q_head = jnp.where(mine, q_block, BF16(0))
            g_head = jnp.where(mine, g_block, BF16(0))
            scores = right_inner(k_block, q_head) + mask[...]
            exponent = jnp.exp(scores - jnp.max(scores, axis=0, keepdims=True))
            total = jnp.sum(exponent, axis=0, keepdims=True)
            probs = exponent * (1.0 / total)
            grad_probs = right_inner(v_block, g_head)
            inner = jnp.sum(probs * grad_probs, axis=0, keepdims=True)
            grad_scores = narrow(probs * (grad_probs - inner))
            grad_v += matmul(narrow(probs), g_head)
            grad_k += matmul(grad_scores, q_head)
            grad_q.append(matmul(k_turned[head * HD : (head + 1) * HD], grad_scores))
        grads[0, :, cut] = narrow(jnp.concatenate(grad_q, axis=0) * scale).T
        grads[1, :, cut] = narrow(grad_k)
        grads[2, :, cut] = narrow(grad_v)


def attention_grad_next_body(*refs):
    attention_grad_body(*refs[:7], *refs[8:])


def normalize(values):
    average = jnp.mean(values, axis=-1, keepdims=True)
    centered = values - average
    spread = jnp.mean(centered * centered, axis=-1, keepdims=True)
    scale = lax.rsqrt(spread + norm_eps)
    return centered * scale, scale


def gelu_and_slope(x):
    phi = 0.5 + 0.5 * lax.erf(x * math.sqrt(0.5))
    return x * phi, phi + x * (jnp.exp(-0.5 * (x * x)) * (1.0 / math.sqrt(2.0 * math.pi)))


CHUNK = 256


def forward_body(
    tokens, context, out_weight, up, down, student, vectors, student_bias,
    pre_first, normed, activated, slope, pre_second, outputs, student_rows, total, rows,
):
    step = pl.program_id(0)
    count = tokens.shape[0]

    @pl.when(step == 0)
    def _():
        rows[...] = turned(vectors[...])
        for low in range(0, count, CHUNK):
            cut = slice(low, low + CHUNK)
            pre = (
                widen(tokens[cut])
                + matmul(context[cut], out_weight[...])
                + rows[OUT_BIAS : OUT_BIAS + 1]
            )
            pre_first[cut] = pre
            hat, _ = normalize(pre)
            value = narrow(hat * rows[GAIN1 : GAIN1 + 1] + rows[BIAS1 : BIAS1 + 1])
            normed[cut] = value
            total[cut] = widen(value) + rows[DOWN_BIAS : DOWN_BIAS + 1]

    bias = rows[pl.ds(UP_BIAS + step, 1)]
    for low in range(0, count, CHUNK):
        cut = slice(low, low + CHUNK)
        value, grad = gelu_and_slope(matmul(normed[cut], up[...]) + bias)
        value = narrow(value)
        activated[cut] = value
        slope[cut] = narrow(grad)
        total[cut] += matmul(value, down[...])

    @pl.when(step == pl.num_programs(0) - 1)
    def _():
        for low in range(0, count, CHUNK):
            cut = slice(low, low + CHUNK)
            pre = total[cut]
            pre_second[cut] = pre
            hat, _ = normalize(pre)
            value = narrow(hat * rows[GAIN2 : GAIN2 + 1] + rows[BIAS2 : BIAS2 + 1])
            outputs[cut] = value
            student_rows[cut] = matmul(value, student[...]) + student_bias[...]


def select_body(index, source, target):
    place = lax.broadcasted_iota(jnp.int32, (index.shape[0], source.shape[0]), 1)
    target[...] = narrow(matmul((index[...] == place).astype(BF16), source[...]))


def student_body(
    student_rows, segment, query, dense_weight, dense_bias, class_weight, class_bias, logits_grad,
    logits, student_grad, small,
):
    count, _ = student_rows.shape
    pairs, classes = logits_grad.shape
    wide = -(-pairs // LANES) * LANES
    head = SD // SH
    scale = 1.0 / math.sqrt(head)
    rows = student_rows[...]
    member = segment[...] == lax.broadcasted_iota(jnp.int32, (count, wide), 1)
    one_hot = member.astype(F32)
    lane = lax.broadcasted_iota(jnp.int32, (count, SD), 1)

    def by_head(values):
        return [
            jnp.sum(
                jnp.where((lane >= a * head) & (lane < (a + 1) * head), values, 0.0),
                axis=1,
                keepdims=True,
            )
            for a in range(SH)
        ]

    def spread(columns):
        value = columns[0]
        for a in range(1, SH):
            value = jnp.where(lane >= a * head, columns[a], value)
        return jnp.broadcast_to(value, (count, SD))

    def of_pair(row):
        return jnp.sum(jnp.where(member, row, 0.0), axis=1, keepdims=True)

    def over_pair(column):
        return jnp.sum(jnp.where(member, column, 0.0), axis=0, keepdims=True)

    weights = []
    for score in by_head(rows * query[...]):
        score = score * scale
        top = jnp.max(jnp.where(member, score, masked_value), axis=0, keepdims=True)
        exponent = jnp.exp(score - of_pair(top))
        weights.append(exponent / of_pair(over_pair(exponent)))
    weight = spread(weights)
    pooled = left_inner(one_hot, weight * rows, highest)
    dense = jnp.tanh(matmul(pooled, dense_weight[...], highest) + dense_bias[...])
    logits[...] = matmul(dense[:pairs], class_weight[...], highest) + class_bias[...]

    grad = logits_grad[...]
    grad_pre = right_inner(grad, class_weight[...], highest) * (
        1.0 - dense[:pairs] * dense[:pairs]
    )
    small[...] = jnp.zeros_like(small)
    small[:pairs] = pooled[:pairs]
    small[pairs : 2 * pairs] = grad_pre
    small[2 * pairs : 3 * pairs] = dense[:pairs]
    small[3 * pairs : 4 * pairs, :classes] = grad
    at = 4 * pairs
    grad_pooled = right_inner(grad_pre, dense_weight[...], highest)
    grad_token = matmul(one_hot[:, :pairs], grad_pooled, highest)
    grad_score = []
    for a, inner in enumerate(by_head(rows * grad_token)):
        product = weights[a] * inner
        grad_score.append(weights[a] * (inner - of_pair(over_pair(product))))
    grad_score = spread(grad_score) * scale
    small[at : at + 1] = jnp.sum(grad_score * rows, axis=0, keepdims=True)
    result = narrow(weight * grad_token + grad_score * query[...])
    student_grad[...] = result
    small[at + 1 : at + 2] = jnp.sum(widen(result), axis=0, keepdims=True)


def head_sums_body(gathered, dense_weight_grad, class_weight_grad, rows, *, pairs):
    everyone = gathered[...]
    width = everyone.shape[2]

    def factor(i):
        return everyone[:, i * pairs : (i + 1) * pairs].reshape(-1, width)

    pooled, grad_pre, dense, grad = (factor(i) for i in range(4))
    dense_weight_grad[...] = left_inner(pooled, grad_pre, highest)
    class_weight_grad[...] = left_inner(dense, grad, highest)
    total = jnp.sum(everyone[:, 4 * pairs : 4 * pairs + 8], axis=0)
    row = lax.broadcasted_iota(jnp.int32, (8, width), 0)
    total = jnp.where(row == 2, jnp.sum(grad_pre, axis=0, keepdims=True), total)
    rows[...] = jnp.where(row == 3, jnp.sum(grad, axis=0, keepdims=True), total)


def norm_grad(grad, pre, gain):
    hat, scale = normalize(pre)
    scaled = grad * gain
    result = scale * (
        scaled
        - jnp.mean(scaled, axis=-1, keepdims=True)
        - hat * jnp.mean(scaled * hat, axis=-1, keepdims=True)
    )
    return (
        result,
        jnp.sum(grad * hat, axis=0, keepdims=True),
        jnp.sum(grad, axis=0, keepdims=True),
    )


def as_columns(rows, count, hidden):
    row = lax.broadcasted_iota(jnp.int32, (LANES, hidden), 0)
    block = jnp.zeros((LANES, hidden), F32)
    for i in range(count):
        block = jnp.where(row == i, rows[i], block)
    return block.T


def down_grad_body(
    slot, returned, student_grad, student, vectors, pre_second, outputs, activated,
    grad_second, grad_down, shards, sums_ref, *, sums, ratio,
):
    step = pl.program_id(0)
    count, hidden = pre_second.shape

    @pl.when(step == 0)
    def _():
        gain = turned(vectors[...])[GAIN2 : GAIN2 + 1]
        place = lax.broadcasted_iota(jnp.int32, (CHUNK, returned.shape[0]), 1)
        parts = []
        for low in range(0, count, CHUNK):
            cut = slice(low, low + CHUNK)
            pick = (slot[cut] == place).astype(BF16)
            grad = matmul(pick, returned[...]) + right_inner(student_grad[cut], student[...])
            result, gain_part, bias_part = norm_grad(grad, pre_second[cut], gain)
            grad_second[cut] = result
            low_result = narrow(result)
            grad_down[cut] = low_result
            parts.append((jnp.sum(widen(low_result), axis=0, keepdims=True), gain_part, bias_part))
        for i in range(3):
            sums_ref[i : i + 1] = sum(part[i] for part in parts)

    sums.store(
        shards,
        left_inner(activated[...], grad_down[...]),
        pl.multiple_of(step * hidden, LANES),
    )

    @pl.when(step == pl.num_programs(0) - 1)
    def _():
        sums.store(shards, left_inner(outputs[...], student_grad[...]), ratio * hidden)
        vector_rows = [sums_ref[i : i + 1] for i in range(3)]
        sums.store(shards, as_columns(vector_rows, 3, hidden), ratio * hidden + SD)


def up_grad_body(
    grad_down, grad_second, down, up, slope, normed, pre_first, context, vectors,
    grad_first, grad_branch, shards, total, bias_rows, *, sums, ratio,
):
    step = pl.program_id(0)
    count, hidden = pre_first.shape

    @pl.when(step == 0)
    def _():
        total[...] = grad_second[...]

    bias_part = 0.0
    pieces = []
    for low in range(0, count, CHUNK):
        cut = slice(low, low + CHUNK)
        grad = right_inner(grad_down[cut], down[...])
        grad = narrow(grad * widen(slope[cut]))
        pieces.append(grad)
        bias_part = bias_part + jnp.sum(widen(grad), axis=0, keepdims=True)
        total[cut] += right_inner(grad, up[...])

    bias_rows[pl.ds(step, 1)] = bias_part
    sums.store(
        shards,
        left_inner(normed[...], jnp.concatenate(pieces, axis=0)),
        pl.multiple_of(step * hidden, LANES),
    )

    @pl.when(step == pl.num_programs(0) - 1)
    def _():
        gain = turned(vectors[...])[GAIN1 : GAIN1 + 1]
        parts = []
        for low in range(0, count, CHUNK):
            cut = slice(low, low + CHUNK)
            result, gain_part, shift_part = norm_grad(total[cut], pre_first[cut], gain)
            grad_first[cut] = result
            low_result = narrow(result)
            grad_branch[cut] = low_result
            parts.append((jnp.sum(widen(low_result), axis=0, keepdims=True), gain_part, shift_part))
        vector_rows = [sum(part[i] for part in parts) for i in range(3)]
        vector_rows += [bias_rows[i : i + 1] for i in range(ratio)]
        sums.store(shards, left_inner(context[...], grad_branch[...]), ratio * hidden)
        sums.store(
            shards, as_columns(vector_rows, 3 + ratio, hidden), (ratio + 1) * hidden
        )


def qkv_grad_body(tokens, grads, shards, bias_rows, *, sums):
    step = pl.program_id(0)
    hidden = tokens.shape[1]
    grad = grads[0]
    bias_rows[pl.ds(step, 1)] = jnp.sum(widen(grad), axis=0, keepdims=True)
    sums.store(
        shards, left_inner(tokens[...], grad), pl.multiple_of(step * hidden, LANES)
    )

    @pl.when(step == pl.num_programs(0) - 1)
    def _():
        vector_rows = [bias_rows[0:1], bias_rows[2:3]]
        sums.store(shards, as_columns(vector_rows, 2, hidden), 3 * hidden)


def token_grad_body(grads, weight, grad_first, result, total):
    step = pl.program_id(0)
    update = right_inner(grads[0], weight[...])

    @pl.when(step == 0)
    def _():
        total[...] = grad_first[...] + update

    @pl.when(step > 0)
    def _():
        total[...] += update

    @pl.when(step == pl.num_programs(0) - 1)
    def _():
        result[...] = narrow(total[...])


def local(
    layout,
    tokens,
    lengths,
    exit_layers,
    destination,
    carried_grad,
    logits_grad,
    qkv_weight,
    query_bias,
    value_bias,
    out_weight,
    out_bias,
    norm1_gain,
    norm1_bias,
    up_weight,
    up_bias,
    down_weight,
    down_bias,
    norm2_gain,
    norm2_bias,
    student_weight,
    student_bias,
    pool_query,
    dense_weight,
    dense_bias,
    class_weight,
    class_bias,
):
    axes, count, dp_count = layout.axes, layout.count, layout.dp_count
    pair_count = lengths.shape[1]
    slots = carried_grad.shape[0]
    slot_width = slots // dp_count
    token_count, hidden = tokens.shape
    inner_dim = up_weight.shape[1]
    part = hidden // count
    ratio = inner_dim // hidden
    classes = class_weight.shape[1]
    sums, whole_sums = Sums(layout, hidden), Sums(layout, hidden, split=False)
    width = 2 * LANES
    blocks = hidden // width
    micro = token_count // ROW

    def array(*shape, dtype=F32):
        return jax.ShapeDtypeStruct(shape, dtype)

    vector_list = (
        query_bias, value_bias, out_bias, norm1_gain, norm1_bias, down_bias, norm2_gain, norm2_bias,
    )
    columns = jnp.concatenate(
        [v[:, None] for v in vector_list]
        + [up_bias.reshape(part, ratio), jnp.zeros((part, LANES - len(vector_list) - ratio), BF16)],
        axis=1,
    )
    packed_width = (1 + 2 * ratio) * hidden + SD
    packed = pl.pallas_call(
        functools.partial(pack_body, ratio=ratio, hidden=hidden),
        out_shape=array(part, packed_width, dtype=BF16),
        compiler_params=params(),
        name="pack",
    )(out_weight, up_weight, down_weight, student_weight)
    gathered = lax.all_gather(packed, axes, axis=0, tiled=True)
    entry = layout.gather(jnp.concatenate([qkv_weight, columns], axis=1))
    student_at = (1 + 2 * ratio) * hidden // LANES
    out_spec = fixed((hidden, hidden), 0, 0)
    up_spec = pl.BlockSpec((hidden, hidden), lambda j: (0, 1 + j))
    down_spec = pl.BlockSpec((hidden, hidden), lambda j: (0, 1 + ratio + j))
    student_spec = fixed((hidden, SD), 0, student_at)
    vector_spec = fixed((hidden, LANES), 0, 3 * hidden // LANES)
    full_spec = fixed((token_count, hidden))
    column_spec = pl.BlockSpec((token_count, hidden), lambda j: (0, j))

    place = jnp.arange(ROW, dtype=jnp.int32)
    pair_ids = jnp.arange(pair_count, dtype=jnp.int32)
    ends = jnp.cumsum(lengths, axis=1)
    starts = ends - lengths
    alive = (exit_layers > LAYER).astype(jnp.int32)
    targets = destination.reshape(micro, pair_count)
    segment = jnp.sum((place[None, :, None] >= ends[:, None, :]).astype(jnp.int32), axis=2)
    member = (segment[:, :, None] == pair_ids[None, None, :]).astype(jnp.int32)
    token_slot = jnp.sum(
        member * jnp.where(alive > 0, targets * slot_width - starts, -slots - ROW)[:, None, :], axis=2
    ) + place[None, :]
    token_slot = jnp.where(token_slot < 0, -1, token_slot).reshape(token_count, 1)
    flat_segment = (segment + pair_count * jnp.arange(micro, dtype=jnp.int32)[:, None]).reshape(
        token_count, 1
    )
    seg_column, seg_row = segment[:, :, None], segment[:, None, :]
    flat_starts = (starts + ROW * jnp.arange(micro, dtype=jnp.int32)[:, None]).reshape(-1)
    dp_ids = jnp.arange(dp_count, dtype=jnp.int32)
    chosen = (destination.reshape(-1)[None, :] == dp_ids[:, None]).astype(jnp.int32)
    send_start = jnp.sum(chosen * flat_starts[None, :], axis=1)
    send_length = jnp.sum(chosen * (lengths * alive).reshape(-1)[None, :], axis=1)
    slot_place = jnp.arange(slot_width, dtype=jnp.int32)
    slot_token = jnp.where(
        slot_place[None, :] < send_length[:, None], send_start[:, None] + slot_place[None, :], -1
    ).reshape(slots, 1)

    row_specs = [
        pl.BlockSpec((1, ROW, 1), lambda r, p: (r, 0, 0)),
        pl.BlockSpec((1, 1, ROW), lambda r, p: (r, 0, 0)),
    ]
    block_spec = pl.BlockSpec((ROW, width), lambda r, p: (r, p))
    pair_flops = 2 * token_count * ROW * hidden
    query, key, value, context = pl.pallas_call(
        attention_body,
        grid=(micro, blocks),
        in_specs=[pl.BlockSpec((ROW, hidden), lambda r, p: (r, 0))]
        + row_specs
        + [
            pl.BlockSpec((hidden, width), lambda r, p: (0, p)),
            pl.BlockSpec((hidden, width), lambda r, p: (0, blocks + p)),
            pl.BlockSpec((hidden, width), lambda r, p: (0, 2 * blocks + p)),
            vector_spec,
        ],
        out_specs=(block_spec,) * 4,
        out_shape=(array(token_count, hidden, dtype=BF16),) * 4,
        scratch_shapes=[pltpu.VMEM((ROW, ROW), F32), pltpu.VMEM((LANES, hidden), F32)],
        compiler_params=params(),
        cost_estimate=cost(1e6, 1e5),
        name="attention",
    )(tokens, seg_column, seg_row, entry, entry, entry, entry)

    context, carried_grad = lax.optimization_barrier((context, carried_grad))
    returned = lax.all_to_all(carried_grad, layout.dp, split_axis=0, concat_axis=0, tiled=True)

    pre_first, normed, activated, slope, pre_second, outputs, student_rows = pl.pallas_call(
        forward_body,
        grid=(ratio,),
        in_specs=[full_spec, full_spec, out_spec, up_spec, down_spec, student_spec, vector_spec, fixed((1, SD))],
        out_specs=(full_spec, full_spec, column_spec, column_spec, full_spec, full_spec, fixed((token_count, SD))),
        out_shape=(
            array(token_count, hidden),
            array(token_count, hidden, dtype=BF16),
            array(token_count, inner_dim, dtype=BF16),
            array(token_count, inner_dim, dtype=BF16),
            array(token_count, hidden),
            array(token_count, hidden, dtype=BF16),
            array(token_count, SD),
        ),
        scratch_shapes=[pltpu.VMEM((token_count, hidden), F32), pltpu.VMEM((LANES, hidden), F32)],
        compiler_params=params(),
        cost_estimate=cost(1e6, 1e5),
        name="forward",
    )(tokens, context, gathered, gathered, gathered, gathered, entry, student_bias[None, :])

    step = 512 if slots % 512 == 0 else slots
    outgoing = pl.pallas_call(
        select_body,
        grid=(slots // step,),
        in_specs=[pl.BlockSpec((step, 1), lambda i: (i, 0)), full_spec],
        out_specs=pl.BlockSpec((step, hidden), lambda i: (i, 0)),
        out_shape=array(slots, hidden, dtype=BF16),
        compiler_params=params(),
        cost_estimate=cost(1e6, 1e5),
        name="select",
    )(slot_token, outputs)
    outgoing, student_rows = lax.optimization_barrier((outgoing, student_rows))
    carried = lax.all_to_all(outgoing, layout.dp, split_axis=0, concat_axis=0, tiled=True)
    pairs = logits_grad.shape[0]
    logits, student_grad, small = pl.pallas_call(
        student_body,
        out_shape=(
            array(*logits_grad.shape),
            array(token_count, SD, dtype=BF16),
            array(4 * pairs + 8, SD),
        ),
        compiler_params=params(),
        cost_estimate=cost(1e6, 1e5),
        name="student",
    )(
        student_rows, flat_segment, pool_query[None, :], dense_weight, dense_bias[None, :],
        class_weight, class_bias[None, :], logits_grad,
    )
    first_width = ratio * hidden + SD + LANES
    grad_second, grad_down, first = pl.pallas_call(
        functools.partial(down_grad_body, sums=whole_sums, ratio=ratio),
        grid=(ratio,),
        in_specs=[
            fixed((token_count, 1)), fixed((slots, hidden)), fixed((token_count, SD)), student_spec,
            vector_spec, full_spec, full_spec, column_spec,
        ],
        out_specs=(full_spec, full_spec, whole_sums.spec(first_width)),
        out_shape=(
            array(token_count, hidden),
            array(token_count, hidden, dtype=BF16),
            whole_sums.shape(first_width),
        ),
        scratch_shapes=[pltpu.VMEM((8, hidden), F32)],
        compiler_params=params(),
        cost_estimate=cost(1e6, 1e5),
        name="down_grad",
    )(token_slot, returned, student_grad, gathered, entry, pre_second, outputs, activated)
    first_sum = widen(lax.psum_scatter(first, axes, scatter_dimension=0, tiled=True))

    second_width = (ratio + 1) * hidden + LANES
    grad_first, grad_branch, second = pl.pallas_call(
        functools.partial(up_grad_body, sums=sums, ratio=ratio),
        grid=(ratio,),
        in_specs=[
            full_spec, full_spec, down_spec, up_spec, column_spec, full_spec, full_spec, full_spec, vector_spec,
        ],
        out_specs=(full_spec, full_spec, sums.spec(second_width)),
        out_shape=(
            array(token_count, hidden),
            array(token_count, hidden, dtype=BF16),
            sums.shape(second_width),
        ),
        scratch_shapes=[pltpu.VMEM((token_count, hidden), F32), pltpu.VMEM((8, hidden), F32)],
        compiler_params=params(),
        cost_estimate=cost(1e6, 1e5),
        name="up_grad",
    )(grad_down, grad_second, gathered, gathered, slope, normed, pre_first, context, entry)
    def attention_grad(r, *operands):
        rows_before = operands[7:]
        return pl.pallas_call(
            attention_grad_body if not rows_before else attention_grad_next_body,
            grid=(1, blocks),
            in_specs=[
                pl.BlockSpec((ROW, hidden), lambda _, p: (r, 0)),
                pl.BlockSpec((1, ROW, 1), lambda _, p: (r, 0, 0)),
                pl.BlockSpec((1, 1, ROW), lambda _, p: (r, 0, 0)),
            ]
            + [pl.BlockSpec((ROW, width), lambda _, p: (r, p))] * 3
            + [pl.BlockSpec((width, hidden), lambda _, p: (p, 0))]
            + [pl.BlockSpec(memory_space=pl.ANY)] * len(rows_before),
            out_specs=pl.BlockSpec((3, ROW, width), lambda _, p: (0, r, p)),
            out_shape=array(3, token_count, hidden, dtype=BF16),
            scratch_shapes=[pltpu.VMEM((ROW, ROW), F32)],
            input_output_aliases={7: 0} if rows_before else {},
            compiler_params=params(),
            cost_estimate=cost(1e6, 1e5),
            name="attention_grad",
        )(*operands)

    row_operands = (grad_branch, seg_column, seg_row, query, key, value, gathered)
    grads = attention_grad(0, *row_operands)
    second, carried = lax.optimization_barrier((second, carried))
    arrived = layout.exchange(sums.parts(second), 0)
    grads, arrived = lax.optimization_barrier((grads, arrived))
    second = layout.total(arrived)
    grads, second = lax.optimization_barrier((grads, second))
    second_arrived = layout.exchange(second, 1)
    for r in range(1, micro):
        grads = attention_grad(r, *row_operands, grads)

    third_width = 3 * hidden + LANES
    grads_spec = pl.BlockSpec((1, token_count, hidden), lambda j: (j, 0, 0))
    third = pl.pallas_call(
        functools.partial(qkv_grad_body, sums=sums),
        grid=(3,),
        in_specs=[full_spec, grads_spec],
        out_specs=sums.spec(third_width),
        out_shape=sums.shape(third_width),
        scratch_shapes=[pltpu.VMEM((8, hidden), F32)],
        compiler_params=params(),
        cost_estimate=cost(1e6, 1e5),
        name="qkv_grad",
    )(tokens, grads)
    third, second_arrived = lax.optimization_barrier((sums.parts(third), second_arrived))
    third = layout.total(layout.permutes(third, 0))
    second = layout.total(second_arrived)
    third_arrived = layout.permutes(third, 1)
    second_arrived = layout.permutes(second, 2)
    third, small = lax.optimization_barrier((third, small))
    small = lax.all_to_all(
        jnp.broadcast_to(small, (count,) + small.shape), axes, split_axis=0, concat_axis=0, tiled=True
    )
    tokens_grad = pl.pallas_call(
        token_grad_body,
        grid=(3,),
        in_specs=[grads_spec, pl.BlockSpec((hidden, hidden), lambda j: (0, j)), full_spec],
        out_specs=full_spec,
        out_shape=array(token_count, hidden, dtype=BF16),
        scratch_shapes=[pltpu.VMEM((token_count, hidden), F32)],
        compiler_params=params(),
        cost_estimate=cost(1e6, 1e5),
        name="token_grad",
    )(grads, entry, grad_first)
    third_arrived, second_arrived, tokens_grad, first_sum, small = lax.optimization_barrier(
        (third_arrived, second_arrived, tokens_grad, first_sum, small)
    )
    third = layout.total(third_arrived)
    third_arrived = layout.exchange(third, 2)
    second_sum = layout.total(second_arrived, F32)[0]
    dense_weight_grad, class_weight_grad, head_rows = pl.pallas_call(
        functools.partial(head_sums_body, pairs=pairs),
        out_shape=(array(SD, SD), array(SD, SD), array(8, SD)),
        compiler_params=params(),
        name="head_sums",
    )(small)
    third_sum = layout.total(third_arrived, F32)[0]

    down_grad = first_sum[:, : ratio * hidden].reshape(ratio * part, hidden)
    student_weight_grad = first_sum[:, ratio * hidden : ratio * hidden + SD]
    first_vectors = first_sum[:, ratio * hidden + SD :]
    up_grad = (
        second_sum[:, : ratio * hidden]
        .reshape(part, ratio, hidden)
        .transpose(0, 2, 1)
        .reshape(part, ratio * hidden)
    )
    out_grad = second_sum[:, ratio * hidden : (ratio + 1) * hidden]
    second_vectors = second_sum[:, (ratio + 1) * hidden :]
    qkv_grad = third_sum[:, : 3 * hidden]
    third_vectors = third_sum[:, 3 * hidden :]
    return (
        carried,
        logits,
        tokens_grad,
        qkv_grad,
        third_vectors[:, 0],
        third_vectors[:, 1],
        out_grad,
        second_vectors[:, 0],
        second_vectors[:, 1],
        second_vectors[:, 2],
        up_grad,
        second_vectors[:, 3 : 3 + ratio].reshape(-1),
        down_grad,
        first_vectors[:, 0],
        first_vectors[:, 1],
        first_vectors[:, 2],
        student_weight_grad,
        head_rows[1],
        head_rows[0],
        dense_weight_grad,
        head_rows[2],
        class_weight_grad[:, :classes],
        head_rows[3, :classes],
    )


def solution(mesh):
    layout = Layout(mesh)
    rows, flat, whole = P(layout.axes, None), P(layout.axes), P()

    def step(*args):
        return local(layout, *args)

    shard = (flat, flat, rows, flat, flat, flat, rows, flat, rows, flat, flat, flat, rows)
    return jax.shard_map(
        step,
        mesh=layout.mesh,
        in_specs=(rows,) * 7 + shard + (whole,) * 6,
        out_specs=(rows,) * 4 + shard + (whole,) * 6,
        check_vma=False,
    )
```

```python
import functools
import math

import jax
import jax.numpy as jnp
from jax import lax
from jax.experimental import pallas as pl
from jax.experimental.pallas import tpu as pltpu
from jax.sharding import Mesh
from jax.sharding import PartitionSpec as P

HD = 64
SD = 128
SH = 2
LAYER = 3
ROW = 512
MICRO = 2
LANES = 128

BF16 = jnp.bfloat16
F32 = jnp.float32
highest = lax.Precision.HIGHEST
norm_eps = 1e-12
masked_value = -1e30

QUERY_BIAS, VALUE_BIAS, OUT_BIAS, GAIN1, BIAS1, DOWN_BIAS, GAIN2, BIAS2, UP_BIAS = range(9)


def narrow(value):
    return value.astype(BF16)


def widen(value):
    return value.astype(F32)


def matmul(left, right, precision=None):
    return lax.dot_general(
        left, right, (((1,), (0,)), ((), ())), preferred_element_type=F32, precision=precision
    )


def left_inner(left, right, precision=None):
    return lax.dot_general(
        left, right, (((0,), (0,)), ((), ())), preferred_element_type=F32, precision=precision
    )


def right_inner(left, right, precision=None):
    return lax.dot_general(
        left, right, (((1,), (1,)), ((), ())), preferred_element_type=F32, precision=precision
    )


def params(*semantics, limit=58):
    return pltpu.CompilerParams(
        dimension_semantics=semantics or None, vmem_limit_bytes=limit * 1024 * 1024
    )


def cost(flops, nbytes, transcendentals=0):
    return pl.CostEstimate(
        flops=int(flops), bytes_accessed=int(nbytes), transcendentals=int(transcendentals)
    )


def fixed(shape, *at):
    where = at or (0,) * len(shape)
    return pl.BlockSpec(shape, lambda *_: where)


class Layout:
    def __init__(self, mesh):
        dp, fsdp = mesh.shape["dp"], mesh.shape["fsdp"]
        devices = mesh.devices
        if (dp, fsdp) == (8, 4):
            self.mesh = Mesh(devices.reshape(4, 2, 2, 2), ("z", "x", "y", "core"))
            self.dp = ("z", "x")
            self.stages = (("core",), ("x", "y"), ("z",))
        elif (dp, fsdp) == (64, 4):
            self.mesh = Mesh(devices.reshape(8, 4, 2, 4), ("z", "x", "core", "y"))
            self.dp = ("z", "x", "core")
            self.stages = (("core",), ("x", "y"), ("z",))
        else:
            self.mesh = mesh
            self.dp = ("dp",)
            self.stages = (("fsdp",), ("dp",))
        self.axes = tuple(self.mesh.axis_names)
        self.sizes = tuple(self.mesh.shape[name] for name in self.axes)
        self.count = math.prod(self.sizes)
        self.dp_count = dp
        self.extents = tuple(math.prod(self.mesh.shape[n] for n in stage) for stage in self.stages)
        order = [self.axes.index(name) for stage in self.stages for name in stage]
        self.place = []
        for device in range(self.count):
            at, rest = [], device
            for size in reversed(self.sizes):
                at.append(rest % size)
                rest //= size
            at = at[::-1]
            position = 0
            for axis in order:
                position = position * self.sizes[axis] + at[axis]
            self.place.append(position)
        self.device_at = [self.place.index(i) for i in range(self.count)]
        rest = self.count // self.sizes[0]
        self.late_place = [d % rest * self.sizes[0] + d // rest for d in range(self.count)]

    def exchange(self, value, stage):
        extent = self.extents[stage]
        value = value.reshape((extent, value.shape[0] // extent) + value.shape[1:])
        return lax.all_to_all(
            value, self.stages[stage], split_axis=0, concat_axis=0, tiled=True
        )

    def gather(self, value, beside):
        for stage in reversed(range(len(self.stages))):
            copies = jnp.broadcast_to(value, (self.extents[stage],) + value.shape)
            value = lax.all_to_all(
                copies, self.stages[stage], split_axis=0, concat_axis=0, tiled=True
            )
            if stage == len(self.stages) - 1:
                value, beside = lax.optimization_barrier((value, beside))
        order = [name for stage in self.stages for name in stage]
        tail = value.shape[-2:]
        value = value.reshape(tuple(self.mesh.shape[name] for name in order) + tail)
        back = tuple(order.index(name) for name in self.axes)
        value = value.transpose(back + (len(order), len(order) + 1))
        return value.reshape(self.count * tail[0], tail[1]), beside

    def late_sum(self, value):
        return lax.psum_scatter(value, self.axes[1:], scatter_dimension=0, tiled=True)

    def last_sum(self, value):
        return lax.psum_scatter(value, self.axes[:1], scatter_dimension=0, tiled=True)

    def permutes(self, value, stage):
        extent, axes = self.extents[stage], self.stages[stage]
        value = value.reshape((extent, value.shape[0] // extent) + value.shape[1:])
        me = lax.axis_index(axes)
        parts = [lax.dynamic_index_in_dim(value, me, 0, keepdims=False)]
        for step in range(1, extent):
            part = lax.dynamic_index_in_dim(value, lax.rem(me + step, extent), 0, keepdims=False)
            pairs = [(i, (i + step) % extent) for i in range(extent)]
            parts.append(lax.ppermute(part, axes, pairs))
        return parts

    def total(self, arrived, dtype=BF16):
        if isinstance(arrived, list):
            return sum(widen(part) for part in arrived).astype(dtype)
        return jnp.sum(widen(arrived), axis=0).astype(dtype)


def store_parts(ref, place, value, column):
    width = value.shape[1]
    if len(ref.shape) == 2:
        ref[:, pl.ds(column, width)] = value.astype(ref.dtype)
        return
    count, part, _ = ref.shape
    for device in range(count):
        ref[place[device], :, pl.ds(column, width)] = value[
            device * part : (device + 1) * part
        ].astype(ref.dtype)


def add_body(left, right, result):
    result[...] = (widen(left[...]) + widen(right[...])).astype(result.dtype)


def add(left, right):
    parts, part, columns = left.shape
    step = 4 if parts % 4 == 0 else 1
    spec = pl.BlockSpec((step, part, columns), lambda i: (i, 0, 0))
    return pl.pallas_call(
        add_body,
        grid=(parts // step,),
        in_specs=[spec, spec],
        out_specs=spec,
        out_shape=jax.ShapeDtypeStruct(left.shape, left.dtype),
        compiler_params=params(),
        cost_estimate=cost(1e6, 1e5),
        name="add",
    )(left, right)


class Return:
    def __init__(self, layout, slots):
        self.layout, self.slots = layout, slots
        extents = [layout.mesh.shape[name] for name in layout.dp]
        self.staged = len(extents) == 2 and extents[1] == 2
        self.extent = extents[0]
        self.here = [lax.axis_index(name) for name in layout.dp]

    def first_stage(self, value):
        if not self.staged:
            return [value]
        value = value.reshape((self.extent, 2, self.slots // (2 * self.extent)) + value.shape[1:])
        near = lax.dynamic_index_in_dim(value, self.here[1], 1, keepdims=False)
        far = lax.dynamic_index_in_dim(value, 1 - self.here[1], 1, keepdims=False)
        return [near, lax.ppermute(far, self.layout.dp[1], [(0, 1), (1, 0)])]

    def second_stage(self, arrived):
        if not self.staged:
            return [lax.all_to_all(arrived[0], self.layout.dp, split_axis=0, concat_axis=0, tiled=True)]
        both = jnp.stack(arrived, axis=1)
        both = both.reshape((self.extent, -1) + both.shape[3:])
        pieces = []
        for step in range(self.extent):
            piece = lax.dynamic_index_in_dim(
                both, lax.rem(self.here[0] + step, self.extent), 0, keepdims=False
            )
            if step > 0:
                pairs = [(i, (i + step) % self.extent) for i in range(self.extent)]
                piece = lax.ppermute(piece, self.layout.dp[0], pairs)
            pieces.append(piece)
        return pieces

    def position(self, target):
        if not self.staged:
            return target
        step = lax.rem(self.here[0] + self.extent - target // 2, self.extent)
        return 2 * step + jnp.bitwise_xor(target % 2, self.here[1])


class Sums:
    def __init__(self, layout, rows, split=True):
        self.layout = layout
        self.count, self.part = layout.count, rows // layout.count
        self.split = split and self.part % 8 == 0 and layout.extents[0] == 2

    def shapes(self, columns):
        if self.split:
            return (jax.ShapeDtypeStruct((self.count // 2, self.part, columns), BF16),) * 2
        return (jax.ShapeDtypeStruct((self.count * self.part, columns), BF16),)

    def specs(self, columns):
        return tuple(fixed(shape.shape) for shape in self.shapes(columns))

    def store(self, refs, core, value, column):
        width = value.shape[1]
        if not self.split:
            refs[0][:, pl.ds(column, width)] = value.astype(BF16)
            return
        half = self.count // 2

        def put(mine):
            for device in range(self.count):
                position = self.layout.place[device]
                ref = refs[0] if position // half == mine else refs[1]
                ref[position % half, :, pl.ds(column, width)] = value[
                    device * self.part : (device + 1) * self.part
                ].astype(BF16)

        for mine in range(2):
            pl.when(core[0] == mine)(functools.partial(put, mine))

    def first_stage(self, values):
        if self.split:
            other = lax.ppermute(values[1], self.layout.stages[0], [(0, 1), (1, 0)])
            return add(values[0], other)
        value = values[0].reshape(self.count, self.part, values[0].shape[1])
        value = value[jnp.asarray(self.layout.device_at)]
        return self.layout.total(self.layout.permutes(value, 0))


def interleave(width, ratio, dtype):
    size = width * ratio
    source = lax.broadcasted_iota(jnp.int32, (size, size), 0)
    target = lax.broadcasted_iota(jnp.int32, (size, size), 1)
    return (source == (target % width) * ratio + target // width).astype(dtype)


def pack_body(out, up, down, student, packed, *, ratio, hidden):
    part = out.shape[0]
    packed[:, :hidden] = out[...]
    base = hidden
    mix = interleave(LANES, ratio, BF16)
    for chunk in range(hidden // LANES):
        piece = narrow(
            matmul(up[:, chunk * ratio * LANES : (chunk + 1) * ratio * LANES], mix)
        )
        for j in range(ratio):
            at = base + j * hidden + chunk * LANES
            packed[:, at : at + LANES] = piece[:, j * LANES : (j + 1) * LANES]
    base += ratio * hidden
    row = lax.broadcasted_iota(jnp.int32, (part, part * ratio), 0)
    column = lax.broadcasted_iota(jnp.int32, (part, part * ratio), 1)
    for j in range(ratio):
        pick = (column == row * ratio + j).astype(BF16)
        packed[:, base + j * hidden : base + (j + 1) * hidden] = narrow(matmul(pick, down[...]))
    base += ratio * hidden
    packed[:, base : base + SD] = student[...]


def turned(vectors):
    return widen(vectors).T


def attention_body(
    tokens, seg_column, seg_row, wq, wk, wv, vectors, query, key, value, context, log_totals, mask, rows
):
    step = pl.program_id(1)
    width = wq.shape[1]

    @pl.when((step == 0) & (pl.program_id(0) == 0))
    def _():
        rows[...] = turned(vectors[...])

    @pl.when(step == 0)
    def _():
        mask[...] = jnp.where(seg_column[0] == seg_row[0], 0.0, masked_value)

    here = pl.ds(pl.multiple_of(step * width, width), width)
    x = tokens[...]
    q = narrow(matmul(x, wq[...]) + rows[QUERY_BIAS : QUERY_BIAS + 1, here])
    k = narrow(matmul(x, wk[...]))
    v = narrow(matmul(x, wv[...]) + rows[VALUE_BIAS : VALUE_BIAS + 1, here])
    query[...] = q
    key[...] = k
    value[...] = v
    lane = lax.broadcasted_iota(jnp.int32, (x.shape[0], LANES), 1)
    scale = BF16(1.0 / math.sqrt(HD))
    for block in range(width // LANES):
        cut = slice(block * LANES, (block + 1) * LANES)
        q_block, k_block, v_turned = q[:, cut] * scale, k[:, cut], v[:, cut].T
        parts = []
        for head in range(LANES // HD):
            mine = (lane >= head * HD) & (lane < (head + 1) * HD)
            scores = right_inner(k_block, jnp.where(mine, q_block, BF16(0))) + mask[...]
            top = jnp.max(scores, axis=0, keepdims=True)
            exponent = jnp.exp(scores - top)
            total = jnp.sum(exponent, axis=0, keepdims=True)
            probs = narrow(exponent * (1.0 / total))
            at = block * (LANES // HD) + head
            log_totals[0, at : at + 1] = top + jnp.log(total)
            parts.append(matmul(v_turned[head * HD : (head + 1) * HD], probs))
        context[:, cut] = narrow(jnp.concatenate(parts, axis=0)).T


def attention_grad_body(
    branch, seg_column, seg_row, query, key, value, log_totals, out_weight, grads, mask
):
    width = query.shape[1]

    @pl.when(pl.program_id(1) == 0)
    def _():
        mask[...] = jnp.where(seg_column[0] == seg_row[0], 0.0, masked_value)

    grad_context = narrow(right_inner(branch[...], out_weight[...]))
    lane = lax.broadcasted_iota(jnp.int32, (branch.shape[0], LANES), 1)
    scale = 1.0 / math.sqrt(HD)
    for block in range(width // LANES):
        cut = slice(block * LANES, (block + 1) * LANES)
        q_block, k_block, v_block = query[:, cut] * BF16(scale), key[:, cut], value[:, cut]
        g_block, k_turned = grad_context[:, cut], k_block.T
        grad_q, grad_k, grad_v = [], 0.0, 0.0
        for head in range(LANES // HD):
            mine = (lane >= head * HD) & (lane < (head + 1) * HD)
            q_head = jnp.where(mine, q_block, BF16(0))
            g_head = jnp.where(mine, g_block, BF16(0))
            scores = right_inner(k_block, q_head) + mask[...]
            at = block * (LANES // HD) + head
            probs = jnp.exp(scores - log_totals[0, at : at + 1])
            grad_probs = right_inner(v_block, g_head)
            inner = jnp.sum(probs * grad_probs, axis=0, keepdims=True)
            grad_scores = narrow(probs * (grad_probs - inner))
            grad_v += matmul(narrow(probs), g_head)
            grad_k += matmul(grad_scores, q_head)
            grad_q.append(matmul(k_turned[head * HD : (head + 1) * HD], grad_scores))
        grads[0, :, cut] = narrow(jnp.concatenate(grad_q, axis=0) * scale).T
        grads[1, :, cut] = narrow(grad_k)
        grads[2, :, cut] = narrow(grad_v)


def normalize(values):
    average = jnp.mean(values, axis=-1, keepdims=True)
    centered = values - average
    spread = jnp.mean(centered * centered, axis=-1, keepdims=True)
    scale = lax.rsqrt(spread + norm_eps)
    return centered * scale, scale


def gelu_and_slope(x):
    phi = 0.5 + 0.5 * lax.erf(x * math.sqrt(0.5))
    return x * phi, phi + x * (jnp.exp(-0.5 * (x * x)) * (1.0 / math.sqrt(2.0 * math.pi)))


CHUNK = 256


def forward_body(
    tokens, context, out_weight, up, down, student, vectors, student_bias,
    pre_first, normed, activated, slope, pre_second, outputs, student_rows, total, rows,
):
    step = pl.program_id(0)
    count = tokens.shape[0]

    @pl.when(step == 0)
    def _():
        rows[...] = turned(vectors[...])
        for low in range(0, count, CHUNK):
            cut = slice(low, low + CHUNK)
            pre = (
                widen(tokens[cut])
                + matmul(context[cut], out_weight[...])
                + rows[OUT_BIAS : OUT_BIAS + 1]
            )
            pre_first[cut] = pre
            hat, _ = normalize(pre)
            value = narrow(hat * rows[GAIN1 : GAIN1 + 1] + rows[BIAS1 : BIAS1 + 1])
            normed[cut] = value
            total[cut] = widen(value) + rows[DOWN_BIAS : DOWN_BIAS + 1]

    bias = rows[pl.ds(UP_BIAS + step, 1)]
    for low in range(0, count, CHUNK):
        cut = slice(low, low + CHUNK)
        value, grad = gelu_and_slope(matmul(normed[cut], up[...]) + bias)
        value = narrow(value)
        activated[cut] = value
        slope[cut] = narrow(grad)
        total[cut] += matmul(value, down[...])

    @pl.when(step == pl.num_programs(0) - 1)
    def _():
        for low in range(0, count, CHUNK):
            cut = slice(low, low + CHUNK)
            pre = total[cut]
            pre_second[cut] = pre
            hat, _ = normalize(pre)
            value = narrow(hat * rows[GAIN2 : GAIN2 + 1] + rows[BIAS2 : BIAS2 + 1])
            outputs[cut] = value
            student_rows[cut] = matmul(value, student[...]) + student_bias[...]


def select_body(index, source, target):
    place = lax.broadcasted_iota(jnp.int32, (index.shape[0], source.shape[0]), 1)
    target[...] = narrow(matmul((index[...] == place).astype(BF16), source[...]))


def student_body(
    student_rows, segment, query, dense_weight, dense_bias, class_weight, class_bias, logits_grad,
    logits, student_grad, small,
):
    count, _ = student_rows.shape
    pairs, classes = logits_grad.shape
    wide = -(-pairs // LANES) * LANES
    head = SD // SH
    scale = 1.0 / math.sqrt(head)
    rows = student_rows[...]
    member = segment[...] == lax.broadcasted_iota(jnp.int32, (count, wide), 1)
    one_hot = member.astype(F32)
    lane = lax.broadcasted_iota(jnp.int32, (count, SD), 1)

    def by_head(values):
        return [
            jnp.sum(
                jnp.where((lane >= a * head) & (lane < (a + 1) * head), values, 0.0),
                axis=1,
                keepdims=True,
            )
            for a in range(SH)
        ]

    def spread(columns):
        value = columns[0]
        for a in range(1, SH):
            value = jnp.where(lane >= a * head, columns[a], value)
        return jnp.broadcast_to(value, (count, SD))

    def of_pair(row):
        return jnp.sum(jnp.where(member, row, 0.0), axis=1, keepdims=True)

    def over_pair(column):
        return jnp.sum(jnp.where(member, column, 0.0), axis=0, keepdims=True)

    weights = []
    for score in by_head(rows * query[...]):
        score = score * scale
        top = jnp.max(jnp.where(member, score, masked_value), axis=0, keepdims=True)
        exponent = jnp.exp(score - of_pair(top))
        weights.append(exponent / of_pair(over_pair(exponent)))
    weight = spread(weights)
    pooled = left_inner(one_hot, weight * rows, highest)
    dense = jnp.tanh(matmul(pooled, dense_weight[...], highest) + dense_bias[...])
    logits[...] = matmul(dense[:pairs], class_weight[...], highest) + class_bias[...]

    grad = logits_grad[...]
    grad_pre = right_inner(grad, class_weight[...], highest) * (
        1.0 - dense[:pairs] * dense[:pairs]
    )
    small[...] = jnp.zeros_like(small)
    small[:pairs] = pooled[:pairs]
    small[pairs : 2 * pairs] = grad_pre
    small[2 * pairs : 3 * pairs] = dense[:pairs]
    small[3 * pairs : 4 * pairs, :classes] = grad
    at = 4 * pairs
    grad_pooled = right_inner(grad_pre, dense_weight[...], highest)
    grad_token = matmul(one_hot[:, :pairs], grad_pooled, highest)
    grad_score = []
    for a, inner in enumerate(by_head(rows * grad_token)):
        product = weights[a] * inner
        grad_score.append(weights[a] * (inner - of_pair(over_pair(product))))
    grad_score = spread(grad_score) * scale
    small[at : at + 1] = jnp.sum(grad_score * rows, axis=0, keepdims=True)
    result = narrow(weight * grad_token + grad_score * query[...])
    student_grad[...] = result
    small[at + 1 : at + 2] = jnp.sum(widen(result), axis=0, keepdims=True)


def head_sums_body(gathered, dense_weight_grad, class_weight_grad, rows, *, pairs):
    everyone = gathered[...]
    width = everyone.shape[2]

    def factor(i):
        return everyone[:, i * pairs : (i + 1) * pairs].reshape(-1, width)

    pooled, grad_pre, dense, grad = (factor(i) for i in range(4))
    dense_weight_grad[...] = left_inner(pooled, grad_pre, highest)
    class_weight_grad[...] = left_inner(dense, grad, highest)
    total = jnp.sum(everyone[:, 4 * pairs : 4 * pairs + 8], axis=0)
    row = lax.broadcasted_iota(jnp.int32, (8, width), 0)
    total = jnp.where(row == 2, jnp.sum(grad_pre, axis=0, keepdims=True), total)
    rows[...] = jnp.where(row == 3, jnp.sum(grad, axis=0, keepdims=True), total)


def norm_grad(grad, pre, gain):
    hat, scale = normalize(pre)
    scaled = grad * gain
    result = scale * (
        scaled
        - jnp.mean(scaled, axis=-1, keepdims=True)
        - hat * jnp.mean(scaled * hat, axis=-1, keepdims=True)
    )
    return (
        result,
        jnp.sum(grad * hat, axis=0, keepdims=True),
        jnp.sum(grad, axis=0, keepdims=True),
    )


def as_columns(rows, count, hidden):
    row = lax.broadcasted_iota(jnp.int32, (LANES, hidden), 0)
    block = jnp.zeros((LANES, hidden), F32)
    for i in range(count):
        block = jnp.where(row == i, rows[i], block)
    return block.T


def down_grad_body(
    slot, student_grad, student, vectors, pre_second, outputs, activated, *refs, ratio, place,
):
    *returned, grad_second, grad_down, shards, sums_ref = refs
    step = pl.program_id(0)
    count, hidden = pre_second.shape

    @pl.when(step == 0)
    def _():
        gain = turned(vectors[...])[GAIN2 : GAIN2 + 1]
        length = returned[0].shape[0]
        slot_place = lax.broadcasted_iota(jnp.int32, (CHUNK, length), 1)
        parts = []
        for low in range(0, count, CHUNK):
            cut = slice(low, low + CHUNK)
            grad = right_inner(student_grad[cut], student[...])
            for i, piece in enumerate(returned):
                pick = (slot[cut] - i * length == slot_place).astype(BF16)
                grad += matmul(pick, piece[...])
            result, gain_part, bias_part = norm_grad(grad, pre_second[cut], gain)
            grad_second[cut] = result
            low_result = narrow(result)
            grad_down[cut] = low_result
            parts.append((jnp.sum(widen(low_result), axis=0, keepdims=True), gain_part, bias_part))
        for i in range(3):
            sums_ref[i : i + 1] = sum(part[i] for part in parts)

    store_parts(
        shards,
        place,
        left_inner(activated[...], grad_down[...]),
        pl.multiple_of(step * hidden, LANES),
    )

    @pl.when(step == pl.num_programs(0) - 1)
    def _():
        at = ratio * hidden
        store_parts(shards, place, left_inner(outputs[...], student_grad[...]), at)
        vector_rows = [sums_ref[i : i + 1] for i in range(3)]
        store_parts(shards, place, as_columns(vector_rows, 3, hidden), at + SD)


def up_grad_body(
    core, grad_down, grad_second, down, up, slope, normed, pre_first, context, vectors,
    grad_first, grad_branch, *refs, sums, ratio,
):
    step = pl.program_id(0)
    *shards, total, bias_rows = refs
    count, hidden = pre_first.shape

    @pl.when(step == 0)
    def _():
        total[...] = grad_second[...]

    bias_part = 0.0
    pieces = []
    for low in range(0, count, CHUNK):
        cut = slice(low, low + CHUNK)
        grad = right_inner(grad_down[cut], down[...])
        grad = narrow(grad * widen(slope[cut]))
        pieces.append(grad)
        bias_part = bias_part + jnp.sum(widen(grad), axis=0, keepdims=True)
        total[cut] += right_inner(grad, up[...])

    bias_rows[pl.ds(step, 1)] = bias_part
    sums.store(
        shards,
        core,
        left_inner(normed[...], jnp.concatenate(pieces, axis=0)),
        pl.multiple_of(step * hidden, LANES),
    )

    @pl.when(step == pl.num_programs(0) - 1)
    def _():
        gain = turned(vectors[...])[GAIN1 : GAIN1 + 1]
        parts = []
        for low in range(0, count, CHUNK):
            cut = slice(low, low + CHUNK)
            result, gain_part, shift_part = norm_grad(total[cut], pre_first[cut], gain)
            grad_first[cut] = result
            low_result = narrow(result)
            grad_branch[cut] = low_result
            parts.append((jnp.sum(widen(low_result), axis=0, keepdims=True), gain_part, shift_part))
        vector_rows = [sum(part[i] for part in parts) for i in range(3)]
        vector_rows += [bias_rows[i : i + 1] for i in range(ratio)]
        sums.store(shards, core, left_inner(context[...], grad_branch[...]), ratio * hidden)
        sums.store(
            shards, core, as_columns(vector_rows, 3 + ratio, hidden), (ratio + 1) * hidden
        )


def qkv_grad_body(core, tokens, grads, *refs, sums):
    step = pl.program_id(0)
    *shards, bias_rows = refs
    hidden = tokens.shape[1]
    grad = grads[0]
    bias_rows[pl.ds(step, 1)] = jnp.sum(widen(grad), axis=0, keepdims=True)
    sums.store(
        shards, core, left_inner(tokens[...], grad), pl.multiple_of(step * hidden, LANES)
    )

    @pl.when(step == pl.num_programs(0) - 1)
    def _():
        vector_rows = [bias_rows[0:1], bias_rows[2:3]]
        sums.store(shards, core, as_columns(vector_rows, 2, hidden), 3 * hidden)


def token_grad_body(grads, weight, grad_first, result, total):
    step = pl.program_id(0)
    update = right_inner(grads[0], weight[...])

    @pl.when(step == 0)
    def _():
        total[...] = grad_first[...] + update

    @pl.when(step > 0)
    def _():
        total[...] += update

    @pl.when(step == pl.num_programs(0) - 1)
    def _():
        result[...] = narrow(total[...])


def stacked(parts):
    return jnp.concatenate([part.reshape(-1, part.shape[-1]) for part in parts], axis=0)


def first_end_body(*refs, hidden, ratio):
    *parts, down_grad, student_grad, vectors = refs
    rows = parts[0].shape[-2]
    every = stacked([widen(part[...]) for part in parts])
    target = lax.broadcasted_iota(jnp.int32, (rows * ratio, every.shape[0]), 0)
    source = lax.broadcasted_iota(jnp.int32, (rows * ratio, every.shape[0]), 1) % rows
    every_low = narrow(every)
    result = 0.0
    for j in range(ratio):
        pick = (target == source * ratio + j).astype(BF16)
        result += matmul(pick, every_low[:, j * hidden : (j + 1) * hidden])
    down_grad[...] = result
    total = sum(every[i : i + rows, ratio * hidden :] for i in range(0, every.shape[0], rows))
    student_grad[...] = total[:, :SD]
    vectors[...] = total[:, SD:]


def second_end_body(*refs, hidden, ratio):
    *parts, up_grad, out_grad, vectors = refs
    rows = parts[0].shape[-2]
    every = stacked([widen(part[...]) for part in parts])
    every_low = narrow(every)
    mix = interleave(LANES, ratio, BF16)
    for chunk in range(hidden // LANES):
        piece = jnp.concatenate(
            [
                every_low[:, j * hidden + chunk * LANES : j * hidden + (chunk + 1) * LANES]
                for j in range(ratio)
            ],
            axis=1,
        )
        piece = right_inner(piece, mix)
        at = chunk * ratio * LANES
        up_grad[:, at : at + ratio * LANES] = sum(
            piece[i : i + rows] for i in range(0, piece.shape[0], rows)
        )
    total = sum(every[i : i + rows, ratio * hidden :] for i in range(0, every.shape[0], rows))
    out_grad[...] = total[:, :hidden]
    vectors[...] = total[:, hidden:]


def third_end_body(*refs, hidden):
    *parts, qkv_grad, vectors = refs
    total = sum(widen(part[...]).reshape(part.shape[-2:]) for part in parts)
    qkv_grad[...] = total[:, : 3 * hidden]
    vectors[...] = total[:, 3 * hidden :]


def local(
    layout,
    tokens,
    lengths,
    exit_layers,
    destination,
    carried_grad,
    logits_grad,
    qkv_weight,
    query_bias,
    value_bias,
    out_weight,
    out_bias,
    norm1_gain,
    norm1_bias,
    up_weight,
    up_bias,
    down_weight,
    down_bias,
    norm2_gain,
    norm2_bias,
    student_weight,
    student_bias,
    pool_query,
    dense_weight,
    dense_bias,
    class_weight,
    class_bias,
):
    axes, count, dp_count = layout.axes, layout.count, layout.dp_count
    pair_count = lengths.shape[1]
    slots = carried_grad.shape[0]
    slot_width = slots // dp_count
    token_count, hidden = tokens.shape
    inner_dim = up_weight.shape[1]
    part = hidden // count
    ratio = inner_dim // hidden
    classes = class_weight.shape[1]
    sums = Sums(layout, hidden)
    core = lax.axis_index(layout.stages[0]).astype(jnp.int32).reshape(1)
    core_spec = pl.BlockSpec(memory_space=pltpu.SMEM)
    width = 2 * LANES
    blocks = hidden // width
    micro = token_count // ROW

    def array(*shape, dtype=F32):
        return jax.ShapeDtypeStruct(shape, dtype)

    vector_list = (
        query_bias, value_bias, out_bias, norm1_gain, norm1_bias, down_bias, norm2_gain, norm2_bias,
    )
    columns = jnp.concatenate(
        [v[:, None] for v in vector_list]
        + [up_bias.reshape(part, ratio), jnp.zeros((part, LANES - len(vector_list) - ratio), BF16)],
        axis=1,
    )
    packed_width = (1 + 2 * ratio) * hidden + SD
    packed = pl.pallas_call(
        functools.partial(pack_body, ratio=ratio, hidden=hidden),
        out_shape=array(part, packed_width, dtype=BF16),
        compiler_params=params(),
        name="pack",
    )(out_weight, up_weight, down_weight, student_weight)
    gathered = lax.all_gather(packed, axes, axis=0, tiled=True)
    returning = Return(layout, slots)
    entry, returned = layout.gather(
        jnp.concatenate([qkv_weight, columns], axis=1), returning.first_stage(carried_grad)
    )
    student_at = (1 + 2 * ratio) * hidden // LANES
    out_spec = fixed((hidden, hidden), 0, 0)
    up_spec = pl.BlockSpec((hidden, hidden), lambda j: (0, 1 + j))
    down_spec = pl.BlockSpec((hidden, hidden), lambda j: (0, 1 + ratio + j))
    student_spec = fixed((hidden, SD), 0, student_at)
    vector_spec = fixed((hidden, LANES), 0, 3 * hidden // LANES)
    full_spec = fixed((token_count, hidden))
    column_spec = pl.BlockSpec((token_count, hidden), lambda j: (0, j))

    place = jnp.arange(ROW, dtype=jnp.int32)
    pair_ids = jnp.arange(pair_count, dtype=jnp.int32)
    ends = jnp.cumsum(lengths, axis=1)
    starts = ends - lengths
    alive = (exit_layers > LAYER).astype(jnp.int32)
    targets = returning.position(destination.reshape(micro, pair_count))
    segment = jnp.sum((place[None, :, None] >= ends[:, None, :]).astype(jnp.int32), axis=2)
    member = (segment[:, :, None] == pair_ids[None, None, :]).astype(jnp.int32)
    token_slot = jnp.sum(
        member * jnp.where(alive > 0, targets * slot_width - starts, -slots - ROW)[:, None, :], axis=2
    ) + place[None, :]
    token_slot = jnp.where(token_slot < 0, -1, token_slot).reshape(token_count, 1)
    flat_segment = (segment + pair_count * jnp.arange(micro, dtype=jnp.int32)[:, None]).reshape(
        token_count, 1
    )
    seg_column, seg_row = segment[:, :, None], segment[:, None, :]
    flat_starts = (starts + ROW * jnp.arange(micro, dtype=jnp.int32)[:, None]).reshape(-1)
    dp_ids = jnp.arange(dp_count, dtype=jnp.int32)
    chosen = (destination.reshape(-1)[None, :] == dp_ids[:, None]).astype(jnp.int32)
    send_start = jnp.sum(chosen * flat_starts[None, :], axis=1)
    send_length = jnp.sum(chosen * (lengths * alive).reshape(-1)[None, :], axis=1)
    slot_place = jnp.arange(slot_width, dtype=jnp.int32)
    slot_token = jnp.where(
        slot_place[None, :] < send_length[:, None], send_start[:, None] + slot_place[None, :], -1
    ).reshape(slots, 1)


    row_specs = [
        pl.BlockSpec((1, ROW, 1), lambda r, p: (r, 0, 0)),
        pl.BlockSpec((1, 1, ROW), lambda r, p: (r, 0, 0)),
    ]
    block_spec = pl.BlockSpec((ROW, width), lambda r, p: (r, p))
    pair_flops = 2 * token_count * ROW * hidden
    heads = max(8, width // HD)
    log_spec = pl.BlockSpec((1, heads, ROW), lambda r, p: (r * blocks + p, 0, 0))
    query, key, value, context, log_totals = pl.pallas_call(
        attention_body,
        grid=(micro, blocks),
        in_specs=[pl.BlockSpec((ROW, hidden), lambda r, p: (r, 0))]
        + row_specs
        + [
            pl.BlockSpec((hidden, width), lambda r, p: (0, p)),
            pl.BlockSpec((hidden, width), lambda r, p: (0, blocks + p)),
            pl.BlockSpec((hidden, width), lambda r, p: (0, 2 * blocks + p)),
            vector_spec,
        ],
        out_specs=(block_spec,) * 4 + (log_spec,),
        out_shape=(array(token_count, hidden, dtype=BF16),) * 4 + (array(micro * blocks, heads, ROW),),
        scratch_shapes=[pltpu.VMEM((ROW, ROW), F32), pltpu.VMEM((LANES, hidden), F32)],
        compiler_params=params(),
        cost_estimate=cost(1e6, 1e5),
        name="attention",
    )(tokens, seg_column, seg_row, entry, entry, entry, entry)

    context, returned = lax.optimization_barrier((context, returned))
    returned = returning.second_stage(returned)

    pre_first, normed, activated, slope, pre_second, outputs, student_rows = pl.pallas_call(
        forward_body,
        grid=(ratio,),
        in_specs=[full_spec, full_spec, out_spec, up_spec, down_spec, student_spec, vector_spec, fixed((1, SD))],
        out_specs=(full_spec, full_spec, column_spec, column_spec, full_spec, full_spec, fixed((token_count, SD))),
        out_shape=(
            array(token_count, hidden),
            array(token_count, hidden, dtype=BF16),
            array(token_count, inner_dim, dtype=BF16),
            array(token_count, inner_dim, dtype=BF16),
            array(token_count, hidden),
            array(token_count, hidden, dtype=BF16),
            array(token_count, SD),
        ),
        scratch_shapes=[pltpu.VMEM((token_count, hidden), F32), pltpu.VMEM((LANES, hidden), F32)],
        compiler_params=params(),
        cost_estimate=cost(1e6, 1e5),
        name="forward",
    )(tokens, context, gathered, gathered, gathered, gathered, entry, student_bias[None, :])

    step = 512 if slots % 512 == 0 else slots
    outgoing = pl.pallas_call(
        select_body,
        grid=(slots // step,),
        in_specs=[pl.BlockSpec((step, 1), lambda i: (i, 0)), full_spec],
        out_specs=pl.BlockSpec((step, hidden), lambda i: (i, 0)),
        out_shape=array(slots, hidden, dtype=BF16),
        compiler_params=params(),
        cost_estimate=cost(1e6, 1e5),
        name="select",
    )(slot_token, outputs)

    pairs = logits_grad.shape[0]
    logits, student_grad, small = pl.pallas_call(
        student_body,
        out_shape=(
            array(*logits_grad.shape),
            array(token_count, SD, dtype=BF16),
            array(4 * pairs + 8, SD),
        ),
        compiler_params=params(),
        cost_estimate=cost(1e6, 1e5),
        name="student",
    )(
        student_rows, flat_segment, pool_query[None, :], dense_weight, dense_bias[None, :],
        class_weight, class_bias[None, :], logits_grad,
    )
    outgoing, student_grad, *returned = lax.optimization_barrier((outgoing, student_grad, *returned))
    carried = lax.all_to_all(outgoing, layout.dp, split_axis=0, concat_axis=0, tiled=True)

    first_width = ratio * hidden + SD + LANES
    first_shape = (count, part, first_width) if part % 8 == 0 else (hidden, first_width)
    grad_second, grad_down, first = pl.pallas_call(
        functools.partial(down_grad_body, ratio=ratio, place=layout.late_place),
        grid=(ratio,),
        in_specs=[
            fixed((token_count, 1)), fixed((token_count, SD)), student_spec,
            vector_spec, full_spec, full_spec, column_spec,
        ]
        + [fixed(piece.shape) for piece in returned],
        out_specs=(full_spec, full_spec, fixed(first_shape)),
        out_shape=(
            array(token_count, hidden),
            array(token_count, hidden, dtype=BF16),
            array(*first_shape, dtype=BF16),
        ),
        scratch_shapes=[pltpu.VMEM((8, hidden), F32)],
        compiler_params=params(),
        cost_estimate=cost(1e6, 1e5),
        name="down_grad",
    )(token_slot, student_grad, gathered, entry, pre_second, outputs, activated, *returned)
    if part % 8 != 0:
        order = [layout.late_place.index(i) for i in range(count)]
        first = first.reshape(count, part, first_width)[jnp.asarray(order)]
    first_part = layout.late_sum(first)

    second_width = (ratio + 1) * hidden + LANES
    grad_first, grad_branch, *second = pl.pallas_call(
        functools.partial(up_grad_body, sums=sums, ratio=ratio),
        grid=(ratio,),
        in_specs=[
            core_spec, full_spec, full_spec, down_spec, up_spec, column_spec, full_spec, full_spec, full_spec,
            vector_spec,
        ],
        out_specs=(full_spec, full_spec) + sums.specs(second_width),
        out_shape=(
            array(token_count, hidden),
            array(token_count, hidden, dtype=BF16),
        )
        + sums.shapes(second_width),
        scratch_shapes=[pltpu.VMEM((token_count, hidden), F32), pltpu.VMEM((8, hidden), F32)],
        compiler_params=params(),
        cost_estimate=cost(1e6, 1e5),
        name="up_grad",
    )(core, grad_down, grad_second, gathered, gathered, slope, normed, pre_first, context, entry)
    second, grad_branch, carried = lax.optimization_barrier(
        (sums.first_stage(second), grad_branch, carried)
    )
    second_arrived = layout.exchange(second, 1)
    grads = pl.pallas_call(
        attention_grad_body,
        grid=(micro, blocks),
        in_specs=[pl.BlockSpec((ROW, hidden), lambda r, p: (r, 0))]
        + row_specs
        + [block_spec] * 3
        + [log_spec, pl.BlockSpec((width, hidden), lambda r, p: (p, 0))],
        out_specs=pl.BlockSpec((3, ROW, width), lambda r, p: (0, r, p)),
        out_shape=array(3, token_count, hidden, dtype=BF16),
        scratch_shapes=[pltpu.VMEM((ROW, ROW), F32)],
        compiler_params=params(),
        cost_estimate=cost(1e6, 1e5),
        name="attention_grad",
    )(grad_branch, seg_column, seg_row, query, key, value, log_totals, gathered)

    third_width = 3 * hidden + LANES
    grads_spec = pl.BlockSpec((1, token_count, hidden), lambda j: (j, 0, 0))
    third = pl.pallas_call(
        functools.partial(qkv_grad_body, sums=sums),
        grid=(3,),
        in_specs=[core_spec, full_spec, grads_spec],
        out_specs=sums.specs(third_width),
        out_shape=sums.shapes(third_width),
        scratch_shapes=[pltpu.VMEM((8, hidden), F32)],
        compiler_params=params(),
        cost_estimate=cost(1e6, 1e5),
        name="qkv_grad",
    )(core, tokens, grads)
    third, second_arrived, small = lax.optimization_barrier((third, second_arrived, small))
    small = lax.all_to_all(
        jnp.broadcast_to(small, (count,) + small.shape), axes, split_axis=0, concat_axis=0, tiled=True
    )
    third = sums.first_stage(third)
    third, second_arrived, first_part = lax.optimization_barrier((third, second_arrived, first_part))
    third_arrived = layout.permutes(third, 1)
    third_arrived[0], second_arrived, small, first_part = lax.optimization_barrier(
        (third_arrived[0], second_arrived, small, first_part)
    )
    first_part = layout.last_sum(first_part)
    second_arrived = layout.exchange(layout.total(second_arrived), 2)
    tokens_grad = pl.pallas_call(
        token_grad_body,
        grid=(3,),
        in_specs=[grads_spec, pl.BlockSpec((hidden, hidden), lambda j: (0, j)), full_spec],
        out_specs=full_spec,
        out_shape=array(token_count, hidden, dtype=BF16),
        scratch_shapes=[pltpu.VMEM((token_count, hidden), F32)],
        compiler_params=params(),
        cost_estimate=cost(1e6, 1e5),
        name="token_grad",
    )(grads, entry, grad_first)
    dense_weight_grad, class_weight_grad, head_rows = pl.pallas_call(
        functools.partial(head_sums_body, pairs=pairs),
        out_shape=(array(SD, SD), array(SD, SD), array(8, SD)),
        compiler_params=params(),
        cost_estimate=cost(1e6, 1e5),
        name="head_sums",
    )(small)
    third_arrived, second_arrived, first_part, tokens_grad, dense_weight_grad = lax.optimization_barrier(
        (third_arrived, second_arrived, first_part, tokens_grad, dense_weight_grad)
    )
    third = layout.total(third_arrived)
    third_arrived = layout.permutes(third, 2)

    def end(body, name, arrived, *shapes):
        return pl.pallas_call(
            body,
            out_shape=tuple(array(*shape) for shape in shapes),
            compiler_params=params(),
            cost_estimate=cost(1e6, 1e5),
            name=name,
        )(*arrived)

    down_grad, student_weight_grad, first_vectors = end(
        functools.partial(first_end_body, hidden=hidden, ratio=ratio), "first_end", [first_part],
        (ratio * part, hidden), (part, SD), (part, LANES),
    )
    up_grad, out_grad, second_vectors = end(
        functools.partial(second_end_body, hidden=hidden, ratio=ratio), "second_end", [second_arrived],
        (part, inner_dim), (part, hidden), (part, LANES),
    )
    qkv_grad, third_vectors = end(
        functools.partial(third_end_body, hidden=hidden), "third_end", third_arrived,
        (part, 3 * hidden), (part, LANES),
    )
    return (
        carried,
        logits,
        tokens_grad,
        qkv_grad,
        third_vectors[:, 0],
        third_vectors[:, 1],
        out_grad,
        second_vectors[:, 0],
        second_vectors[:, 1],
        second_vectors[:, 2],
        up_grad,
        second_vectors[:, 3 : 3 + ratio].reshape(-1),
        down_grad,
        first_vectors[:, 0],
        first_vectors[:, 1],
        first_vectors[:, 2],
        student_weight_grad,
        head_rows[1],
        head_rows[0],
        dense_weight_grad,
        head_rows[2],
        class_weight_grad[:, :classes],
        head_rows[3, :classes],
    )


def solution(mesh):
    layout = Layout(mesh)
    rows, flat, whole = P(layout.axes, None), P(layout.axes), P()

    def step(*args):
        return local(layout, *args)

    shard = (flat, flat, rows, flat, flat, flat, rows, flat, rows, flat, flat, flat, rows)
    return jax.shard_map(
        step,
        mesh=layout.mesh,
        in_specs=(rows,) * 7 + shard + (whole,) * 6,
        out_specs=(rows,) * 4 + shard + (whole,) * 6,
        check_vma=False,
    )
```

```python
import functools
import math

import jax
import jax.numpy as jnp
from jax import lax
from jax.experimental import pallas as pl
from jax.experimental.pallas import tpu as pltpu
from jax.sharding import Mesh
from jax.sharding import PartitionSpec as P

HD = 64
SD = 128
SH = 2
LAYER = 3
ROW = 512
MICRO = 2
LANES = 128

BF16 = jnp.bfloat16
F32 = jnp.float32
highest = lax.Precision.HIGHEST
norm_eps = 1e-12
masked_value = -1e30

QUERY_BIAS, VALUE_BIAS, OUT_BIAS, GAIN1, BIAS1, DOWN_BIAS, GAIN2, BIAS2, UP_BIAS = range(9)


def narrow(value):
    return value.astype(BF16)


def widen(value):
    return value.astype(F32)


def matmul(left, right, precision=None):
    return lax.dot_general(
        left, right, (((1,), (0,)), ((), ())), preferred_element_type=F32, precision=precision
    )


def left_inner(left, right, precision=None):
    return lax.dot_general(
        left, right, (((0,), (0,)), ((), ())), preferred_element_type=F32, precision=precision
    )


def right_inner(left, right, precision=None):
    return lax.dot_general(
        left, right, (((1,), (1,)), ((), ())), preferred_element_type=F32, precision=precision
    )


def params(*semantics, limit=58):
    return pltpu.CompilerParams(
        dimension_semantics=semantics or None, vmem_limit_bytes=limit * 1024 * 1024
    )


def cost(flops, nbytes, transcendentals=0):
    return pl.CostEstimate(
        flops=int(flops), bytes_accessed=int(nbytes), transcendentals=int(transcendentals)
    )


def fixed(shape, *at):
    where = at or (0,) * len(shape)
    return pl.BlockSpec(shape, lambda *_: where)


class Layout:
    def __init__(self, mesh):
        dp, fsdp = mesh.shape["dp"], mesh.shape["fsdp"]
        devices = mesh.devices
        if (dp, fsdp) == (8, 4):
            self.mesh = Mesh(devices.reshape(4, 2, 2, 2), ("z", "x", "y", "core"))
            self.dp = ("z", "x")
            self.stages = (("core",), ("x", "y"), ("z",))
        elif (dp, fsdp) == (64, 4):
            self.mesh = Mesh(devices.reshape(8, 4, 2, 4), ("z", "x", "core", "y"))
            self.dp = ("z", "x", "core")
            self.stages = (("core",), ("x", "y"), ("z",))
        else:
            self.mesh = mesh
            self.dp = ("dp",)
            self.stages = (("fsdp",), ("dp",))
        self.axes = tuple(self.mesh.axis_names)
        self.sizes = tuple(self.mesh.shape[name] for name in self.axes)
        self.count = math.prod(self.sizes)
        self.dp_count = dp
        self.extents = tuple(math.prod(self.mesh.shape[n] for n in stage) for stage in self.stages)
        order = [self.axes.index(name) for stage in self.stages for name in stage]
        self.place = []
        for device in range(self.count):
            at, rest = [], device
            for size in reversed(self.sizes):
                at.append(rest % size)
                rest //= size
            at = at[::-1]
            position = 0
            for axis in order:
                position = position * self.sizes[axis] + at[axis]
            self.place.append(position)
        self.device_at = [self.place.index(i) for i in range(self.count)]
        rest = self.count // self.sizes[0]
        self.late_place = [d % rest * self.sizes[0] + d // rest for d in range(self.count)]

    def exchange(self, value, stage):
        extent = self.extents[stage]
        value = value.reshape((extent, value.shape[0] // extent) + value.shape[1:])
        return lax.all_to_all(
            value, self.stages[stage], split_axis=0, concat_axis=0, tiled=True
        )

    def gather(self, value, beside):
        for stage in reversed(range(len(self.stages))):
            copies = jnp.broadcast_to(value, (self.extents[stage],) + value.shape)
            value = lax.all_to_all(
                copies, self.stages[stage], split_axis=0, concat_axis=0, tiled=True
            )
            if stage == len(self.stages) - 1:
                value, beside = lax.optimization_barrier((value, beside))
        order = [name for stage in self.stages for name in stage]
        tail = value.shape[-2:]
        value = value.reshape(tuple(self.mesh.shape[name] for name in order) + tail)
        back = tuple(order.index(name) for name in self.axes)
        value = value.transpose(back + (len(order), len(order) + 1))
        return value.reshape(self.count * tail[0], tail[1]), beside

    def late_sum(self, value):
        return lax.psum_scatter(value, self.axes[1:], scatter_dimension=0, tiled=True)

    def last_sum(self, value):
        return lax.psum_scatter(value, self.axes[:1], scatter_dimension=0, tiled=True)

    def permutes(self, value, stage):
        extent, axes = self.extents[stage], self.stages[stage]
        value = value.reshape((extent, value.shape[0] // extent) + value.shape[1:])
        me = lax.axis_index(axes)
        parts = [lax.dynamic_index_in_dim(value, me, 0, keepdims=False)]
        for step in range(1, extent):
            part = lax.dynamic_index_in_dim(value, lax.rem(me + step, extent), 0, keepdims=False)
            pairs = [(i, (i + step) % extent) for i in range(extent)]
            parts.append(lax.ppermute(part, axes, pairs))
        return parts

    def total(self, arrived, dtype=BF16):
        if isinstance(arrived, list):
            return sum(widen(part) for part in arrived).astype(dtype)
        return jnp.sum(widen(arrived), axis=0).astype(dtype)


def store_parts(ref, place, value, column):
    width = value.shape[1]
    if len(ref.shape) == 2:
        ref[:, pl.ds(column, width)] = value.astype(ref.dtype)
        return
    count, part, _ = ref.shape
    for device in range(count):
        ref[place[device], :, pl.ds(column, width)] = value[
            device * part : (device + 1) * part
        ].astype(ref.dtype)


def add_body(left, right, result):
    result[...] = (widen(left[...]) + widen(right[...])).astype(result.dtype)


def add(left, right):
    parts, part, columns = left.shape
    step = 4 if parts % 4 == 0 else 1
    spec = pl.BlockSpec((step, part, columns), lambda i: (i, 0, 0))
    return pl.pallas_call(
        add_body,
        grid=(parts // step,),
        in_specs=[spec, spec],
        out_specs=spec,
        out_shape=jax.ShapeDtypeStruct(left.shape, left.dtype),
        compiler_params=params(),
        cost_estimate=cost(1e6, 1e5),
        name="add",
    )(left, right)


class Return:
    def __init__(self, layout, slots):
        self.layout, self.slots = layout, slots
        extents = [layout.mesh.shape[name] for name in layout.dp]
        self.staged = len(extents) == 2 and extents[1] == 2
        self.extent = extents[0]
        self.here = [lax.axis_index(name) for name in layout.dp]

    def first_stage(self, value):
        if not self.staged:
            return [value]
        value = value.reshape((self.extent, 2, self.slots // (2 * self.extent)) + value.shape[1:])
        near = lax.dynamic_index_in_dim(value, self.here[1], 1, keepdims=False)
        far = lax.dynamic_index_in_dim(value, 1 - self.here[1], 1, keepdims=False)
        return [near, lax.ppermute(far, self.layout.dp[1], [(0, 1), (1, 0)])]

    def second_stage(self, arrived):
        if not self.staged:
            return [lax.all_to_all(arrived[0], self.layout.dp, split_axis=0, concat_axis=0, tiled=True)]
        both = jnp.stack(arrived, axis=1)
        both = both.reshape((self.extent, -1) + both.shape[3:])
        pieces = []
        for step in range(self.extent):
            piece = lax.dynamic_index_in_dim(
                both, lax.rem(self.here[0] + step, self.extent), 0, keepdims=False
            )
            if step > 0:
                pairs = [(i, (i + step) % self.extent) for i in range(self.extent)]
                piece = lax.ppermute(piece, self.layout.dp[0], pairs)
            pieces.append(piece)
        return pieces

    def position(self, target):
        if not self.staged:
            return target
        step = lax.rem(self.here[0] + self.extent - target // 2, self.extent)
        return 2 * step + jnp.bitwise_xor(target % 2, self.here[1])


class Sums:
    def __init__(self, layout, rows, split=True):
        self.layout = layout
        self.count, self.part = layout.count, rows // layout.count
        self.split = split and self.part % 8 == 0 and layout.extents[0] == 2

    def shapes(self, columns):
        if self.split:
            return (jax.ShapeDtypeStruct((self.count // 2, self.part, columns), BF16),) * 2
        return (jax.ShapeDtypeStruct((self.count * self.part, columns), BF16),)

    def specs(self, columns):
        return tuple(fixed(shape.shape) for shape in self.shapes(columns))

    def store(self, refs, core, value, column):
        width = value.shape[1]
        if not self.split:
            refs[0][:, pl.ds(column, width)] = value.astype(BF16)
            return
        half = self.count // 2

        def put(mine):
            for device in range(self.count):
                position = self.layout.place[device]
                ref = refs[0] if position // half == mine else refs[1]
                ref[position % half, :, pl.ds(column, width)] = value[
                    device * self.part : (device + 1) * self.part
                ].astype(BF16)

        for mine in range(2):
            pl.when(core[0] == mine)(functools.partial(put, mine))

    def first_stage(self, values):
        if self.split:
            other = lax.ppermute(values[1], self.layout.stages[0], [(0, 1), (1, 0)])
            return add(values[0], other)
        value = values[0].reshape(self.count, self.part, values[0].shape[1])
        value = value[jnp.asarray(self.layout.device_at)]
        return self.layout.total(self.layout.permutes(value, 0))


def interleave(width, ratio, dtype):
    size = width * ratio
    source = lax.broadcasted_iota(jnp.int32, (size, size), 0)
    target = lax.broadcasted_iota(jnp.int32, (size, size), 1)
    return (source == (target % width) * ratio + target // width).astype(dtype)


def pack_body(out, up, down, student, packed, *, ratio, hidden):
    part = out.shape[0]
    packed[:, :hidden] = out[...]
    base = hidden
    mix = interleave(LANES, ratio, BF16)
    for chunk in range(hidden // LANES):
        piece = narrow(
            matmul(up[:, chunk * ratio * LANES : (chunk + 1) * ratio * LANES], mix)
        )
        for j in range(ratio):
            at = base + j * hidden + chunk * LANES
            packed[:, at : at + LANES] = piece[:, j * LANES : (j + 1) * LANES]
    base += ratio * hidden
    row = lax.broadcasted_iota(jnp.int32, (part, part * ratio), 0)
    column = lax.broadcasted_iota(jnp.int32, (part, part * ratio), 1)
    for j in range(ratio):
        pick = (column == row * ratio + j).astype(BF16)
        packed[:, base + j * hidden : base + (j + 1) * hidden] = narrow(matmul(pick, down[...]))
    base += ratio * hidden
    packed[:, base : base + SD] = student[...]


def turned(vectors):
    return widen(vectors).T


def attention_body(
    tokens, seg_column, seg_row, wq, wk, wv, vectors, query, key, value, context, log_totals, mask, rows
):
    step = pl.program_id(1)
    width = wq.shape[1]

    @pl.when((step == 0) & (pl.program_id(0) == 0))
    def _():
        rows[...] = turned(vectors[...])

    @pl.when(step == 0)
    def _():
        mask[...] = jnp.where(seg_column[0] == seg_row[0], 0.0, masked_value)

    here = pl.ds(pl.multiple_of(step * width, width), width)
    x = tokens[...]
    q = narrow(matmul(x, wq[...]) + rows[QUERY_BIAS : QUERY_BIAS + 1, here])
    k = narrow(matmul(x, wk[...]))
    v = narrow(matmul(x, wv[...]) + rows[VALUE_BIAS : VALUE_BIAS + 1, here])
    query[...] = q
    key[...] = k
    value[...] = v
    lane = lax.broadcasted_iota(jnp.int32, (x.shape[0], LANES), 1)
    scale = BF16(1.0 / math.sqrt(HD))
    for block in range(width // LANES):
        cut = slice(block * LANES, (block + 1) * LANES)
        q_block, k_block, v_turned = q[:, cut] * scale, k[:, cut], v[:, cut].T
        parts = []
        for head in range(LANES // HD):
            mine = (lane >= head * HD) & (lane < (head + 1) * HD)
            scores = right_inner(k_block, jnp.where(mine, q_block, BF16(0))) + mask[...]
            top = jnp.max(scores, axis=0, keepdims=True)
            exponent = jnp.exp(scores - top)
            total = jnp.sum(exponent, axis=0, keepdims=True)
            probs = narrow(exponent * (1.0 / total))
            at = block * (LANES // HD) + head
            log_totals[0, at : at + 1] = top + jnp.log(total)
            parts.append(matmul(v_turned[head * HD : (head + 1) * HD], probs))
        context[:, cut] = narrow(jnp.concatenate(parts, axis=0)).T


def attention_grad_body(
    branch, seg_column, seg_row, query, key, value, log_totals, out_weight, grads, mask
):
    width = query.shape[1]

    @pl.when(pl.program_id(1) == 0)
    def _():
        mask[...] = jnp.where(seg_column[0] == seg_row[0], 0.0, masked_value)

    grad_context = narrow(right_inner(branch[...], out_weight[...]))
    lane = lax.broadcasted_iota(jnp.int32, (branch.shape[0], LANES), 1)
    scale = 1.0 / math.sqrt(HD)
    for block in range(width // LANES):
        cut = slice(block * LANES, (block + 1) * LANES)
        q_block, k_block, v_block = query[:, cut] * BF16(scale), key[:, cut], value[:, cut]
        g_block, k_turned = grad_context[:, cut], k_block.T
        grad_q, grad_k, grad_v = [], 0.0, 0.0
        for head in range(LANES // HD):
            mine = (lane >= head * HD) & (lane < (head + 1) * HD)
            q_head = jnp.where(mine, q_block, BF16(0))
            g_head = jnp.where(mine, g_block, BF16(0))
            scores = right_inner(k_block, q_head) + mask[...]
            at = block * (LANES // HD) + head
            probs = jnp.exp(scores - log_totals[0, at : at + 1])
            grad_probs = right_inner(v_block, g_head)
            inner = jnp.sum(probs * grad_probs, axis=0, keepdims=True)
            grad_scores = narrow(probs * (grad_probs - inner))
            grad_v += matmul(narrow(probs), g_head)
            grad_k += matmul(grad_scores, q_head)
            grad_q.append(matmul(k_turned[head * HD : (head + 1) * HD], grad_scores))
        grads[0, :, cut] = narrow(jnp.concatenate(grad_q, axis=0) * scale).T
        grads[1, :, cut] = narrow(grad_k)
        grads[2, :, cut] = narrow(grad_v)


def normalize(values):
    average = jnp.mean(values, axis=-1, keepdims=True)
    centered = values - average
    spread = jnp.mean(centered * centered, axis=-1, keepdims=True)
    scale = lax.rsqrt(spread + norm_eps)
    return centered * scale, scale


def gelu_and_slope(x):
    phi = 0.5 + 0.5 * lax.erf(x * math.sqrt(0.5))
    return x * phi, phi + x * (jnp.exp(-0.5 * (x * x)) * (1.0 / math.sqrt(2.0 * math.pi)))


CHUNK = 256


def forward_body(
    tokens, context, out_weight, up, down, student, vectors, student_bias,
    pre_first, normed, activated, slope, pre_second, outputs, student_rows, total, rows,
):
    step = pl.program_id(0)
    count = tokens.shape[0]

    @pl.when(step == 0)
    def _():
        rows[...] = turned(vectors[...])
        for low in range(0, count, CHUNK):
            cut = slice(low, low + CHUNK)
            pre = (
                widen(tokens[cut])
                + matmul(context[cut], out_weight[...])
                + rows[OUT_BIAS : OUT_BIAS + 1]
            )
            pre_first[cut] = pre
            hat, _ = normalize(pre)
            value = narrow(hat * rows[GAIN1 : GAIN1 + 1] + rows[BIAS1 : BIAS1 + 1])
            normed[cut] = value
            total[cut] = widen(value) + rows[DOWN_BIAS : DOWN_BIAS + 1]

    bias = rows[pl.ds(UP_BIAS + step, 1)]
    for low in range(0, count, CHUNK):
        cut = slice(low, low + CHUNK)
        value, grad = gelu_and_slope(matmul(normed[cut], up[...]) + bias)
        value = narrow(value)
        activated[cut] = value
        slope[cut] = narrow(grad)
        total[cut] += matmul(value, down[...])

    @pl.when(step == pl.num_programs(0) - 1)
    def _():
        for low in range(0, count, CHUNK):
            cut = slice(low, low + CHUNK)
            pre = total[cut]
            pre_second[cut] = pre
            hat, _ = normalize(pre)
            value = narrow(hat * rows[GAIN2 : GAIN2 + 1] + rows[BIAS2 : BIAS2 + 1])
            outputs[cut] = value
            student_rows[cut] = matmul(value, student[...]) + student_bias[...]


def select_body(index, source, target):
    place = lax.broadcasted_iota(jnp.int32, (index.shape[0], source.shape[0]), 1)
    target[...] = narrow(matmul((index[...] == place).astype(BF16), source[...]))


def student_body(
    student_rows, segment, query, dense_weight, dense_bias, class_weight, class_bias, logits_grad,
    logits, student_grad, small,
):
    count, _ = student_rows.shape
    pairs, classes = logits_grad.shape
    wide = -(-pairs // LANES) * LANES
    head = SD // SH
    scale = 1.0 / math.sqrt(head)
    rows = student_rows[...]
    member = segment[...] == lax.broadcasted_iota(jnp.int32, (count, wide), 1)
    one_hot = member.astype(F32)
    lane = lax.broadcasted_iota(jnp.int32, (count, SD), 1)

    def by_head(values):
        return [
            jnp.sum(
                jnp.where((lane >= a * head) & (lane < (a + 1) * head), values, 0.0),
                axis=1,
                keepdims=True,
            )
            for a in range(SH)
        ]

    def spread(columns):
        value = columns[0]
        for a in range(1, SH):
            value = jnp.where(lane >= a * head, columns[a], value)
        return jnp.broadcast_to(value, (count, SD))

    def of_pair(row):
        return jnp.sum(jnp.where(member, row, 0.0), axis=1, keepdims=True)

    def over_pair(column):
        return jnp.sum(jnp.where(member, column, 0.0), axis=0, keepdims=True)

    weights = []
    for score in by_head(rows * query[...]):
        score = score * scale
        top = jnp.max(jnp.where(member, score, masked_value), axis=0, keepdims=True)
        exponent = jnp.exp(score - of_pair(top))
        weights.append(exponent / of_pair(over_pair(exponent)))
    weight = spread(weights)
    pooled = left_inner(one_hot, weight * rows, highest)
    dense = jnp.tanh(matmul(pooled, dense_weight[...], highest) + dense_bias[...])
    logits[...] = matmul(dense[:pairs], class_weight[...], highest) + class_bias[...]

    grad = logits_grad[...]
    grad_pre = right_inner(grad, class_weight[...], highest) * (
        1.0 - dense[:pairs] * dense[:pairs]
    )
    small[...] = jnp.zeros_like(small)
    small[:pairs] = pooled[:pairs]
    small[pairs : 2 * pairs] = grad_pre
    small[2 * pairs : 3 * pairs] = dense[:pairs]
    small[3 * pairs : 4 * pairs, :classes] = grad
    at = 4 * pairs
    grad_pooled = right_inner(grad_pre, dense_weight[...], highest)
    grad_token = matmul(one_hot[:, :pairs], grad_pooled, highest)
    grad_score = []
    for a, inner in enumerate(by_head(rows * grad_token)):
        product = weights[a] * inner
        grad_score.append(weights[a] * (inner - of_pair(over_pair(product))))
    grad_score = spread(grad_score) * scale
    small[at : at + 1] = jnp.sum(grad_score * rows, axis=0, keepdims=True)
    result = narrow(weight * grad_token + grad_score * query[...])
    student_grad[...] = result
    small[at + 1 : at + 2] = jnp.sum(widen(result), axis=0, keepdims=True)


def head_sums_body(gathered, dense_weight_grad, class_weight_grad, rows, *, pairs):
    everyone = gathered[...]
    width = everyone.shape[2]

    def factor(i):
        return everyone[:, i * pairs : (i + 1) * pairs].reshape(-1, width)

    pooled, grad_pre, dense, grad = (factor(i) for i in range(4))
    dense_weight_grad[...] = left_inner(pooled, grad_pre, highest)
    class_weight_grad[...] = left_inner(dense, grad, highest)
    total = jnp.sum(everyone[:, 4 * pairs : 4 * pairs + 8], axis=0)
    row = lax.broadcasted_iota(jnp.int32, (8, width), 0)
    total = jnp.where(row == 2, jnp.sum(grad_pre, axis=0, keepdims=True), total)
    rows[...] = jnp.where(row == 3, jnp.sum(grad, axis=0, keepdims=True), total)


def norm_grad(grad, pre, gain):
    hat, scale = normalize(pre)
    scaled = grad * gain
    result = scale * (
        scaled
        - jnp.mean(scaled, axis=-1, keepdims=True)
        - hat * jnp.mean(scaled * hat, axis=-1, keepdims=True)
    )
    return (
        result,
        jnp.sum(grad * hat, axis=0, keepdims=True),
        jnp.sum(grad, axis=0, keepdims=True),
    )


def as_columns(rows, count, hidden):
    row = lax.broadcasted_iota(jnp.int32, (LANES, hidden), 0)
    block = jnp.zeros((LANES, hidden), F32)
    for i in range(count):
        block = jnp.where(row == i, rows[i], block)
    return block.T


def down_grad_body(
    slot, student_grad, student, vectors, pre_second, outputs, activated, *refs, ratio, place,
):
    *returned, grad_second, grad_down, shards, sums_ref = refs
    step = pl.program_id(0)
    count, hidden = pre_second.shape

    @pl.when(step == 0)
    def _():
        gain = turned(vectors[...])[GAIN2 : GAIN2 + 1]
        length = returned[0].shape[0]
        slot_place = lax.broadcasted_iota(jnp.int32, (CHUNK, length), 1)
        parts = []
        for low in range(0, count, CHUNK):
            cut = slice(low, low + CHUNK)
            grad = right_inner(student_grad[cut], student[...])
            for i, piece in enumerate(returned):
                pick = (slot[cut] - i * length == slot_place).astype(BF16)
                grad += matmul(pick, piece[...])
            result, gain_part, bias_part = norm_grad(grad, pre_second[cut], gain)
            grad_second[cut] = result
            low_result = narrow(result)
            grad_down[cut] = low_result
            parts.append((jnp.sum(widen(low_result), axis=0, keepdims=True), gain_part, bias_part))
        for i in range(3):
            sums_ref[i : i + 1] = sum(part[i] for part in parts)

    store_parts(
        shards,
        place,
        left_inner(activated[...], grad_down[...]),
        pl.multiple_of(step * hidden, LANES),
    )

    @pl.when(step == pl.num_programs(0) - 1)
    def _():
        at = ratio * hidden
        store_parts(shards, place, left_inner(outputs[...], student_grad[...]), at)
        vector_rows = [sums_ref[i : i + 1] for i in range(3)]
        store_parts(shards, place, as_columns(vector_rows, 3, hidden), at + SD)


def up_grad_body(
    core, grad_down, grad_second, down, up, slope, normed, pre_first, context, vectors,
    grad_first, grad_branch, *refs, sums, ratio,
):
    step = pl.program_id(0)
    *shards, total, bias_rows = refs
    count, hidden = pre_first.shape

    @pl.when(step == 0)
    def _():
        total[...] = grad_second[...]

    bias_part = 0.0
    pieces = []
    for low in range(0, count, CHUNK):
        cut = slice(low, low + CHUNK)
        grad = right_inner(grad_down[cut], down[...])
        grad = narrow(grad * widen(slope[cut]))
        pieces.append(grad)
        bias_part = bias_part + jnp.sum(widen(grad), axis=0, keepdims=True)
        total[cut] += right_inner(grad, up[...])

    bias_rows[pl.ds(step, 1)] = bias_part
    sums.store(
        shards,
        core,
        left_inner(normed[...], jnp.concatenate(pieces, axis=0)),
        pl.multiple_of(step * hidden, LANES),
    )

    @pl.when(step == pl.num_programs(0) - 1)
    def _():
        gain = turned(vectors[...])[GAIN1 : GAIN1 + 1]
        parts = []
        for low in range(0, count, CHUNK):
            cut = slice(low, low + CHUNK)
            result, gain_part, shift_part = norm_grad(total[cut], pre_first[cut], gain)
            grad_first[cut] = result
            low_result = narrow(result)
            grad_branch[cut] = low_result
            parts.append((jnp.sum(widen(low_result), axis=0, keepdims=True), gain_part, shift_part))
        vector_rows = [sum(part[i] for part in parts) for i in range(3)]
        vector_rows += [bias_rows[i : i + 1] for i in range(ratio)]
        sums.store(shards, core, left_inner(context[...], grad_branch[...]), ratio * hidden)
        sums.store(
            shards, core, as_columns(vector_rows, 3 + ratio, hidden), (ratio + 1) * hidden
        )


def qkv_grad_body(core, tokens, grads, *refs, sums):
    step = pl.program_id(0)
    *shards, bias_rows = refs
    hidden = tokens.shape[1]
    grad = grads[0]
    bias_rows[pl.ds(step, 1)] = jnp.sum(widen(grad), axis=0, keepdims=True)
    sums.store(
        shards, core, left_inner(tokens[...], grad), pl.multiple_of(step * hidden, LANES)
    )

    @pl.when(step == pl.num_programs(0) - 1)
    def _():
        vector_rows = [bias_rows[0:1], bias_rows[2:3]]
        sums.store(shards, core, as_columns(vector_rows, 2, hidden), 3 * hidden)


def token_grad_body(grads, weight, grad_first, result, total):
    step = pl.program_id(0)
    update = right_inner(grads[0], weight[...])

    @pl.when(step == 0)
    def _():
        total[...] = grad_first[...] + update

    @pl.when(step > 0)
    def _():
        total[...] += update

    @pl.when(step == pl.num_programs(0) - 1)
    def _():
        result[...] = narrow(total[...])


def stacked(parts):
    return jnp.concatenate([part.reshape(-1, part.shape[-1]) for part in parts], axis=0)


def first_end_body(*refs, hidden, ratio):
    *parts, down_grad, student_grad, vectors = refs
    rows = parts[0].shape[-2]
    every = stacked([widen(part[...]) for part in parts])
    target = lax.broadcasted_iota(jnp.int32, (rows * ratio, every.shape[0]), 0)
    source = lax.broadcasted_iota(jnp.int32, (rows * ratio, every.shape[0]), 1) % rows
    every_low = narrow(every)
    result = 0.0
    for j in range(ratio):
        pick = (target == source * ratio + j).astype(BF16)
        result += matmul(pick, every_low[:, j * hidden : (j + 1) * hidden])
    down_grad[...] = result
    total = sum(every[i : i + rows, ratio * hidden :] for i in range(0, every.shape[0], rows))
    student_grad[...] = total[:, :SD]
    vectors[...] = total[:, SD:]


def second_end_body(*refs, hidden, ratio):
    *parts, up_grad, out_grad, vectors = refs
    rows = parts[0].shape[-2]
    every = stacked([widen(part[...]) for part in parts])
    every_low = narrow(every)
    mix = interleave(LANES, ratio, BF16)
    for chunk in range(hidden // LANES):
        piece = jnp.concatenate(
            [
                every_low[:, j * hidden + chunk * LANES : j * hidden + (chunk + 1) * LANES]
                for j in range(ratio)
            ],
            axis=1,
        )
        piece = right_inner(piece, mix)
        at = chunk * ratio * LANES
        up_grad[:, at : at + ratio * LANES] = sum(
            piece[i : i + rows] for i in range(0, piece.shape[0], rows)
        )
    total = sum(every[i : i + rows, ratio * hidden :] for i in range(0, every.shape[0], rows))
    out_grad[...] = total[:, :hidden]
    vectors[...] = total[:, hidden:]


def third_end_body(*refs, hidden):
    *parts, qkv_grad, vectors = refs
    total = sum(widen(part[...]).reshape(part.shape[-2:]) for part in parts)
    qkv_grad[...] = total[:, : 3 * hidden]
    vectors[...] = total[:, 3 * hidden :]


def local(
    layout,
    tokens,
    lengths,
    exit_layers,
    destination,
    carried_grad,
    logits_grad,
    qkv_weight,
    query_bias,
    value_bias,
    out_weight,
    out_bias,
    norm1_gain,
    norm1_bias,
    up_weight,
    up_bias,
    down_weight,
    down_bias,
    norm2_gain,
    norm2_bias,
    student_weight,
    student_bias,
    pool_query,
    dense_weight,
    dense_bias,
    class_weight,
    class_bias,
):
    axes, count, dp_count = layout.axes, layout.count, layout.dp_count
    pair_count = lengths.shape[1]
    slots = carried_grad.shape[0]
    slot_width = slots // dp_count
    token_count, hidden = tokens.shape
    inner_dim = up_weight.shape[1]
    part = hidden // count
    ratio = inner_dim // hidden
    classes = class_weight.shape[1]
    sums = Sums(layout, hidden)
    core = lax.axis_index(layout.stages[0]).astype(jnp.int32).reshape(1)
    core_spec = pl.BlockSpec(memory_space=pltpu.SMEM)
    width = 2 * LANES
    blocks = hidden // width
    micro = token_count // ROW

    def array(*shape, dtype=F32):
        return jax.ShapeDtypeStruct(shape, dtype)

    vector_list = (
        query_bias, value_bias, out_bias, norm1_gain, norm1_bias, down_bias, norm2_gain, norm2_bias,
    )
    columns = jnp.concatenate(
        [v[:, None] for v in vector_list]
        + [up_bias.reshape(part, ratio), jnp.zeros((part, LANES - len(vector_list) - ratio), BF16)],
        axis=1,
    )
    packed_width = (1 + 2 * ratio) * hidden + SD
    packed = pl.pallas_call(
        functools.partial(pack_body, ratio=ratio, hidden=hidden),
        out_shape=array(part, packed_width, dtype=BF16),
        compiler_params=params(),
        name="pack",
    )(out_weight, up_weight, down_weight, student_weight)
    gathered = lax.all_gather(packed, axes, axis=0, tiled=True)
    returning = Return(layout, slots)
    entry, returned = layout.gather(
        jnp.concatenate([qkv_weight, columns], axis=1), returning.first_stage(carried_grad)
    )
    student_at = (1 + 2 * ratio) * hidden // LANES
    out_spec = fixed((hidden, hidden), 0, 0)
    up_spec = pl.BlockSpec((hidden, hidden), lambda j: (0, 1 + j))
    down_spec = pl.BlockSpec((hidden, hidden), lambda j: (0, 1 + ratio + j))
    student_spec = fixed((hidden, SD), 0, student_at)
    vector_spec = fixed((hidden, LANES), 0, 3 * hidden // LANES)
    full_spec = fixed((token_count, hidden))
    column_spec = pl.BlockSpec((token_count, hidden), lambda j: (0, j))

    place = jnp.arange(ROW, dtype=jnp.int32)
    pair_ids = jnp.arange(pair_count, dtype=jnp.int32)
    ends = jnp.cumsum(lengths, axis=1)
    starts = ends - lengths
    alive = (exit_layers > LAYER).astype(jnp.int32)
    targets = returning.position(destination.reshape(micro, pair_count))
    segment = jnp.sum((place[None, :, None] >= ends[:, None, :]).astype(jnp.int32), axis=2)
    member = (segment[:, :, None] == pair_ids[None, None, :]).astype(jnp.int32)
    token_slot = jnp.sum(
        member * jnp.where(alive > 0, targets * slot_width - starts, -slots - ROW)[:, None, :], axis=2
    ) + place[None, :]
    token_slot = jnp.where(token_slot < 0, -1, token_slot).reshape(token_count, 1)
    flat_segment = (segment + pair_count * jnp.arange(micro, dtype=jnp.int32)[:, None]).reshape(
        token_count, 1
    )
    seg_column, seg_row = segment[:, :, None], segment[:, None, :]
    flat_starts = (starts + ROW * jnp.arange(micro, dtype=jnp.int32)[:, None]).reshape(-1)
    dp_ids = jnp.arange(dp_count, dtype=jnp.int32)
    chosen = (destination.reshape(-1)[None, :] == dp_ids[:, None]).astype(jnp.int32)
    send_start = jnp.sum(chosen * flat_starts[None, :], axis=1)
    send_length = jnp.sum(chosen * (lengths * alive).reshape(-1)[None, :], axis=1)
    slot_place = jnp.arange(slot_width, dtype=jnp.int32)
    slot_token = jnp.where(
        slot_place[None, :] < send_length[:, None], send_start[:, None] + slot_place[None, :], -1
    ).reshape(slots, 1)


    row_specs = [
        pl.BlockSpec((1, ROW, 1), lambda r, p: (r, 0, 0)),
        pl.BlockSpec((1, 1, ROW), lambda r, p: (r, 0, 0)),
    ]
    block_spec = pl.BlockSpec((ROW, width), lambda r, p: (r, p))
    pair_flops = 2 * token_count * ROW * hidden
    heads = max(8, width // HD)
    log_spec = pl.BlockSpec((1, heads, ROW), lambda r, p: (r * blocks + p, 0, 0))
    query, key, value, context, log_totals = pl.pallas_call(
        attention_body,
        grid=(micro, blocks),
        in_specs=[pl.BlockSpec((ROW, hidden), lambda r, p: (r, 0))]
        + row_specs
        + [
            pl.BlockSpec((hidden, width), lambda r, p: (0, p)),
            pl.BlockSpec((hidden, width), lambda r, p: (0, blocks + p)),
            pl.BlockSpec((hidden, width), lambda r, p: (0, 2 * blocks + p)),
            vector_spec,
        ],
        out_specs=(block_spec,) * 4 + (log_spec,),
        out_shape=(array(token_count, hidden, dtype=BF16),) * 4 + (array(micro * blocks, heads, ROW),),
        scratch_shapes=[pltpu.VMEM((ROW, ROW), F32), pltpu.VMEM((LANES, hidden), F32)],
        compiler_params=params(),
        cost_estimate=cost(1e6, 1e5),
        name="attention",
    )(tokens, seg_column, seg_row, entry, entry, entry, entry)

    context, returned = lax.optimization_barrier((context, returned))
    returned = returning.second_stage(returned)

    pre_first, normed, activated, slope, pre_second, outputs, student_rows = pl.pallas_call(
        forward_body,
        grid=(ratio,),
        in_specs=[full_spec, full_spec, out_spec, up_spec, down_spec, student_spec, vector_spec, fixed((1, SD))],
        out_specs=(full_spec, full_spec, column_spec, column_spec, full_spec, full_spec, fixed((token_count, SD))),
        out_shape=(
            array(token_count, hidden),
            array(token_count, hidden, dtype=BF16),
            array(token_count, inner_dim, dtype=BF16),
            array(token_count, inner_dim, dtype=BF16),
            array(token_count, hidden),
            array(token_count, hidden, dtype=BF16),
            array(token_count, SD),
        ),
        scratch_shapes=[pltpu.VMEM((token_count, hidden), F32), pltpu.VMEM((LANES, hidden), F32)],
        compiler_params=params(),
        cost_estimate=cost(1e6, 1e5),
        name="forward",
    )(tokens, context, gathered, gathered, gathered, gathered, entry, student_bias[None, :])

    step = 512 if slots % 512 == 0 else slots
    outgoing = pl.pallas_call(
        select_body,
        grid=(slots // step,),
        in_specs=[pl.BlockSpec((step, 1), lambda i: (i, 0)), full_spec],
        out_specs=pl.BlockSpec((step, hidden), lambda i: (i, 0)),
        out_shape=array(slots, hidden, dtype=BF16),
        compiler_params=params(),
        cost_estimate=cost(1e6, 1e5),
        name="select",
    )(slot_token, outputs)

    pairs = logits_grad.shape[0]
    logits, student_grad, small = pl.pallas_call(
        student_body,
        out_shape=(
            array(*logits_grad.shape),
            array(token_count, SD, dtype=BF16),
            array(4 * pairs + 8, SD),
        ),
        compiler_params=params(),
        cost_estimate=cost(1e6, 1e5),
        name="student",
    )(
        student_rows, flat_segment, pool_query[None, :], dense_weight, dense_bias[None, :],
        class_weight, class_bias[None, :], logits_grad,
    )
    outgoing, student_grad, *returned = lax.optimization_barrier((outgoing, student_grad, *returned))
    carried = lax.all_to_all(outgoing, layout.dp, split_axis=0, concat_axis=0, tiled=True)

    first_width = ratio * hidden + SD + LANES
    first_shape = (count, part, first_width) if part % 8 == 0 else (hidden, first_width)
    grad_second, grad_down, first = pl.pallas_call(
        functools.partial(down_grad_body, ratio=ratio, place=layout.late_place),
        grid=(ratio,),
        in_specs=[
            fixed((token_count, 1)), fixed((token_count, SD)), student_spec,
            vector_spec, full_spec, full_spec, column_spec,
        ]
        + [fixed(piece.shape) for piece in returned],
        out_specs=(full_spec, full_spec, fixed(first_shape)),
        out_shape=(
            array(token_count, hidden),
            array(token_count, hidden, dtype=BF16),
            array(*first_shape, dtype=BF16),
        ),
        scratch_shapes=[pltpu.VMEM((8, hidden), F32)],
        compiler_params=params(),
        cost_estimate=cost(1e6, 1e5),
        name="down_grad",
    )(token_slot, student_grad, gathered, entry, pre_second, outputs, activated, *returned)
    if part % 8 != 0:
        order = [layout.late_place.index(i) for i in range(count)]
        first = first.reshape(count, part, first_width)[jnp.asarray(order)]
    first_part = layout.late_sum(first)

    second_width = (ratio + 1) * hidden + LANES
    grad_first, grad_branch, *second = pl.pallas_call(
        functools.partial(up_grad_body, sums=sums, ratio=ratio),
        grid=(ratio,),
        in_specs=[
            core_spec, full_spec, full_spec, down_spec, up_spec, column_spec, full_spec, full_spec, full_spec,
            vector_spec,
        ],
        out_specs=(full_spec, full_spec) + sums.specs(second_width),
        out_shape=(
            array(token_count, hidden),
            array(token_count, hidden, dtype=BF16),
        )
        + sums.shapes(second_width),
        scratch_shapes=[pltpu.VMEM((token_count, hidden), F32), pltpu.VMEM((8, hidden), F32)],
        compiler_params=params(),
        cost_estimate=cost(1e6, 1e5),
        name="up_grad",
    )(core, grad_down, grad_second, gathered, gathered, slope, normed, pre_first, context, entry)
    second, grad_branch, carried = lax.optimization_barrier(
        (sums.first_stage(second), grad_branch, carried)
    )
    second_arrived = layout.exchange(second, 1)
    grads = pl.pallas_call(
        attention_grad_body,
        grid=(micro, blocks),
        in_specs=[pl.BlockSpec((ROW, hidden), lambda r, p: (r, 0))]
        + row_specs
        + [block_spec] * 3
        + [log_spec, pl.BlockSpec((width, hidden), lambda r, p: (p, 0))],
        out_specs=pl.BlockSpec((3, ROW, width), lambda r, p: (0, r, p)),
        out_shape=array(3, token_count, hidden, dtype=BF16),
        scratch_shapes=[pltpu.VMEM((ROW, ROW), F32)],
        compiler_params=params(),
        cost_estimate=cost(1e6, 1e5),
        name="attention_grad",
    )(grad_branch, seg_column, seg_row, query, key, value, log_totals, gathered)

    third_width = 3 * hidden + LANES
    grads_spec = pl.BlockSpec((1, token_count, hidden), lambda j: (j, 0, 0))
    third = pl.pallas_call(
        functools.partial(qkv_grad_body, sums=sums),
        grid=(3,),
        in_specs=[core_spec, full_spec, grads_spec],
        out_specs=sums.specs(third_width),
        out_shape=sums.shapes(third_width),
        scratch_shapes=[pltpu.VMEM((8, hidden), F32)],
        compiler_params=params(),
        cost_estimate=cost(1e6, 1e5),
        name="qkv_grad",
    )(core, tokens, grads)
    third, second_arrived, small = lax.optimization_barrier((third, second_arrived, small))
    small = lax.all_to_all(
        jnp.broadcast_to(small, (count,) + small.shape), axes, split_axis=0, concat_axis=0, tiled=True
    )
    third = sums.first_stage(third)
    third, second_arrived, first_part = lax.optimization_barrier((third, second_arrived, first_part))
    third_arrived = layout.permutes(third, 1)
    first_part = layout.last_sum(first_part)
    third_arrived[1], second_arrived, small = lax.optimization_barrier(
        (third_arrived[1], second_arrived, small)
    )
    second_arrived = layout.exchange(layout.total(second_arrived), 2)
    tokens_grad = pl.pallas_call(
        token_grad_body,
        grid=(3,),
        in_specs=[grads_spec, pl.BlockSpec((hidden, hidden), lambda j: (0, j)), full_spec],
        out_specs=full_spec,
        out_shape=array(token_count, hidden, dtype=BF16),
        scratch_shapes=[pltpu.VMEM((token_count, hidden), F32)],
        compiler_params=params(),
        cost_estimate=cost(1e6, 1e5),
        name="token_grad",
    )(grads, entry, grad_first)
    dense_weight_grad, class_weight_grad, head_rows = pl.pallas_call(
        functools.partial(head_sums_body, pairs=pairs),
        out_shape=(array(SD, SD), array(SD, SD), array(8, SD)),
        compiler_params=params(),
        cost_estimate=cost(1e6, 1e5),
        name="head_sums",
    )(small)
    third_arrived, first_part, tokens_grad, dense_weight_grad = lax.optimization_barrier(
        (third_arrived, first_part, tokens_grad, dense_weight_grad)
    )
    third = layout.total(third_arrived)
    third_arrived = layout.permutes(third, 2)

    def end(body, name, arrived, *shapes):
        return pl.pallas_call(
            body,
            out_shape=tuple(array(*shape) for shape in shapes),
            compiler_params=params(),
            cost_estimate=cost(1e6, 1e5),
            name=name,
        )(*arrived)

    down_grad, student_weight_grad, first_vectors = end(
        functools.partial(first_end_body, hidden=hidden, ratio=ratio), "first_end", [first_part],
        (ratio * part, hidden), (part, SD), (part, LANES),
    )
    up_grad, out_grad, second_vectors = end(
        functools.partial(second_end_body, hidden=hidden, ratio=ratio), "second_end", [second_arrived],
        (part, inner_dim), (part, hidden), (part, LANES),
    )
    qkv_grad, third_vectors = end(
        functools.partial(third_end_body, hidden=hidden), "third_end", third_arrived,
        (part, 3 * hidden), (part, LANES),
    )
    return (
        carried,
        logits,
        tokens_grad,
        qkv_grad,
        third_vectors[:, 0],
        third_vectors[:, 1],
        out_grad,
        second_vectors[:, 0],
        second_vectors[:, 1],
        second_vectors[:, 2],
        up_grad,
        second_vectors[:, 3 : 3 + ratio].reshape(-1),
        down_grad,
        first_vectors[:, 0],
        first_vectors[:, 1],
        first_vectors[:, 2],
        student_weight_grad,
        head_rows[1],
        head_rows[0],
        dense_weight_grad,
        head_rows[2],
        class_weight_grad[:, :classes],
        head_rows[3, :classes],
    )


def solution(mesh):
    layout = Layout(mesh)
    rows, flat, whole = P(layout.axes, None), P(layout.axes), P()

    def step(*args):
        return local(layout, *args)

    shard = (flat, flat, rows, flat, flat, flat, rows, flat, rows, flat, flat, flat, rows)
    return jax.shard_map(
        step,
        mesh=layout.mesh,
        in_specs=(rows,) * 7 + shard + (whole,) * 6,
        out_specs=(rows,) * 4 + shard + (whole,) * 6,
        check_vma=False,
    )
```

```python
import functools
import math

import jax
import jax.numpy as jnp
from jax import lax
from jax.experimental import pallas as pl
from jax.experimental.pallas import tpu as pltpu
from jax.sharding import Mesh
from jax.sharding import PartitionSpec as P

HD = 64
SD = 128
SH = 2
LAYER = 3
ROW = 512
MICRO = 2
LANES = 128

BF16 = jnp.bfloat16
F32 = jnp.float32
highest = lax.Precision.HIGHEST
norm_eps = 1e-12
masked_value = -1e30

QUERY_BIAS, VALUE_BIAS, OUT_BIAS, GAIN1, BIAS1, DOWN_BIAS, GAIN2, BIAS2, UP_BIAS = range(9)


def narrow(value):
    return value.astype(BF16)


def widen(value):
    return value.astype(F32)


def matmul(left, right, precision=None):
    return lax.dot_general(
        left, right, (((1,), (0,)), ((), ())), preferred_element_type=F32, precision=precision
    )


def left_inner(left, right, precision=None):
    return lax.dot_general(
        left, right, (((0,), (0,)), ((), ())), preferred_element_type=F32, precision=precision
    )


def right_inner(left, right, precision=None):
    return lax.dot_general(
        left, right, (((1,), (1,)), ((), ())), preferred_element_type=F32, precision=precision
    )


def params(*semantics, limit=58):
    return pltpu.CompilerParams(
        dimension_semantics=semantics or None, vmem_limit_bytes=limit * 1024 * 1024
    )


def cost(flops, nbytes, transcendentals=0):
    return pl.CostEstimate(
        flops=int(flops), bytes_accessed=int(nbytes), transcendentals=int(transcendentals)
    )


def fixed(shape, *at):
    where = at or (0,) * len(shape)
    return pl.BlockSpec(shape, lambda *_: where)


class Layout:
    def __init__(self, mesh):
        dp, fsdp = mesh.shape["dp"], mesh.shape["fsdp"]
        devices = mesh.devices
        if (dp, fsdp) == (8, 4):
            self.mesh = Mesh(devices.reshape(4, 2, 2, 2), ("z", "x", "y", "core"))
            self.dp = ("z", "x")
            self.stages = (("core",), ("x", "y"), ("z",))
        elif (dp, fsdp) == (64, 4):
            self.mesh = Mesh(devices.reshape(8, 4, 2, 4), ("z", "x", "core", "y"))
            self.dp = ("z", "x", "core")
            self.stages = (("core",), ("x", "y"), ("z",))
        else:
            self.mesh = mesh
            self.dp = ("dp",)
            self.stages = (("fsdp",), ("dp",))
        self.axes = tuple(self.mesh.axis_names)
        self.sizes = tuple(self.mesh.shape[name] for name in self.axes)
        self.count = math.prod(self.sizes)
        self.dp_count = dp
        self.extents = tuple(math.prod(self.mesh.shape[n] for n in stage) for stage in self.stages)
        order = [self.axes.index(name) for stage in self.stages for name in stage]
        self.place = []
        for device in range(self.count):
            at, rest = [], device
            for size in reversed(self.sizes):
                at.append(rest % size)
                rest //= size
            at = at[::-1]
            position = 0
            for axis in order:
                position = position * self.sizes[axis] + at[axis]
            self.place.append(position)
        self.device_at = [self.place.index(i) for i in range(self.count)]
        rest = self.count // self.sizes[0]
        self.late_place = [d % rest * self.sizes[0] + d // rest for d in range(self.count)]

    def exchange(self, value, stage):
        extent = self.extents[stage]
        value = value.reshape((extent, value.shape[0] // extent) + value.shape[1:])
        return lax.all_to_all(
            value, self.stages[stage], split_axis=0, concat_axis=0, tiled=True
        )

    def gather(self, value, beside):
        for stage in reversed(range(len(self.stages))):
            copies = jnp.broadcast_to(value, (self.extents[stage],) + value.shape)
            value = lax.all_to_all(
                copies, self.stages[stage], split_axis=0, concat_axis=0, tiled=True
            )
            if stage == len(self.stages) - 1:
                value, beside = lax.optimization_barrier((value, beside))
        order = [name for stage in self.stages for name in stage]
        tail = value.shape[-2:]
        value = value.reshape(tuple(self.mesh.shape[name] for name in order) + tail)
        back = tuple(order.index(name) for name in self.axes)
        value = value.transpose(back + (len(order), len(order) + 1))
        return value.reshape(self.count * tail[0], tail[1]), beside

    def late_sum(self, value):
        return lax.psum_scatter(value, self.axes[1:], scatter_dimension=0, tiled=True)

    def last_sum(self, value):
        return lax.psum_scatter(value, self.axes[:1], scatter_dimension=0, tiled=True)

    def permutes(self, value, stage):
        extent, axes = self.extents[stage], self.stages[stage]
        value = value.reshape((extent, value.shape[0] // extent) + value.shape[1:])
        me = lax.axis_index(axes)
        parts = [lax.dynamic_index_in_dim(value, me, 0, keepdims=False)]
        for step in range(1, extent):
            part = lax.dynamic_index_in_dim(value, lax.rem(me + step, extent), 0, keepdims=False)
            pairs = [(i, (i + step) % extent) for i in range(extent)]
            parts.append(lax.ppermute(part, axes, pairs))
        return parts

    def total(self, arrived, dtype=BF16):
        if isinstance(arrived, list):
            return sum(widen(part) for part in arrived).astype(dtype)
        return jnp.sum(widen(arrived), axis=0).astype(dtype)


def store_parts(ref, place, value, column):
    width = value.shape[1]
    if len(ref.shape) == 2:
        ref[:, pl.ds(column, width)] = value.astype(ref.dtype)
        return
    count, part, _ = ref.shape
    for device in range(count):
        ref[place[device], :, pl.ds(column, width)] = value[
            device * part : (device + 1) * part
        ].astype(ref.dtype)


def add_body(left, right, result):
    result[...] = (widen(left[...]) + widen(right[...])).astype(result.dtype)


def add(left, right):
    parts, part, columns = left.shape
    rows = parts * part
    step = next(n for n in (96, 64, 48, 32, rows) if rows % n == 0)
    spec = pl.BlockSpec((step, columns), lambda i: (i, 0))
    total = pl.pallas_call(
        add_body,
        grid=(rows // step,),
        in_specs=[spec, spec],
        out_specs=spec,
        out_shape=jax.ShapeDtypeStruct((rows, columns), left.dtype),
        compiler_params=params(),
        cost_estimate=cost(1e6, 1e5),
        name="add",
    )(left.reshape(rows, columns), right.reshape(rows, columns))
    return total.reshape(left.shape)


class Return:
    def __init__(self, layout, slots):
        self.layout, self.slots = layout, slots
        extents = [layout.mesh.shape[name] for name in layout.dp]
        self.staged = len(extents) == 2 and extents[1] == 2
        self.extent = extents[0]
        self.here = [lax.axis_index(name) for name in layout.dp]

    def first_stage(self, value):
        if not self.staged:
            return [value]
        value = value.reshape((self.extent, 2, self.slots // (2 * self.extent)) + value.shape[1:])
        near = lax.dynamic_index_in_dim(value, self.here[1], 1, keepdims=False)
        far = lax.dynamic_index_in_dim(value, 1 - self.here[1], 1, keepdims=False)
        return [near, lax.ppermute(far, self.layout.dp[1], [(0, 1), (1, 0)])]

    def second_stage(self, arrived):
        if not self.staged:
            return [lax.all_to_all(arrived[0], self.layout.dp, split_axis=0, concat_axis=0, tiled=True)]
        both = jnp.stack(arrived, axis=1)
        both = both.reshape((self.extent, -1) + both.shape[3:])
        pieces = []
        for step in range(self.extent):
            piece = lax.dynamic_index_in_dim(
                both, lax.rem(self.here[0] + step, self.extent), 0, keepdims=False
            )
            if step > 0:
                pairs = [(i, (i + step) % self.extent) for i in range(self.extent)]
                piece = lax.ppermute(piece, self.layout.dp[0], pairs)
            pieces.append(piece)
        return pieces

    def position(self, target):
        if not self.staged:
            return target
        step = lax.rem(self.here[0] + self.extent - target // 2, self.extent)
        return 2 * step + jnp.bitwise_xor(target % 2, self.here[1])


class Sums:
    def __init__(self, layout, rows, split=True):
        self.layout = layout
        self.count, self.part = layout.count, rows // layout.count
        self.split = split and self.part % 8 == 0 and layout.extents[0] == 2

    def shapes(self, columns):
        if self.split:
            return (jax.ShapeDtypeStruct((self.count // 2, self.part, columns), BF16),) * 2
        return (jax.ShapeDtypeStruct((self.count * self.part, columns), BF16),)

    def specs(self, columns):
        return tuple(fixed(shape.shape) for shape in self.shapes(columns))

    def store(self, refs, core, value, column):
        width = value.shape[1]
        if not self.split:
            refs[0][:, pl.ds(column, width)] = value.astype(BF16)
            return
        half = self.count // 2

        def put(mine):
            for device in range(self.count):
                position = self.layout.place[device]
                ref = refs[0] if position // half == mine else refs[1]
                ref[position % half, :, pl.ds(column, width)] = value[
                    device * self.part : (device + 1) * self.part
                ].astype(BF16)

        for mine in range(2):
            pl.when(core[0] == mine)(functools.partial(put, mine))

    def first_stage(self, values):
        if self.split:
            other = lax.ppermute(values[1], self.layout.stages[0], [(0, 1), (1, 0)])
            return add(values[0], other)
        value = values[0].reshape(self.count, self.part, values[0].shape[1])
        value = value[jnp.asarray(self.layout.device_at)]
        return self.layout.total(self.layout.permutes(value, 0))


def interleave(width, ratio, dtype):
    size = width * ratio
    source = lax.broadcasted_iota(jnp.int32, (size, size), 0)
    target = lax.broadcasted_iota(jnp.int32, (size, size), 1)
    return (source == (target % width) * ratio + target // width).astype(dtype)


def pack_body(out, up, down, student, packed, *, ratio, hidden):
    part = out.shape[0]
    packed[:, :hidden] = out[...]
    base = hidden
    mix = interleave(LANES, ratio, BF16)
    for chunk in range(hidden // LANES):
        piece = narrow(
            matmul(up[:, chunk * ratio * LANES : (chunk + 1) * ratio * LANES], mix)
        )
        for j in range(ratio):
            at = base + j * hidden + chunk * LANES
            packed[:, at : at + LANES] = piece[:, j * LANES : (j + 1) * LANES]
    base += ratio * hidden
    row = lax.broadcasted_iota(jnp.int32, (part, part * ratio), 0)
    column = lax.broadcasted_iota(jnp.int32, (part, part * ratio), 1)
    for j in range(ratio):
        pick = (column == row * ratio + j).astype(BF16)
        packed[:, base + j * hidden : base + (j + 1) * hidden] = narrow(matmul(pick, down[...]))
    base += ratio * hidden
    packed[:, base : base + SD] = student[...]


def turned(vectors):
    return widen(vectors).T


def attention_body(
    tokens, seg_column, seg_row, wq, wk, wv, vectors, query, key, value, context, log_totals, mask, rows
):
    step = pl.program_id(1)
    width = wq.shape[1]

    @pl.when((step == 0) & (pl.program_id(0) == 0))
    def _():
        rows[...] = turned(vectors[...])

    @pl.when(step == 0)
    def _():
        mask[...] = jnp.where(seg_column[0] == seg_row[0], 0.0, masked_value)

    here = pl.ds(pl.multiple_of(step * width, width), width)
    x = tokens[...]
    q = narrow(matmul(x, wq[...]) + rows[QUERY_BIAS : QUERY_BIAS + 1, here])
    k = narrow(matmul(x, wk[...]))
    v = narrow(matmul(x, wv[...]) + rows[VALUE_BIAS : VALUE_BIAS + 1, here])
    query[...] = q
    key[...] = k
    value[...] = v
    lane = lax.broadcasted_iota(jnp.int32, (x.shape[0], LANES), 1)
    scale = BF16(1.0 / math.sqrt(HD))
    for block in range(width // LANES):
        cut = slice(block * LANES, (block + 1) * LANES)
        q_block, k_block, v_turned = q[:, cut] * scale, k[:, cut], v[:, cut].T
        parts = []
        for head in range(LANES // HD):
            mine = (lane >= head * HD) & (lane < (head + 1) * HD)
            scores = right_inner(k_block, jnp.where(mine, q_block, BF16(0))) + mask[...]
            top = jnp.max(scores, axis=0, keepdims=True)
            exponent = jnp.exp(scores - top)
            total = jnp.sum(exponent, axis=0, keepdims=True)
            probs = narrow(exponent * (1.0 / total))
            at = block * (LANES // HD) + head
            log_totals[0, at : at + 1] = top + jnp.log(total)
            parts.append(matmul(v_turned[head * HD : (head + 1) * HD], probs))
        context[:, cut] = narrow(jnp.concatenate(parts, axis=0)).T


def attention_grad_body(
    branch, seg_column, seg_row, query, key, value, log_totals, out_weight, grads, mask
):
    width = query.shape[1]

    @pl.when(pl.program_id(1) == 0)
    def _():
        mask[...] = jnp.where(seg_column[0] == seg_row[0], 0.0, masked_value)

    grad_context = narrow(right_inner(branch[...], out_weight[...]))
    lane = lax.broadcasted_iota(jnp.int32, (branch.shape[0], LANES), 1)
    scale = 1.0 / math.sqrt(HD)
    for block in range(width // LANES):
        cut = slice(block * LANES, (block + 1) * LANES)
        q_block, k_block, v_block = query[:, cut] * BF16(scale), key[:, cut], value[:, cut]
        g_block, k_turned = grad_context[:, cut], k_block.T
        grad_q, grad_k, grad_v = [], 0.0, 0.0
        for head in range(LANES // HD):
            mine = (lane >= head * HD) & (lane < (head + 1) * HD)
            q_head = jnp.where(mine, q_block, BF16(0))
            g_head = jnp.where(mine, g_block, BF16(0))
            scores = right_inner(k_block, q_head) + mask[...]
            at = block * (LANES // HD) + head
            probs = jnp.exp(scores - log_totals[0, at : at + 1])
            grad_probs = right_inner(v_block, g_head)
            inner = jnp.sum(probs * grad_probs, axis=0, keepdims=True)
            grad_scores = narrow(probs * (grad_probs - inner))
            grad_v += matmul(narrow(probs), g_head)
            grad_k += matmul(grad_scores, q_head)
            grad_q.append(matmul(k_turned[head * HD : (head + 1) * HD], grad_scores))
        grads[0, :, cut] = narrow(jnp.concatenate(grad_q, axis=0) * scale).T
        grads[1, :, cut] = narrow(grad_k)
        grads[2, :, cut] = narrow(grad_v)


def normalize(values):
    average = jnp.mean(values, axis=-1, keepdims=True)
    centered = values - average
    spread = jnp.mean(centered * centered, axis=-1, keepdims=True)
    scale = lax.rsqrt(spread + norm_eps)
    return centered * scale, scale


def gelu_and_slope(x):
    phi = 0.5 + 0.5 * lax.erf(x * math.sqrt(0.5))
    return x * phi, phi + x * (jnp.exp(-0.5 * (x * x)) * (1.0 / math.sqrt(2.0 * math.pi)))


CHUNK = 256


def forward_body(
    tokens, context, out_weight, up, down, student, vectors, student_bias,
    pre_first, normed, activated, slope, pre_second, outputs, student_rows, total, rows,
):
    step = pl.program_id(0)
    count = tokens.shape[0]

    @pl.when(step == 0)
    def _():
        rows[...] = turned(vectors[...])
        for low in range(0, count, CHUNK):
            cut = slice(low, low + CHUNK)
            pre = (
                widen(tokens[cut])
                + matmul(context[cut], out_weight[...])
                + rows[OUT_BIAS : OUT_BIAS + 1]
            )
            pre_first[cut] = pre
            hat, _ = normalize(pre)
            value = narrow(hat * rows[GAIN1 : GAIN1 + 1] + rows[BIAS1 : BIAS1 + 1])
            normed[cut] = value
            total[cut] = widen(value) + rows[DOWN_BIAS : DOWN_BIAS + 1]

    bias = rows[pl.ds(UP_BIAS + step, 1)]
    for low in range(0, count, CHUNK):
        cut = slice(low, low + CHUNK)
        value, grad = gelu_and_slope(matmul(normed[cut], up[...]) + bias)
        value = narrow(value)
        activated[cut] = value
        slope[cut] = narrow(grad)
        total[cut] += matmul(value, down[...])

    @pl.when(step == pl.num_programs(0) - 1)
    def _():
        for low in range(0, count, CHUNK):
            cut = slice(low, low + CHUNK)
            pre = total[cut]
            pre_second[cut] = pre
            hat, _ = normalize(pre)
            value = narrow(hat * rows[GAIN2 : GAIN2 + 1] + rows[BIAS2 : BIAS2 + 1])
            outputs[cut] = value
            student_rows[cut] = matmul(value, student[...]) + student_bias[...]


def select_body(index, source, target):
    place = lax.broadcasted_iota(jnp.int32, (index.shape[0], source.shape[0]), 1)
    target[...] = narrow(matmul((index[...] == place).astype(BF16), source[...]))


def student_body(
    student_rows, segment, query, dense_weight, dense_bias, class_weight, class_bias, logits_grad,
    logits, student_grad, small,
):
    count, _ = student_rows.shape
    pairs, classes = logits_grad.shape
    wide = -(-pairs // LANES) * LANES
    head = SD // SH
    scale = 1.0 / math.sqrt(head)
    rows = student_rows[...]
    member = segment[...] == lax.broadcasted_iota(jnp.int32, (count, wide), 1)
    one_hot = member.astype(F32)
    lane = lax.broadcasted_iota(jnp.int32, (count, SD), 1)

    def by_head(values):
        return [
            jnp.sum(
                jnp.where((lane >= a * head) & (lane < (a + 1) * head), values, 0.0),
                axis=1,
                keepdims=True,
            )
            for a in range(SH)
        ]

    def spread(columns):
        value = columns[0]
        for a in range(1, SH):
            value = jnp.where(lane >= a * head, columns[a], value)
        return jnp.broadcast_to(value, (count, SD))

    def of_pair(row):
        return jnp.sum(jnp.where(member, row, 0.0), axis=1, keepdims=True)

    def over_pair(column):
        return jnp.sum(jnp.where(member, column, 0.0), axis=0, keepdims=True)

    weights = []
    for score in by_head(rows * query[...]):
        score = score * scale
        top = jnp.max(jnp.where(member, score, masked_value), axis=0, keepdims=True)
        exponent = jnp.exp(score - of_pair(top))
        weights.append(exponent / of_pair(over_pair(exponent)))
    weight = spread(weights)
    pooled = left_inner(one_hot, weight * rows, highest)
    dense = jnp.tanh(matmul(pooled, dense_weight[...], highest) + dense_bias[...])
    logits[...] = matmul(dense[:pairs], class_weight[...], highest) + class_bias[...]

    grad = logits_grad[...]
    grad_pre = right_inner(grad, class_weight[...], highest) * (
        1.0 - dense[:pairs] * dense[:pairs]
    )
    small[...] = jnp.zeros_like(small)
    small[:pairs] = pooled[:pairs]
    small[pairs : 2 * pairs, :classes] = grad
    at = 2 * pairs
    grad_pooled = right_inner(grad_pre, dense_weight[...], highest)
    grad_token = matmul(one_hot[:, :pairs], grad_pooled, highest)
    grad_score = []
    for a, inner in enumerate(by_head(rows * grad_token)):
        product = weights[a] * inner
        grad_score.append(weights[a] * (inner - of_pair(over_pair(product))))
    grad_score = spread(grad_score) * scale
    small[at : at + 1] = jnp.sum(grad_score * rows, axis=0, keepdims=True)
    result = narrow(weight * grad_token + grad_score * query[...])
    student_grad[...] = result
    small[at + 1 : at + 2] = jnp.sum(widen(result), axis=0, keepdims=True)


def head_sums_body(
    gathered, dense_weight, dense_bias, class_weight, dense_weight_grad, class_weight_grad, rows, *, pairs
):
    everyone = gathered[...]
    width = everyone.shape[2]

    def factor(i):
        return everyone[:, i * pairs : (i + 1) * pairs].reshape(-1, width)

    pooled, grad = factor(0), factor(1)
    dense = jnp.tanh(matmul(pooled, dense_weight[...], highest) + dense_bias[...])
    grad_pre = right_inner(grad[:, : class_weight.shape[1]], class_weight[...], highest) * (
        1.0 - dense * dense
    )
    total = jnp.sum(everyone[:, 2 * pairs : 2 * pairs + 8], axis=0)
    row = lax.broadcasted_iota(jnp.int32, (8, width), 0)
    total = jnp.where(row == 2, jnp.sum(grad_pre, axis=0, keepdims=True), total)
    total = jnp.where(row == 3, jnp.sum(grad, axis=0, keepdims=True), total)

    @pl.when(pl.program_id(0) == 0)
    def _():
        dense_weight_grad[...] = jnp.zeros_like(dense_weight_grad)
        class_weight_grad[...] = jnp.zeros_like(class_weight_grad)
        rows[...] = jnp.zeros_like(rows)

    dense_weight_grad[...] += left_inner(pooled, grad_pre, highest)
    class_weight_grad[...] += left_inner(dense, grad, highest)
    rows[...] += total


def norm_grad(grad, pre, gain):
    hat, scale = normalize(pre)
    scaled = grad * gain
    result = scale * (
        scaled
        - jnp.mean(scaled, axis=-1, keepdims=True)
        - hat * jnp.mean(scaled * hat, axis=-1, keepdims=True)
    )
    return (
        result,
        jnp.sum(grad * hat, axis=0, keepdims=True),
        jnp.sum(grad, axis=0, keepdims=True),
    )


def as_columns(rows, count, hidden):
    row = lax.broadcasted_iota(jnp.int32, (LANES, hidden), 0)
    block = jnp.zeros((LANES, hidden), F32)
    for i in range(count):
        block = jnp.where(row == i, rows[i], block)
    return block.T


def down_grad_body(
    slot, student_grad, student, vectors, pre_second, outputs, activated, *refs, ratio, place,
):
    *returned, grad_second, grad_down, shards, sums_ref = refs
    step = pl.program_id(0)
    count, hidden = pre_second.shape

    @pl.when(step == 0)
    def _():
        gain = turned(vectors[...])[GAIN2 : GAIN2 + 1]
        length = returned[0].shape[0]
        slot_place = lax.broadcasted_iota(jnp.int32, (CHUNK, length), 1)
        parts = []
        for low in range(0, count, CHUNK):
            cut = slice(low, low + CHUNK)
            grad = right_inner(student_grad[cut], student[...])
            for i, piece in enumerate(returned):
                pick = (slot[cut] - i * length == slot_place).astype(BF16)
                grad += matmul(pick, piece[...])
            result, gain_part, bias_part = norm_grad(grad, pre_second[cut], gain)
            grad_second[cut] = result
            low_result = narrow(result)
            grad_down[cut] = low_result
            parts.append((jnp.sum(widen(low_result), axis=0, keepdims=True), gain_part, bias_part))
        for i in range(3):
            sums_ref[i : i + 1] = sum(part[i] for part in parts)

    store_parts(
        shards,
        place,
        left_inner(activated[...], grad_down[...]),
        pl.multiple_of(step * hidden, LANES),
    )

    @pl.when(step == pl.num_programs(0) - 1)
    def _():
        at = ratio * hidden
        store_parts(shards, place, left_inner(outputs[...], student_grad[...]), at)
        vector_rows = [sums_ref[i : i + 1] for i in range(3)]
        store_parts(shards, place, as_columns(vector_rows, 3, hidden), at + SD)


def up_grad_body(
    core, grad_down, grad_second, down, up, slope, normed, pre_first, context, vectors,
    grad_first, grad_branch, *refs, sums, ratio,
):
    step = pl.program_id(0)
    *shards, total, bias_rows = refs
    count, hidden = pre_first.shape

    @pl.when(step == 0)
    def _():
        total[...] = grad_second[...]

    bias_part = 0.0
    pieces = []
    for low in range(0, count, CHUNK):
        cut = slice(low, low + CHUNK)
        grad = right_inner(grad_down[cut], down[...])
        grad = narrow(grad * widen(slope[cut]))
        pieces.append(grad)
        bias_part = bias_part + jnp.sum(widen(grad), axis=0, keepdims=True)
        total[cut] += right_inner(grad, up[...])

    bias_rows[pl.ds(step, 1)] = bias_part
    sums.store(
        shards,
        core,
        left_inner(normed[...], jnp.concatenate(pieces, axis=0)),
        pl.multiple_of(step * hidden, LANES),
    )

    @pl.when(step == pl.num_programs(0) - 1)
    def _():
        gain = turned(vectors[...])[GAIN1 : GAIN1 + 1]
        parts = []
        for low in range(0, count, CHUNK):
            cut = slice(low, low + CHUNK)
            result, gain_part, shift_part = norm_grad(total[cut], pre_first[cut], gain)
            grad_first[cut] = result
            low_result = narrow(result)
            grad_branch[cut] = low_result
            parts.append((jnp.sum(widen(low_result), axis=0, keepdims=True), gain_part, shift_part))
        vector_rows = [sum(part[i] for part in parts) for i in range(3)]
        vector_rows += [bias_rows[i : i + 1] for i in range(ratio)]
        sums.store(shards, core, left_inner(context[...], grad_branch[...]), ratio * hidden)
        sums.store(
            shards, core, as_columns(vector_rows, 3 + ratio, hidden), (ratio + 1) * hidden
        )


def qkv_grad_body(core, tokens, grads, *refs, sums):
    step = pl.program_id(0)
    *shards, bias_rows = refs
    hidden = tokens.shape[1]
    grad = grads[0]
    bias_rows[pl.ds(step, 1)] = jnp.sum(widen(grad), axis=0, keepdims=True)
    sums.store(
        shards, core, left_inner(tokens[...], grad), pl.multiple_of(step * hidden, LANES)
    )

    @pl.when(step == pl.num_programs(0) - 1)
    def _():
        vector_rows = [bias_rows[0:1], bias_rows[2:3]]
        sums.store(shards, core, as_columns(vector_rows, 2, hidden), 3 * hidden)


def token_grad_body(grads, weight, grad_first, result, total):
    step = pl.program_id(0)
    update = right_inner(grads[0], weight[...])

    @pl.when(step == 0)
    def _():
        total[...] = grad_first[...] + update

    @pl.when(step > 0)
    def _():
        total[...] += update

    @pl.when(step == pl.num_programs(0) - 1)
    def _():
        result[...] = narrow(total[...])


def stacked(parts):
    return jnp.concatenate([part.reshape(-1, part.shape[-1]) for part in parts], axis=0)


def first_end_body(*refs, hidden, ratio):
    *parts, down_grad, student_grad, vectors = refs
    rows = parts[0].shape[-2]
    every = stacked([widen(part[...]) for part in parts])
    target = lax.broadcasted_iota(jnp.int32, (rows * ratio, every.shape[0]), 0)
    source = lax.broadcasted_iota(jnp.int32, (rows * ratio, every.shape[0]), 1) % rows
    every_low = narrow(every)
    result = 0.0
    for j in range(ratio):
        pick = (target == source * ratio + j).astype(BF16)
        result += matmul(pick, every_low[:, j * hidden : (j + 1) * hidden])
    down_grad[...] = result
    total = sum(every[i : i + rows, ratio * hidden :] for i in range(0, every.shape[0], rows))
    student_grad[...] = total[:, :SD]
    vectors[...] = total[:, SD:]


def second_end_body(*refs, hidden, ratio):
    *parts, up_grad, out_grad, vectors = refs
    rows = parts[0].shape[-2]
    every = stacked([widen(part[...]) for part in parts])
    every_low = narrow(every)
    mix = interleave(LANES, ratio, BF16)
    for chunk in range(hidden // LANES):
        piece = jnp.concatenate(
            [
                every_low[:, j * hidden + chunk * LANES : j * hidden + (chunk + 1) * LANES]
                for j in range(ratio)
            ],
            axis=1,
        )
        piece = right_inner(piece, mix)
        at = chunk * ratio * LANES
        up_grad[:, at : at + ratio * LANES] = sum(
            piece[i : i + rows] for i in range(0, piece.shape[0], rows)
        )
    total = sum(every[i : i + rows, ratio * hidden :] for i in range(0, every.shape[0], rows))
    out_grad[...] = total[:, :hidden]
    vectors[...] = total[:, hidden:]


def third_end_body(*refs, hidden):
    *parts, qkv_grad, vectors = refs
    total = sum(widen(part[...]).reshape(part.shape[-2:]) for part in parts)
    qkv_grad[...] = total[:, : 3 * hidden]
    vectors[...] = total[:, 3 * hidden :]


def local(
    layout,
    tokens,
    lengths,
    exit_layers,
    destination,
    carried_grad,
    logits_grad,
    qkv_weight,
    query_bias,
    value_bias,
    out_weight,
    out_bias,
    norm1_gain,
    norm1_bias,
    up_weight,
    up_bias,
    down_weight,
    down_bias,
    norm2_gain,
    norm2_bias,
    student_weight,
    student_bias,
    pool_query,
    dense_weight,
    dense_bias,
    class_weight,
    class_bias,
):
    axes, count, dp_count = layout.axes, layout.count, layout.dp_count
    pair_count = lengths.shape[1]
    slots = carried_grad.shape[0]
    slot_width = slots // dp_count
    token_count, hidden = tokens.shape
    inner_dim = up_weight.shape[1]
    part = hidden // count
    ratio = inner_dim // hidden
    classes = class_weight.shape[1]
    sums = Sums(layout, hidden)
    core = lax.axis_index(layout.stages[0]).astype(jnp.int32).reshape(1)
    core_spec = pl.BlockSpec(memory_space=pltpu.SMEM)
    width = 2 * LANES
    blocks = hidden // width
    micro = token_count // ROW

    def array(*shape, dtype=F32):
        return jax.ShapeDtypeStruct(shape, dtype)

    vector_list = (
        query_bias, value_bias, out_bias, norm1_gain, norm1_bias, down_bias, norm2_gain, norm2_bias,
    )
    columns = jnp.concatenate(
        [v[:, None] for v in vector_list]
        + [up_bias.reshape(part, ratio), jnp.zeros((part, LANES - len(vector_list) - ratio), BF16)],
        axis=1,
    )
    packed_width = (1 + 2 * ratio) * hidden + SD
    packed = pl.pallas_call(
        functools.partial(pack_body, ratio=ratio, hidden=hidden),
        out_shape=array(part, packed_width, dtype=BF16),
        compiler_params=params(),
        name="pack",
    )(out_weight, up_weight, down_weight, student_weight)
    gathered = lax.all_gather(packed, axes, axis=0, tiled=True)
    returning = Return(layout, slots)
    entry, returned = layout.gather(
        jnp.concatenate([qkv_weight, columns], axis=1), returning.first_stage(carried_grad)
    )
    student_at = (1 + 2 * ratio) * hidden // LANES
    out_spec = fixed((hidden, hidden), 0, 0)
    up_spec = pl.BlockSpec((hidden, hidden), lambda j: (0, 1 + j))
    down_spec = pl.BlockSpec((hidden, hidden), lambda j: (0, 1 + ratio + j))
    student_spec = fixed((hidden, SD), 0, student_at)
    vector_spec = fixed((hidden, LANES), 0, 3 * hidden // LANES)
    full_spec = fixed((token_count, hidden))
    column_spec = pl.BlockSpec((token_count, hidden), lambda j: (0, j))

    place = jnp.arange(ROW, dtype=jnp.int32)
    pair_ids = jnp.arange(pair_count, dtype=jnp.int32)
    ends = jnp.cumsum(lengths, axis=1)
    starts = ends - lengths
    alive = (exit_layers > LAYER).astype(jnp.int32)
    targets = returning.position(destination.reshape(micro, pair_count))
    segment = jnp.sum((place[None, :, None] >= ends[:, None, :]).astype(jnp.int32), axis=2)
    member = (segment[:, :, None] == pair_ids[None, None, :]).astype(jnp.int32)
    token_slot = jnp.sum(
        member * jnp.where(alive > 0, targets * slot_width - starts, -slots - ROW)[:, None, :], axis=2
    ) + place[None, :]
    token_slot = jnp.where(token_slot < 0, -1, token_slot).reshape(token_count, 1)
    flat_segment = (segment + pair_count * jnp.arange(micro, dtype=jnp.int32)[:, None]).reshape(
        token_count, 1
    )
    seg_column, seg_row = segment[:, :, None], segment[:, None, :]
    flat_starts = (starts + ROW * jnp.arange(micro, dtype=jnp.int32)[:, None]).reshape(-1)
    dp_ids = jnp.arange(dp_count, dtype=jnp.int32)
    chosen = (destination.reshape(-1)[None, :] == dp_ids[:, None]).astype(jnp.int32)
    send_start = jnp.sum(chosen * flat_starts[None, :], axis=1)
    send_length = jnp.sum(chosen * (lengths * alive).reshape(-1)[None, :], axis=1)
    slot_place = jnp.arange(slot_width, dtype=jnp.int32)
    slot_token = jnp.where(
        slot_place[None, :] < send_length[:, None], send_start[:, None] + slot_place[None, :], -1
    ).reshape(slots, 1)


    row_specs = [
        pl.BlockSpec((1, ROW, 1), lambda r, p: (r, 0, 0)),
        pl.BlockSpec((1, 1, ROW), lambda r, p: (r, 0, 0)),
    ]
    block_spec = pl.BlockSpec((ROW, width), lambda r, p: (r, p))
    pair_flops = 2 * token_count * ROW * hidden
    heads = max(8, width // HD)
    log_spec = pl.BlockSpec((1, heads, ROW), lambda r, p: (r * blocks + p, 0, 0))
    query, key, value, context, log_totals = pl.pallas_call(
        attention_body,
        grid=(micro, blocks),
        in_specs=[pl.BlockSpec((ROW, hidden), lambda r, p: (r, 0))]
        + row_specs
        + [
            pl.BlockSpec((hidden, width), lambda r, p: (0, p)),
            pl.BlockSpec((hidden, width), lambda r, p: (0, blocks + p)),
            pl.BlockSpec((hidden, width), lambda r, p: (0, 2 * blocks + p)),
            vector_spec,
        ],
        out_specs=(block_spec,) * 4 + (log_spec,),
        out_shape=(array(token_count, hidden, dtype=BF16),) * 4 + (array(micro * blocks, heads, ROW),),
        scratch_shapes=[pltpu.VMEM((ROW, ROW), F32), pltpu.VMEM((LANES, hidden), F32)],
        compiler_params=params(),
        cost_estimate=cost(1e6, 1e5),
        name="attention",
    )(tokens, seg_column, seg_row, entry, entry, entry, entry)

    context, returned = lax.optimization_barrier((context, returned))
    returned = returning.second_stage(returned)

    pre_first, normed, activated, slope, pre_second, outputs, student_rows = pl.pallas_call(
        forward_body,
        grid=(ratio,),
        in_specs=[full_spec, full_spec, out_spec, up_spec, down_spec, student_spec, vector_spec, fixed((1, SD))],
        out_specs=(full_spec, full_spec, column_spec, column_spec, full_spec, full_spec, fixed((token_count, SD))),
        out_shape=(
            array(token_count, hidden),
            array(token_count, hidden, dtype=BF16),
            array(token_count, inner_dim, dtype=BF16),
            array(token_count, inner_dim, dtype=BF16),
            array(token_count, hidden),
            array(token_count, hidden, dtype=BF16),
            array(token_count, SD),
        ),
        scratch_shapes=[pltpu.VMEM((token_count, hidden), F32), pltpu.VMEM((LANES, hidden), F32)],
        compiler_params=params(),
        cost_estimate=cost(1e6, 1e5),
        name="forward",
    )(tokens, context, gathered, gathered, gathered, gathered, entry, student_bias[None, :])

    step = 512 if slots % 512 == 0 else slots
    outgoing = pl.pallas_call(
        select_body,
        grid=(slots // step,),
        in_specs=[pl.BlockSpec((step, 1), lambda i: (i, 0)), full_spec],
        out_specs=pl.BlockSpec((step, hidden), lambda i: (i, 0)),
        out_shape=array(slots, hidden, dtype=BF16),
        compiler_params=params(),
        cost_estimate=cost(1e6, 1e5),
        name="select",
    )(slot_token, outputs)

    pairs = logits_grad.shape[0]
    logits, student_grad, small = pl.pallas_call(
        student_body,
        out_shape=(
            array(*logits_grad.shape),
            array(token_count, SD, dtype=BF16),
            array(2 * pairs + 8, SD),
        ),
        compiler_params=params(),
        cost_estimate=cost(1e6, 1e5),
        name="student",
    )(
        student_rows, flat_segment, pool_query[None, :], dense_weight, dense_bias[None, :],
        class_weight, class_bias[None, :], logits_grad,
    )
    outgoing, student_grad, *returned = lax.optimization_barrier((outgoing, student_grad, *returned))
    carried = lax.all_to_all(outgoing, layout.dp, split_axis=0, concat_axis=0, tiled=True)

    first_width = ratio * hidden + SD + LANES
    first_shape = (count, part, first_width) if part % 8 == 0 else (hidden, first_width)
    grad_second, grad_down, first = pl.pallas_call(
        functools.partial(down_grad_body, ratio=ratio, place=layout.late_place),
        grid=(ratio,),
        in_specs=[
            fixed((token_count, 1)), fixed((token_count, SD)), student_spec,
            vector_spec, full_spec, full_spec, column_spec,
        ]
        + [fixed(piece.shape) for piece in returned],
        out_specs=(full_spec, full_spec, fixed(first_shape)),
        out_shape=(
            array(token_count, hidden),
            array(token_count, hidden, dtype=BF16),
            array(*first_shape, dtype=BF16),
        ),
        scratch_shapes=[pltpu.VMEM((8, hidden), F32)],
        compiler_params=params(),
        cost_estimate=cost(1e6, 1e5),
        name="down_grad",
    )(token_slot, student_grad, gathered, entry, pre_second, outputs, activated, *returned)
    if part % 8 != 0:
        order = [layout.late_place.index(i) for i in range(count)]
        first = first.reshape(count, part, first_width)[jnp.asarray(order)]
    first_part = layout.late_sum(first)

    second_width = (ratio + 1) * hidden + LANES
    grad_first, grad_branch, *second = pl.pallas_call(
        functools.partial(up_grad_body, sums=sums, ratio=ratio),
        grid=(ratio,),
        in_specs=[
            core_spec, full_spec, full_spec, down_spec, up_spec, column_spec, full_spec, full_spec, full_spec,
            vector_spec,
        ],
        out_specs=(full_spec, full_spec) + sums.specs(second_width),
        out_shape=(
            array(token_count, hidden),
            array(token_count, hidden, dtype=BF16),
        )
        + sums.shapes(second_width),
        scratch_shapes=[pltpu.VMEM((token_count, hidden), F32), pltpu.VMEM((8, hidden), F32)],
        compiler_params=params(),
        cost_estimate=cost(1e6, 1e5),
        name="up_grad",
    )(core, grad_down, grad_second, gathered, gathered, slope, normed, pre_first, context, entry)
    second, grad_branch, carried = lax.optimization_barrier(
        (sums.first_stage(second), grad_branch, carried)
    )
    second_arrived = layout.exchange(second, 1)
    grads = pl.pallas_call(
        attention_grad_body,
        grid=(micro, blocks),
        in_specs=[pl.BlockSpec((ROW, hidden), lambda r, p: (r, 0))]
        + row_specs
        + [block_spec] * 3
        + [log_spec, pl.BlockSpec((width, hidden), lambda r, p: (p, 0))],
        out_specs=pl.BlockSpec((3, ROW, width), lambda r, p: (0, r, p)),
        out_shape=array(3, token_count, hidden, dtype=BF16),
        scratch_shapes=[pltpu.VMEM((ROW, ROW), F32)],
        compiler_params=params(),
        cost_estimate=cost(1e6, 1e5),
        name="attention_grad",
    )(grad_branch, seg_column, seg_row, query, key, value, log_totals, gathered)

    third_width = 3 * hidden + LANES
    grads_spec = pl.BlockSpec((1, token_count, hidden), lambda j: (j, 0, 0))
    third = pl.pallas_call(
        functools.partial(qkv_grad_body, sums=sums),
        grid=(3,),
        in_specs=[core_spec, full_spec, grads_spec],
        out_specs=sums.specs(third_width),
        out_shape=sums.shapes(third_width),
        scratch_shapes=[pltpu.VMEM((8, hidden), F32)],
        compiler_params=params(),
        cost_estimate=cost(1e6, 1e5),
        name="qkv_grad",
    )(core, tokens, grads)
    third, second_arrived, small = lax.optimization_barrier((third, second_arrived, small))
    small = lax.all_to_all(
        jnp.broadcast_to(small, (count,) + small.shape), axes, split_axis=0, concat_axis=0, tiled=True
    )
    third = sums.first_stage(third)
    third, second_arrived, first_part = lax.optimization_barrier((third, second_arrived, first_part))
    third_arrived = layout.permutes(third, 1)
    first_part = layout.last_sum(first_part)
    third_arrived[1], second_arrived, small = lax.optimization_barrier(
        (third_arrived[1], second_arrived, small)
    )
    second_arrived = layout.exchange(layout.total(second_arrived), 2)
    tokens_grad = pl.pallas_call(
        token_grad_body,
        grid=(3,),
        in_specs=[grads_spec, pl.BlockSpec((hidden, hidden), lambda j: (0, j)), full_spec],
        out_specs=full_spec,
        out_shape=array(token_count, hidden, dtype=BF16),
        scratch_shapes=[pltpu.VMEM((token_count, hidden), F32)],
        compiler_params=params(),
        cost_estimate=cost(1e6, 1e5),
        name="token_grad",
    )(grads, entry, grad_first)
    group = 32 if count % 32 == 0 else count
    dense_weight_grad, class_weight_grad, head_rows = pl.pallas_call(
        functools.partial(head_sums_body, pairs=pairs),
        grid=(count // group,),
        in_specs=[
            pl.BlockSpec((group,) + small.shape[1:], lambda i: (i, 0, 0)),
            fixed(dense_weight.shape),
            fixed((1, SD)),
            fixed(class_weight.shape),
        ],
        out_specs=(fixed((SD, SD)), fixed((SD, SD)), fixed((8, SD))),
        out_shape=(array(SD, SD), array(SD, SD), array(8, SD)),
        compiler_params=params(),
        cost_estimate=cost(1e6, 1e5),
        name="head_sums",
    )(small, dense_weight, dense_bias[None, :], class_weight)
    third_arrived, first_part, tokens_grad, dense_weight_grad = lax.optimization_barrier(
        (third_arrived, first_part, tokens_grad, dense_weight_grad)
    )
    third = layout.total(third_arrived)
    third_arrived = layout.permutes(third, 2)

    def end(body, name, arrived, *shapes):
        return pl.pallas_call(
            body,
            out_shape=tuple(array(*shape) for shape in shapes),
            compiler_params=params(),
            cost_estimate=cost(1e6, 1e5),
            name=name,
        )(*arrived)

    down_grad, student_weight_grad, first_vectors = end(
        functools.partial(first_end_body, hidden=hidden, ratio=ratio), "first_end", [first_part],
        (ratio * part, hidden), (part, SD), (part, LANES),
    )
    up_grad, out_grad, second_vectors = end(
        functools.partial(second_end_body, hidden=hidden, ratio=ratio), "second_end", [second_arrived],
        (part, inner_dim), (part, hidden), (part, LANES),
    )
    up_grad, down_grad, *third_arrived = lax.optimization_barrier((up_grad, down_grad, *third_arrived))
    qkv_grad, third_vectors = end(
        functools.partial(third_end_body, hidden=hidden), "third_end", third_arrived,
        (part, 3 * hidden), (part, LANES),
    )
    return (
        carried,
        logits,
        tokens_grad,
        qkv_grad,
        third_vectors[:, 0],
        third_vectors[:, 1],
        out_grad,
        second_vectors[:, 0],
        second_vectors[:, 1],
        second_vectors[:, 2],
        up_grad,
        second_vectors[:, 3 : 3 + ratio].reshape(-1),
        down_grad,
        first_vectors[:, 0],
        first_vectors[:, 1],
        first_vectors[:, 2],
        student_weight_grad,
        head_rows[1],
        head_rows[0],
        dense_weight_grad,
        head_rows[2],
        class_weight_grad[:, :classes],
        head_rows[3, :classes],
    )


def solution(mesh):
    layout = Layout(mesh)
    rows, flat, whole = P(layout.axes, None), P(layout.axes), P()

    def step(*args):
        return local(layout, *args)

    shard = (flat, flat, rows, flat, flat, flat, rows, flat, rows, flat, flat, flat, rows)
    return jax.shard_map(
        step,
        mesh=layout.mesh,
        in_specs=(rows,) * 7 + shard + (whole,) * 6,
        out_specs=(rows,) * 4 + shard + (whole,) * 6,
        check_vma=False,
    )
```
